32 devices in a mesh: gx: 2 (over core), gy: 4 (over y, x), gz: 4 (over z).
Axes of the slice: x: 2, y: 2, z: 4, core: 2. Of those that a mesh axis runs over, the one named last changes fastest.
Arguments:
- orbitals: bfloat16 [2, 128, 64000], P(None, ('gx', 'gy', 'gz')), may hold values from -6 to 6
- dest: int32 [128], replicated, may hold values from 0 to 31, as said below
- partners: int32 [128, 2], replicated, may hold values from 0 to 127, as said below
- anchors: int32 [128, 3], replicated, may hold values from 0 to 767, as said below
Outputs:
- exchange: float32 [2, 224, 64000], P(None, ('gx', 'gy', 'gz'))
The draws below stay inside these ranges and needn't reach their ends.
Inputs may be any that keep to these rules, and one draw needn't show every extreme that they name: `dest`: box i goes to its first device or to the device just before or just after it in the numbering; a device passes at most 2 boxes to the device before and at most 1 to the device after, and holds at most 7 boxes after the move; every device holds one or more; each of these three bounds is reached in every draw. A box's partners (the box itself or the same box twice may occur) sit at first on the same device as the box or on one next to it in the numbering, and after the move likewise. Before the move and after it, exactly 1 of the boxes of a device are partners of boxes on the device after it, and exactly 1 are partners of boxes on the device before it (where that device exists). `anchors`: columns are the three grid dimensions, each within its own grid extent; along each, a partner's anchor differs from its box's by at most 20 cells, the difference taken modulo the grid.
All inputs are finite; a program needn't handle non-finite values.
Results may differ from the reference program's by a relative error of at most 0.0072.
Values may be sent and summed in bfloat16 or wider, within the bound.
No kernel may reach another device: no remote copies, remote signals or barrier semaphores. Data moves between devices by JAX's collectives and lax.ppermute only.
A program may use at most 64 MiB of HBM per device.

```python
import jax
import jax.numpy as jnp
from jax import lax

SPINS = 2
EDGE = 40
CELLS = 64000
PARTNERS = 2
GRID_X = 768
GRID_Y = 384
GRID_Z = 384
BOX_DEV = 4
BACK = 2
AHEAD = 1
CAP = 7
WINDOW = 1
STEP = 10
BOXES = 128
SLOTS = 224
DEVICES = 32


def chain_layout(key):
    devices = BOXES // BOX_DEV
    subkeys = [jax.random.fold_in(key, 101 + number) for number in range(9)]
    ahead_count = jax.random.randint(subkeys[0], (devices + 1,), 1, AHEAD + 1)
    back_count = jax.random.randint(subkeys[1], (devices + 1,), 1, BACK + 1)
    marker = jax.random.randint(subkeys[2], (), 2, devices - 2)
    bound_index = jnp.arange(devices + 1)
    ahead_count = jnp.where(bound_index == marker, AHEAD, ahead_count)
    ahead_count = jnp.where(bound_index == marker + 1, 0, ahead_count)
    back_count = jnp.where(bound_index == marker, 0, back_count)
    back_count = jnp.where(bound_index == marker + 1, BACK, back_count)
    at_ends = (bound_index == 0) | (bound_index == devices)
    ahead_count = jnp.where(at_ends, 0, ahead_count).astype(jnp.int32)
    back_count = jnp.where(at_ends, 0, back_count).astype(jnp.int32)
    box_ids = jnp.arange(BOXES, dtype=jnp.int32)
    owner = box_ids // BOX_DEV
    shuffles = jax.vmap(lambda subkey: jax.random.permutation(subkey, BOX_DEV))(jax.random.split(subkeys[3], devices))
    rank = shuffles.reshape(-1).astype(jnp.int32)
    box_of = jnp.zeros((BOXES,), jnp.int32).at[owner * BOX_DEV + rank].set(box_ids)
    back_own = jnp.take(back_count, owner)
    ahead_next = jnp.take(ahead_count, owner + 1)
    go_back = rank < back_own
    go_ahead = rank >= BOX_DEV - ahead_next
    dest = (owner - go_back.astype(jnp.int32) + go_ahead.astype(jnp.int32)).astype(jnp.int32)
    core_count = BOX_DEV - back_own - ahead_next
    random_pick = jax.random.randint(subkeys[4], (BOXES,), 0, WINDOW)
    core_pick = (rank - back_own) % WINDOW
    picked = jnp.where(go_back | go_ahead, random_pick, core_pick)
    own_rank = back_own + jax.random.randint(subkeys[5], (BOXES,), 0, BOX_DEV) % core_count
    own_core = jnp.take(box_of, owner * BOX_DEV + own_rank)
    first_dev = jnp.where(go_ahead, owner, owner - 1)
    first_safe = jnp.clip(first_dev, 0, devices - 1)
    plus_box = jnp.take(box_of, first_safe * BOX_DEV + jnp.take(back_count, first_safe) + picked)
    first = jnp.where(first_dev < 0, own_core, plus_box)
    second_dev = jnp.where(go_back, owner, owner + 1)
    second_safe = jnp.clip(second_dev, 0, devices - 1)
    minus_box = jnp.take(box_of, second_safe * BOX_DEV + BOX_DEV - jnp.take(ahead_count, second_safe + 1) - 1 - picked)
    second = jnp.where(second_dev > devices - 1, own_core, minus_box)
    partners = jnp.stack([first, second], axis=1).astype(jnp.int32)
    strides = jax.random.randint(subkeys[6], (devices, 3), -STEP, STEP + 1)
    opening = jax.random.randint(subkeys[7], (1, 3), 0, GRID_Y)
    base = opening + jnp.cumsum(strides, axis=0)
    jitter = jax.random.randint(subkeys[8], (BOXES, 3), 0, STEP + 1)
    extent = jnp.array([GRID_X, GRID_Y, GRID_Z], jnp.int32)
    anchors = ((jnp.take(base, owner, axis=0) + jitter) % extent).astype(jnp.int32)
    lift = GRID_X - 1 - jnp.max(anchors[:, 0])
    anchors = anchors.at[:, 0].add(lift).astype(jnp.int32)
    return (dest, partners, anchors)


def draw_dest(key, part):
    return chain_layout(key)[0]


def draw_partners(key, part):
    return chain_layout(key)[1]


def draw_anchors(key, part):
    return chain_layout(key)[2]


def level_of(rng, dims, cuts, low, largest):
    gain, own = 1.0, jax.random.fold_in(rng, 6)
    for dim, parts in cuts:
        heights = jnp.exp(jax.random.uniform(jax.random.fold_in(own, dim), (parts,), jnp.float32, low / len(cuts), largest / len(cuts)))
        gain = gain * jnp.repeat(heights, dims[dim] // parts).reshape([-1 if axis == dim else 1 for axis in range(len(dims))])
    return gain


def gaussian(key, shape, spread, limit, pieces=(), held_as=jnp.bfloat16):
    result = jax.random.normal(key, shape, jnp.float32) * spread
    if len(pieces) > 0:
        result = level_of(key, shape, pieces, -0.22, 0.18) * result
    return jnp.clip(result, min=-limit, max=limit).astype(held_as)


def setup_inputs(seed: int = 0) -> dict:
    keys = jax.random.split(jax.random.key(seed), 5)
    return {
        "orbitals": gaussian(keys[0], (SPINS, BOXES, CELLS), 1.0, 6.0, ((1, 32),)),
        "dest": draw_dest(jax.random.fold_in(keys[4], 71), 0),
        "partners": draw_partners(jax.random.fold_in(keys[4], 71), 0),
        "anchors": draw_anchors(jax.random.fold_in(keys[4], 71), 0),
    }


SCREEN = 0.001

def sine_basis(edge_cells):
    counter = jnp.arange(edge_cells, dtype=jnp.float32) + 1.0
    angles = jnp.pi * counter[:, None] * counter[None, :] / (edge_cells + 1.0)
    sine_table = (jnp.sqrt(2.0 / (edge_cells + 1.0)) * jnp.sin(angles)).astype(jnp.bfloat16)
    levels = 2.0 - 2.0 * jnp.cos(jnp.pi * counter / (edge_cells + 1.0))
    spectrum = levels[:, None, None] + levels[None, :, None] + levels[None, None, :] + SCREEN
    return (sine_table, spectrum)

def sine_pass(volume, sine_table):
    finest = lax.Precision.HIGHEST
    table = sine_table.astype(jnp.float32)
    volume = jnp.einsum('ak,sabc->skbc', table, volume.astype(jnp.float32), precision=finest).astype(jnp.bfloat16)
    volume = jnp.einsum('bk,sabc->sakc', table, volume.astype(jnp.float32), precision=finest).astype(jnp.bfloat16)
    return jnp.einsum('ck,sabc->sabk', table, volume.astype(jnp.float32), precision=finest)

def reference(orbitals, dest, partners, anchors):
    sine_table, spectrum = sine_basis(EDGE)
    extent = jnp.array([GRID_X, GRID_Y, GRID_Z], dtype=jnp.int32)
    cube_shape = (SPINS, EDGE, EDGE, EDGE)

    def box_term(box_index):
        center = orbitals[:, box_index].astype(jnp.float32).reshape(cube_shape)
        summed = jnp.zeros(cube_shape, jnp.float32)
        for number in range(PARTNERS):
            partner_id = partners[box_index, number]
            difference = anchors[partner_id] - anchors[box_index]
            shift_by = jnp.clip((difference + extent // 2) % extent - extent // 2, -EDGE, EDGE)
            partner_cube = orbitals[:, partner_id].astype(jnp.float32).reshape(cube_shape)
            padded = jnp.pad(partner_cube, ((0, 0), (EDGE, EDGE), (EDGE, EDGE), (EDGE, EDGE)))
            corner = (EDGE - shift_by).astype(jnp.int32)
            shifted = lax.dynamic_slice(padded, (jnp.int32(0), corner[0], corner[1], corner[2]), cube_shape)
            density = (center * shifted).astype(jnp.bfloat16)
            spectral = (sine_pass(density, sine_table) / spectrum).astype(jnp.bfloat16)
            potential = sine_pass(spectral, sine_table)
            summed = summed + potential * shifted
        return summed.reshape(SPINS, CELLS)
    box_terms = lax.map(box_term, jnp.arange(BOXES, dtype=jnp.int32))
    onehot = (dest[:, None] == jnp.arange(DEVICES, dtype=jnp.int32)[None, :]).astype(jnp.int32)
    before_count = jnp.cumsum(onehot, axis=0) - onehot
    slot_of = dest * CAP + lax.optimization_barrier(jnp.sum(before_count * onehot, axis=1))
    exchange = jnp.zeros((SPINS, SLOTS, CELLS), jnp.float32)
    return exchange.at[:, slot_of].set(jnp.moveaxis(box_terms, 0, 1))
```

```python
import jax
import jax.numpy as jnp
import numpy as np
from jax import lax
from jax.experimental import pallas as pl
from jax.experimental.pallas import tpu as pltpu
from jax.sharding import PartitionSpec as P

EDGE = 40
PARTNERS = 2
GRID_X = 768
GRID_Y = 384
GRID_Z = 384
BACK = 2
AHEAD = 1
CAP = 7
SCREEN = 0.001

AXES = ("gx", "gy", "gz")
LANES = 128
FACE = EDGE * EDGE
TILES = -(-FACE // LANES)
WIDE = TILES * LANES
NCHUNK = 256
NSTEPS = -(-FACE // NCHUNK)
NWIDE = NSTEPS * NCHUNK
FLAT = EDGE ** 3 // LANES
HALF = EDGE // 2
PAIRT = 2 * FACE // LANES
PAD = 24
ROWS = EDGE + 2 * PAD
ZERO_TILES = 7
BF = jnp.bfloat16
F32 = jnp.float32


def tables():
    counter = np.arange(EDGE, dtype=np.float32) + 1.0
    angles = np.float32(np.pi) * counter[:, None] * counter[None, :] / np.float32(EDGE + 1.0)
    sine = (np.sqrt(np.float32(2.0 / (EDGE + 1.0))) * np.sin(angles)).astype(jnp.bfloat16)
    sine = sine.astype(np.float32)
    levels = 2.0 - 2.0 * np.cos(np.pi * counter.astype(np.float64) / (EDGE + 1.0))
    lam = levels[:, None, None] + levels[None, :, None] + levels[None, None, :] + SCREEN
    inverse = np.zeros((EDGE, NWIDE), np.float32)
    inverse[:, :FACE] = (1.0 / lam).reshape(EDGE, FACE)
    repeated = np.zeros((EDGE, NWIDE), np.float32)
    repeated[:, :FACE] = np.repeat(sine, EDGE, axis=1)
    tiled = np.zeros((EDGE, NWIDE), np.float32)
    tiled[:, :FACE] = np.tile(sine, (1, EDGE))
    return sine, inverse, repeated, tiled


def lane_iota():
    return lax.broadcasted_iota(jnp.int32, (1, LANES), 1)


def split_boxes(orb_ref, flat_ref, spin, boxes):
    def step(i, _):
        base = pl.multiple_of(i * PAIRT * LANES, LANES)
        x = orb_ref[spin, :, pl.ds(base, PAIRT * LANES)].astype(F32)
        for j in range(PAIRT):
            flat_ref[pl.ds(pl.multiple_of((i * PAIRT + j) * 8, 8), boxes), :] = x[:, j * LANES:(j + 1) * LANES]
        return 0
    lax.fori_loop(0, HALF, step, 0)


def flat_to_slabs(load, store):
    low = lane_iota() < LANES // 2
    rolled = None
    for t in range(PAIRT):
        x = load(t)
        if t < TILES:
            store(t, 0, x)
        if t >= TILES - 1:
            turned = pltpu.roll(x, LANES // 2, 1)
            if rolled is not None:
                store(t - TILES, 1, jnp.where(low, rolled, turned))
            rolled = turned
    store(TILES - 1, 1, rolled)


def slabs_to_flat(load, store):
    low = lane_iota() < LANES // 2
    for t in range(TILES - 1):
        store(t, load(t, 0))
    before = load(TILES - 1, 0)
    for v in range(TILES):
        turned = pltpu.roll(load(v, 1), LANES // 2, 1)
        store(TILES - 1 + v, jnp.where(low, before, turned))
        before = turned


def window_kernel(win_ref, orb_ref, ahead_ref, back_ref, flat_ref):
    boxes = orb_ref.shape[1]
    for spin in range(2):
        split_boxes(orb_ref, flat_ref, spin, boxes)
        ahead_ref[spin] = flat_ref[pl.ds(win_ref[0], FLAT, stride=8), :].astype(BF)
        back_ref[spin] = flat_ref[pl.ds(win_ref[1], FLAT, stride=8), :].astype(BF)


def prepare_kernel(orb_ref, rep_ref, til_ref, own_ref, kron_ref, flat_ref):
    boxes = orb_ref.shape[1]
    for spin in range(2):
        split_boxes(orb_ref, flat_ref, spin, boxes)

        def one(box, _):
            flat_to_slabs(
                lambda t: flat_ref[pl.ds(box + 8 * t, HALF, stride=8 * PAIRT), :],
                lambda u, parity, x: own_ref.__setitem__((box, spin, u, pl.ds(parity, HALF, stride=2), slice(None)), x),
            )
            return 0
        lax.fori_loop(0, boxes, one, 0)

    def build(i, _):
        row = pl.multiple_of(i * 2 * EDGE, 16)
        for c in range(NSTEPS):
            cols = slice(c * NCHUNK, (c + 1) * NCHUNK)
            til = til_ref[:, cols]
            first = rep_ref[pl.ds(2 * i, 1), cols] * til
            second = rep_ref[pl.ds(2 * i + 1, 1), cols] * til
            kron_ref[pl.ds(row, 2 * EDGE), cols] = jnp.concatenate([first, second], axis=0).astype(BF)
        return 0
    lax.fori_loop(0, HALF, build, 0)
    kron_ref[FACE:, :] = jnp.zeros((WIDE - FACE, NWIDE), BF)


def pair_kernel(tab_ref, own_ref, kron_ref, prev_ref, next_ref, diag_ref, inv_ref,
                out_ref, sent_ahead_ref, sent_back_ref,
                pad_ref, mov_ref, x_ref, y_ref, flat_ref, res_ref):
    boxes = own_ref.shape[0]
    body = pl.ds(PAD, EDGE)
    lanes = lane_iota()
    rows = lax.broadcasted_iota(jnp.int32, (EDGE, 1), 0)

    def stage(box, _):
        for spin in range(2):
            for u in range(TILES):
                pad_ref[box, spin, u, body, :] = own_ref[box, spin, u]
        return 0
    lax.fori_loop(0, boxes, stage, 0)
    for side, ref in ((0, prev_ref), (1, next_ref)):
        for spin in range(2):
            flat_ref[...] = ref[spin].astype(F32)
            flat_to_slabs(
                lambda t: flat_ref[pl.ds(t, HALF, stride=PAIRT), :],
                lambda u, parity, x: pad_ref.__setitem__(
                    (boxes + side, spin, u, pl.ds(PAD + parity, HALF, stride=2), slice(None)), x),
            )

    def dense(box, _):
        keep, places = [], []
        for number in range(PARTNERS):
            base = 1 + (box * PARTNERS + number) * 4
            source = tab_ref[base]
            da, db, dc = tab_ref[base + 1], tab_ref[base + 2], tab_ref[base + 3]
            offset = ZERO_TILES * LANES - (db * EDGE + dc)
            quotient, rest = offset // LANES, offset % LANES
            row_ok = (rows >= da) & (rows < da + EDGE)
            places.append((source, da, db, dc, quotient, rest, row_ok))
        for spin in range(2):
            last = [None] * PARTNERS
            for u in range(TILES + 1):
                values = []
                for number in range(PARTNERS):
                    source, da, db, dc, quotient, rest, row_ok = places[number]
                    tile = jnp.clip(quotient + (u - ZERO_TILES), 0, TILES - 1)
                    x = pad_ref[source, spin, tile, pl.ds(PAD - da, EDGE), :]
                    turned = pltpu.roll(x, (LANES - rest) % LANES, 1)
                    if u > 0:
                        cell = lanes + (u - 1) * LANES
                        b = (cell * 52429) >> 21
                        c = cell - b * EDGE
                        ok = (b >= db) & (b < db + EDGE) & (c >= dc) & (c < dc + EDGE) & (b < EDGE)
                        moved = jnp.where(row_ok & ok, jnp.where(lanes < LANES - rest, last[number], turned), 0.0)
                        mov_ref[box, spin, number, u - 1] = moved
                        values.append(own_ref[box, spin, u - 1] * moved)
                    last[number] = turned
                if u > 0:
                    both = jnp.concatenate(values, axis=0)
                    if u == TILES:
                        both = jnp.where(lanes < FACE - (TILES - 1) * LANES, both, 0.0)
                    x_ref[pl.ds(pl.multiple_of((box * 2 + spin) * PARTNERS * EDGE, 16), PARTNERS * EDGE),
                          (u - 1) * LANES:u * LANES] = both.astype(BF)
        return 0
    lax.fori_loop(0, boxes, dense, 0)

    group = 2 * PARTNERS * EDGE
    diag = diag_ref[...]

    def first_pass(box, _):
        where = pl.ds(pl.multiple_of(box * group, 16), group)
        y_ref[where, :WIDE] = jnp.dot(diag, x_ref[where, :WIDE], preferred_element_type=F32).astype(BF)
        return 0
    lax.fori_loop(0, boxes, first_pass, 0)

    cubes = boxes * 2 * PARTNERS

    def forward(n, _):
        cols = pl.ds(pl.multiple_of(n * NCHUNK, NCHUNK), NCHUNK)
        z = jnp.dot(y_ref[:, :WIDE], kron_ref[:, cols], preferred_element_type=F32)
        z = z.reshape(cubes, EDGE, NCHUNK) * inv_ref[:, cols][None]
        x_ref[:, cols] = z.reshape(cubes * EDGE, NCHUNK).astype(BF)
        return 0
    lax.fori_loop(0, NSTEPS, forward, 0)

    def backward(n, _):
        cols = pl.ds(pl.multiple_of(n * NCHUNK, NCHUNK), NCHUNK)
        y_ref[:, cols] = jnp.dot(x_ref[:, :WIDE], kron_ref[:, cols], preferred_element_type=F32).astype(BF)
        return 0
    lax.fori_loop(0, NSTEPS, backward, 0)

    def finish(box, _):
        where = pl.ds(pl.multiple_of(box * group, 16), group)
        for u in range(TILES):
            potential = jnp.dot(diag, y_ref[where, u * LANES:(u + 1) * LANES], preferred_element_type=F32)
            for spin in range(2):
                total = 0.0
                for number in range(PARTNERS):
                    first = (spin * PARTNERS + number) * EDGE
                    total = total + potential[first:first + EDGE] * mov_ref[box, spin, number, u]
                res_ref[spin, u] = total
        for spin in range(2):
            slabs_to_flat(
                lambda u, parity: res_ref[spin, u, pl.ds(parity, HALF, stride=2), :],
                lambda t, x: out_ref.__setitem__(
                    (box, pl.ds(2 * t + spin, HALF, stride=2 * PAIRT), slice(None)), x),
            )
        return 0
    lax.fori_loop(0, boxes, finish, 0)
    base = 1 + boxes * PARTNERS * 4
    for k in range(AHEAD):
        sent_ahead_ref[k] = out_ref[tab_ref[base + k]].astype(BF)
    for k in range(BACK):
        sent_back_ref[k] = out_ref[tab_ref[base + AHEAD + k]].astype(BF)


def place_kernel(code_ref, own_ref, prev_ref, next_ref, out_ref):
    boxes = own_ref.shape[0]
    code = code_ref[pl.program_id(0)]

    @pl.when(code < boxes)
    def _():
        out_ref[0] = own_ref[jnp.minimum(code, boxes - 1)]

    @pl.when((code >= boxes) & (code < boxes + AHEAD))
    def _():
        out_ref[0] = prev_ref[jnp.clip(code - boxes, 0, AHEAD - 1)].astype(F32)

    @pl.when((code >= boxes + AHEAD) & (code < boxes + AHEAD + BACK))
    def _():
        out_ref[0] = next_ref[jnp.clip(code - boxes - AHEAD, 0, BACK - 1)].astype(F32)

    @pl.when(code >= boxes + AHEAD + BACK)
    def _():
        out_ref[...] = jnp.zeros_like(out_ref)


def from_behind(value, steps):
    count = lax.axis_size(AXES)
    initial, last = (max(0, -steps), min(count, count - steps))
    return lax.ppermute(value, AXES, [(source, source + steps) for source in range(initial, last)])


def whole(count):
    return [pl.BlockSpec(memory_space=pltpu.VMEM)] * count


SCALARS = pl.BlockSpec(memory_space=pltpu.SMEM)


def shards(orbitals, dest, partners, anchors):
    boxes = orbitals.shape[1]
    device = lax.axis_index(AXES)
    sine, inverse, repeated, tiled = tables()

    around = lax.dynamic_slice_in_dim(
        jnp.pad(partners, ((boxes, boxes), (0, 0)), constant_values=-1), device * boxes, 3 * boxes, axis=0)
    local = around - device * boxes
    mine = jnp.where((local >= 0) & (local < boxes), local, 0)
    window = jnp.stack([jnp.max(mine[2 * boxes:]), jnp.max(mine[:boxes])]).astype(jnp.int32)

    ahead_box, back_box = pl.pallas_call(
        window_kernel,
        out_shape=[jax.ShapeDtypeStruct((2, FLAT, LANES), BF)] * 2,
        in_specs=[SCALARS] + whole(1),
        out_specs=whole(2),
        scratch_shapes=[pltpu.VMEM((FLAT * 8, LANES), F32)],
        compiler_params=pltpu.CompilerParams(vmem_limit_bytes=8 << 20),
        name="window",
    )(window, orbitals)
    prev_box = from_behind(ahead_box, 1)
    next_box = from_behind(back_box, -1)

    own, kron = pl.pallas_call(
        prepare_kernel,
        out_shape=[jax.ShapeDtypeStruct((boxes, 2, TILES, EDGE, LANES), F32),
                   jax.ShapeDtypeStruct((WIDE, NWIDE), BF)],
        in_specs=whole(3),
        out_specs=whole(2),
        scratch_shapes=[pltpu.VMEM((FLAT * 8, LANES), F32)],
        compiler_params=pltpu.CompilerParams(vmem_limit_bytes=16 << 20),
        cost_estimate=pl.CostEstimate(flops=10_000_000, bytes_accessed=10_000_000, transcendentals=0),
        name="prepare",
    )(orbitals, repeated, tiled)

    pairs = local[boxes:2 * boxes]
    side = pairs // boxes
    source = jnp.where(side < 0, boxes, jnp.where(side > 0, boxes + 1, pairs))
    spots = lax.dynamic_slice_in_dim(
        jnp.pad(anchors, ((boxes, boxes), (0, 0))), device * boxes, 3 * boxes, axis=0)
    pick = (jnp.clip(pairs + boxes, 0, 3 * boxes - 1)[:, :, None] == jnp.arange(3 * boxes, dtype=jnp.int32))
    there = jnp.sum(jnp.where(pick[..., None], spots[None, None], 0), axis=2)
    extent = jnp.array([GRID_X, GRID_Y, GRID_Z], jnp.int32)
    difference = there - spots[boxes:2 * boxes, None, :]
    delta = (difference + extent // 2) % extent - extent // 2
    delta = jnp.clip(delta, -(PAD - 4), PAD - 4)
    pair_table = jnp.concatenate([source[..., None], delta], axis=-1).reshape(-1)

    nearby = lax.dynamic_slice_in_dim(
        jnp.pad(dest, (boxes, boxes), constant_values=-1), device * boxes, 3 * boxes)
    place = jnp.arange(3 * boxes, dtype=jnp.int32)
    earlier = (nearby[:, None] == nearby[None, :]) & (place[None, :] < place[:, None])
    same = (place[:, None] // boxes) == (place[None, :] // boxes)
    rank = jnp.sum(earlier.astype(jnp.int32), axis=1)
    inside = jnp.sum((earlier & same).astype(jnp.int32), axis=1)
    block = place // boxes
    code = jnp.where(block == 1, place - boxes,
                     jnp.where(block == 0, boxes + inside, boxes + AHEAD + inside))
    slot = jnp.arange(CAP, dtype=jnp.int32)
    taken = (nearby[None, :] == device) & (rank[None, :] == slot[:, None])
    none = boxes + AHEAD + BACK
    codes = none + jnp.sum(jnp.where(taken, code[None, :] - none, 0), axis=1)
    goes = nearby[boxes:2 * boxes]
    order = inside[boxes:2 * boxes]
    box_line = jnp.arange(boxes, dtype=jnp.int32)
    leave_ahead = [jnp.sum(jnp.where((goes == device + 1) & (order == k), box_line, 0)) for k in range(AHEAD)]
    leave_back = [jnp.sum(jnp.where((goes == device - 1) & (order == k), box_line, 0)) for k in range(BACK)]
    table = jnp.concatenate([device[None].astype(jnp.int32), pair_table,
                             jnp.stack(leave_ahead + leave_back)]).astype(jnp.int32)

    diag = np.kron(np.eye(2 * PARTNERS, dtype=np.float32), sine).astype(jnp.bfloat16)
    cubes = boxes * 2 * PARTNERS
    terms, sent_ahead, sent_back = pl.pallas_call(
        pair_kernel,
        out_shape=[jax.ShapeDtypeStruct((boxes, 2 * FLAT, LANES), F32),
                   jax.ShapeDtypeStruct((AHEAD, 2 * FLAT, LANES), BF),
                   jax.ShapeDtypeStruct((BACK, 2 * FLAT, LANES), BF)],
        in_specs=[SCALARS] + whole(6),
        out_specs=whole(3),
        scratch_shapes=[
            pltpu.VMEM((boxes + 2, 2, TILES, ROWS, LANES), F32),
            pltpu.VMEM((boxes, 2, PARTNERS, TILES, EDGE, LANES), F32),
            pltpu.VMEM((cubes * EDGE, NWIDE), BF),
            pltpu.VMEM((cubes * EDGE, NWIDE), BF),
            pltpu.VMEM((FLAT, LANES), F32),
            pltpu.VMEM((2, TILES, EDGE, LANES), F32),
        ],
        compiler_params=pltpu.CompilerParams(vmem_limit_bytes=48 << 20),
        name="pairs",
    )(table, own, kron, prev_box, next_box, diag, inverse)
    from_prev = from_behind(sent_ahead, 1)
    from_next = from_behind(sent_back, -1)

    placed = pl.pallas_call(
        place_kernel,
        out_shape=jax.ShapeDtypeStruct((CAP, 2 * FLAT, LANES), F32),
        grid=(CAP,),
        in_specs=[SCALARS] + whole(3),
        out_specs=pl.BlockSpec((1, 2 * FLAT, LANES), lambda i: (i, 0, 0)),
        compiler_params=pltpu.CompilerParams(vmem_limit_bytes=16 << 20),
        name="place",
    )(codes, terms, from_prev, from_next)
    placed = placed.reshape(CAP, FLAT, 2, LANES)
    return placed.transpose(2, 0, 1, 3).reshape(2, CAP, FLAT * LANES)


def solution(mesh):
    return jax.shard_map(
        shards,
        mesh=mesh,
        in_specs=(P(None, AXES, None), P(), P(), P()),
        out_specs=P(None, AXES, None),
        check_vma=False,
    )
```

```python
import jax
import jax.numpy as jnp
import numpy as np
from jax import lax
from jax.experimental import pallas as pl
from jax.experimental.pallas import tpu as pltpu
from jax.sharding import PartitionSpec as P


EDGE = 40
PARTNERS = 2
GRID_X = 768
GRID_Y = 384
GRID_Z = 384
BACK = 2
AHEAD = 1
CAP = 7
SCREEN = 0.001

AXES = ("gx", "gy", "gz")
LANES = 128
FACE = EDGE * EDGE
TILES = -(-FACE // LANES)
WIDE = TILES * LANES
NCHUNK = 256
NSTEPS = -(-FACE // NCHUNK)
NWIDE = NSTEPS * NCHUNK
FLAT = EDGE ** 3 // LANES
HALF = EDGE // 2
PAIRT = 2 * FACE // LANES
PAD = 24
ROWS = EDGE + 2 * PAD
ZERO_TILES = 7
BF = jnp.bfloat16
F32 = jnp.float32


def tables():
    counter = np.arange(EDGE, dtype=np.float32) + 1.0
    angles = np.float32(np.pi) * counter[:, None] * counter[None, :] / np.float32(EDGE + 1.0)
    sine = (np.sqrt(np.float32(2.0 / (EDGE + 1.0))) * np.sin(angles)).astype(jnp.bfloat16)
    sine = sine.astype(np.float32)
    levels = 2.0 - 2.0 * np.cos(np.pi * counter.astype(np.float64) / (EDGE + 1.0))
    lam = levels[:, None, None] + levels[None, :, None] + levels[None, None, :] + SCREEN
    inverse = np.zeros((EDGE, NWIDE), np.float32)
    inverse[:, :FACE] = (1.0 / lam).reshape(EDGE, FACE)
    repeated = np.zeros((EDGE, NWIDE), np.float32)
    repeated[:, :FACE] = np.repeat(sine, EDGE, axis=1)
    tiled = np.zeros((EDGE, NWIDE), np.float32)
    tiled[:, :FACE] = np.tile(sine, (1, EDGE))
    return sine, inverse, repeated, tiled


def lane_iota():
    return lax.broadcasted_iota(jnp.int32, (1, LANES), 1)


def split_boxes(orb_ref, flat_ref, spin, boxes):
    def step(i, _):
        base = pl.multiple_of(i * PAIRT * LANES, LANES)
        x = orb_ref[spin, :, pl.ds(base, PAIRT * LANES)].astype(F32)
        for j in range(PAIRT):
            flat_ref[pl.ds(pl.multiple_of((i * PAIRT + j) * 8, 8), boxes), :] = x[:, j * LANES:(j + 1) * LANES]
        return 0

    lax.fori_loop(0, HALF, step, 0)


def flat_to_slabs(load, store):
    low = lane_iota() < LANES // 2
    rolled = None
    for t in range(PAIRT):
        x = load(t)
        if t < TILES:
            store(t, 0, x)
        if t >= TILES - 1:
            turned = pltpu.roll(x, LANES // 2, 1)
            if rolled is not None:
                store(t - TILES, 1, jnp.where(low, rolled, turned))
            rolled = turned
    store(TILES - 1, 1, rolled)


def slabs_to_flat(load, store):
    low = lane_iota() < LANES // 2
    for t in range(TILES - 1):
        store(t, load(t, 0))
    before = load(TILES - 1, 0)
    for v in range(TILES):
        turned = pltpu.roll(load(v, 1), LANES // 2, 1)
        store(TILES - 1 + v, jnp.where(low, before, turned))
        before = turned


def window_kernel(part_ref, orb_ref, *refs):
    outs, (orb, flat_ref, sems) = refs[:4], refs[4:]
    boxes = orb_ref.shape[1]
    total = part_ref.shape[1]
    device = lax.axis_index(AXES)
    copies = [pltpu.make_async_copy(orb_ref.at[spin], orb.at[spin], sems.at[spin]) for spin in range(2)]
    for copy in copies:
        copy.start()
    wanted = []
    for step in (1, -1):
        found = jnp.int32(0)
        for k in range(boxes):
            other = (device + step) * boxes + k
            inside = (other >= 0) & (other < total)
            for number in range(PARTNERS):
                local = part_ref[number, jnp.clip(other, 0, total - 1)] - device * boxes
                found = jnp.where(inside & (local >= 0) & (local < boxes), local, found)
        wanted.append(found)
    for spin in range(2):
        copies[spin].wait()
        split_boxes(orb, flat_ref, spin, boxes)
        for side in range(2):
            outs[2 * spin + side][...] = flat_ref[pl.ds(wanted[side], FLAT, stride=8), :].astype(BF)


def table_layout(boxes):
    pairs = 0
    codes = pairs + boxes * PARTNERS * 4
    slots = codes + CAP + 1
    leaves = slots + AHEAD + BACK + 1
    return pairs, codes, slots, leaves, leaves + AHEAD + BACK + 1


def prepare_kernel(dest_ref, part_ref, anc_ref, orb_ref, rep_ref, til_ref, own_ref, kron_ref, tab_ref, flat_ref):
    boxes = orb_ref.shape[1]
    total = part_ref.shape[1]
    device = lax.axis_index(AXES)
    pairs, codes, slots, leaves, _ = table_layout(boxes)
    for box in range(boxes):
        me = device * boxes + box
        for number in range(PARTNERS):
            other = part_ref[number, me]
            local = other - device * boxes
            base = pairs + (box * PARTNERS + number) * 4
            tab_ref[base] = jnp.where(local < 0, boxes, jnp.where(local >= boxes, boxes + 1, local))
            for axis, extent in enumerate((GRID_X, GRID_Y, GRID_Z)):
                moved = anc_ref[axis, other] - anc_ref[axis, me] + extent // 2
                moved = jnp.where(moved < 0, moved + extent, jnp.where(moved >= extent, moved - extent, moved))
                tab_ref[base + 1 + axis] = jnp.clip(moved - extent // 2, -(PAD - 4), PAD - 4)
    for k in range(CAP + 1):
        tab_ref[codes + k] = boxes + AHEAD + BACK
    for k in range(AHEAD + BACK + 1):
        tab_ref[slots + k] = CAP
        tab_ref[leaves + k] = 0
    count = jnp.int32(0)
    for block in range(3):
        arrived = jnp.int32(0)
        ahead, back = jnp.int32(0), jnp.int32(0)
        for k in range(boxes):
            box = (device + (block - 1)) * boxes + k
            inside = (box >= 0) & (box < total)
            goes = dest_ref[jnp.clip(box, 0, total - 1)]
            hit = inside & (goes == device)
            if block == 1:
                code = jnp.int32(k)
                leaves_ahead, leaves_back = goes == device + 1, goes == device - 1
                spare = leaves + AHEAD + BACK
                tab_ref[jnp.where(leaves_ahead, leaves + jnp.minimum(ahead, AHEAD - 1), spare)] = jnp.int32(k)
                tab_ref[jnp.where(leaves_back, leaves + AHEAD + jnp.minimum(back, BACK - 1), spare)] = jnp.int32(k)
                ahead = ahead + leaves_ahead.astype(jnp.int32)
                back = back + leaves_back.astype(jnp.int32)
            else:
                first, most = (0, AHEAD) if block == 0 else (AHEAD, BACK)
                where = first + jnp.minimum(arrived, most - 1)
                code = boxes + where
                tab_ref[jnp.where(hit, slots + where, slots + AHEAD + BACK)] = count
                arrived = arrived + hit.astype(jnp.int32)
            tab_ref[jnp.where(hit, codes + jnp.minimum(count, CAP - 1), codes + CAP)] = code
            count = count + hit.astype(jnp.int32)

    for spin in range(2):
        split_boxes(orb_ref, flat_ref, spin, boxes)

        def one(box, _):
            flat_to_slabs(
                lambda t: flat_ref[pl.ds(box + 8 * t, HALF, stride=8 * PAIRT), :],
                lambda u, parity, x: own_ref.__setitem__((box, spin, u, pl.ds(parity, HALF, stride=2), slice(None)), x),
            )
            return 0

        lax.fori_loop(0, boxes, one, 0)

    def build(i, _):
        row = pl.multiple_of(i * 2 * EDGE, 16)
        for c in range(NSTEPS):
            cols = slice(c * NCHUNK, (c + 1) * NCHUNK)
            til = til_ref[:, cols]
            first = rep_ref[pl.ds(2 * i, 1), cols] * til
            second = rep_ref[pl.ds(2 * i + 1, 1), cols] * til
            kron_ref[pl.ds(row, 2 * EDGE), cols] = jnp.concatenate([first, second], axis=0).astype(BF)
        return 0

    lax.fori_loop(0, HALF, build, 0)
    kron_ref[FACE:, :] = jnp.zeros((WIDE - FACE, NWIDE), BF)


def pair_kernel(spin, tab_ref, own_ref, kron_ref, prev_ref, next_ref, diag_ref, inv_ref,
                out_ref, sent_ahead_ref, sent_back_ref,
                pad_ref, mov_ref, x_ref, y_ref, flat_ref, res_ref):
    boxes = own_ref.shape[0]
    pairs, _, _, leaves, _ = table_layout(boxes)
    body = pl.ds(PAD, EDGE)
    lanes = lane_iota()
    rows = lax.broadcasted_iota(jnp.int32, (EDGE, 1), 0)

    def stage(box, _):
        for u in range(TILES):
            pad_ref[box, u, body, :] = own_ref[box, spin, u]
        return 0

    lax.fori_loop(0, boxes, stage, 0)
    for side, ref in ((0, prev_ref), (1, next_ref)):
        flat_ref[...] = ref[...].astype(F32)
        flat_to_slabs(
            lambda t: flat_ref[pl.ds(t, HALF, stride=PAIRT), :],
            lambda u, parity, x: pad_ref.__setitem__(
                (boxes + side, u, pl.ds(PAD + parity, HALF, stride=2), slice(None)), x),
        )

    def dense(box, _):
        places = []
        for number in range(PARTNERS):
            base = pairs + (box * PARTNERS + number) * 4
            source = tab_ref[base]
            da, db, dc = tab_ref[base + 1], tab_ref[base + 2], tab_ref[base + 3]
            offset = ZERO_TILES * LANES - (db * EDGE + dc)
            row_ok = jnp.abs(2 * (rows - da) - (EDGE - 1)) < EDGE
            places.append((source, da, db, dc, offset // LANES, offset % LANES, row_ok))
        last = [None] * PARTNERS
        for u in range(TILES + 1):
            values = []
            for number in range(PARTNERS):
                source, da, db, dc, quotient, rest, row_ok = places[number]
                tile = jnp.clip(quotient + (u - ZERO_TILES), 0, TILES - 1)
                x = pad_ref[source, tile, pl.ds(PAD - da, EDGE), :]
                turned = pltpu.roll(x, (LANES - rest) % LANES, 1)
                if u > 0:
                    cell = lanes + (u - 1) * LANES
                    b = (cell * 52429) >> 21
                    c = cell - b * EDGE
                    ok = (jnp.abs(2 * (b - db) - (EDGE - 1)) < EDGE) & (jnp.abs(2 * (c - dc) - (EDGE - 1)) < EDGE)
                    if u == TILES:
                        ok = ok & (lanes < FACE - (TILES - 1) * LANES)
                    moved = jnp.where(row_ok & ok, jnp.where(lanes < LANES - rest, last[number], turned), 0.0)
                    mov_ref[box, number, u - 1] = moved
                    values.append(own_ref[box, spin, u - 1] * moved)
                last[number] = turned
            if u > 0:
                both = jnp.concatenate(values, axis=0)
                if u == TILES:
                    both = jnp.where(lanes < FACE - (TILES - 1) * LANES, both, 0.0)
                x_ref[pl.ds(pl.multiple_of(box * PARTNERS * EDGE, 16), PARTNERS * EDGE),
                      (u - 1) * LANES:u * LANES] = both.astype(BF)
        return 0

    lax.fori_loop(0, boxes, dense, 0)

    group = diag_ref.shape[0]
    cubes = boxes * PARTNERS
    diag = diag_ref[...]

    def first_pass(i, _):
        where = pl.ds(pl.multiple_of(i * group, 16), group)
        y_ref[where, :WIDE] = jnp.dot(diag, x_ref[where, :WIDE], preferred_element_type=F32).astype(BF)
        return 0

    lax.fori_loop(0, cubes * EDGE // group, first_pass, 0)

    def forward(n, _):
        cols = pl.ds(pl.multiple_of(n * NCHUNK, NCHUNK), NCHUNK)
        z = jnp.dot(y_ref[:, :WIDE], kron_ref[:, cols], preferred_element_type=F32)
        z = z.reshape(cubes, EDGE, NCHUNK) * inv_ref[:, cols][None]
        x_ref[:, cols] = z.reshape(cubes * EDGE, NCHUNK).astype(BF)
        return 0

    lax.fori_loop(0, NSTEPS, forward, 0)

    def backward(n, _):
        cols = pl.ds(pl.multiple_of(n * NCHUNK, NCHUNK), NCHUNK)
        y_ref[:, cols] = jnp.dot(x_ref[:, :WIDE], kron_ref[:, cols], preferred_element_type=F32).astype(BF)
        return 0

    lax.fori_loop(0, NSTEPS, backward, 0)

    held = group // (PARTNERS * EDGE)

    def finish(i, _):
        where = pl.ds(pl.multiple_of(i * group, 16), group)
        for u in range(TILES):
            potential = jnp.dot(diag, y_ref[where, u * LANES:(u + 1) * LANES], preferred_element_type=F32)
            for k in range(held):
                total = 0.0
                for number in range(PARTNERS):
                    first = (k * PARTNERS + number) * EDGE
                    total = total + potential[first:first + EDGE] * mov_ref[i * held + k, number, u]
                res_ref[k, u] = total
        for k in range(held):
            slabs_to_flat(
                lambda u, parity: res_ref[k, u, pl.ds(parity, HALF, stride=2), :],
                lambda t, x: out_ref.__setitem__((i * held + k, pl.ds(t, HALF, stride=PAIRT), slice(None)), x),
            )
        return 0

    lax.fori_loop(0, boxes // held, finish, 0)
    for k in range(AHEAD):
        sent_ahead_ref[k] = out_ref[tab_ref[leaves + k]].astype(BF)
    for k in range(BACK):
        sent_back_ref[k] = out_ref[tab_ref[leaves + AHEAD + k]].astype(BF)


def interleave(out, both_ref, load):
    for spin in range(2):
        both_ref[pl.ds(spin, FLAT, stride=2), :] = load(spin)

    def step(i, _):
        base = pl.multiple_of(i * PAIRT * LANES, LANES)
        chunk = both_ref[pl.ds(pl.multiple_of(i * 2 * PAIRT, 2), 2 * PAIRT), :]
        for j in range(PAIRT):
            out[:, pl.ds(pl.multiple_of(base + j * LANES, LANES), LANES)] = chunk[2 * j:2 * j + 2]
        return 0

    lax.fori_loop(0, HALF, step, 0)


def keep_kernel(tab_ref, low_ref, high_ref, out_ref, both_ref):
    boxes = low_ref.shape[0]
    code = tab_ref[table_layout(boxes)[1] + pl.program_id(0)]

    @pl.when(code < boxes)
    def _():
        box = jnp.minimum(code, boxes - 1)
        interleave(out_ref.at[0], both_ref, lambda spin: (low_ref, high_ref)[spin][box])

    @pl.when(code >= boxes + AHEAD + BACK)
    def _():
        out_ref[...] = jnp.zeros_like(out_ref)


def place_kernel(boxes, tab_ref, prev_low, next_low, prev_high, next_high, kept_ref, out_ref, form_ref, both_ref, sems):
    slots = table_layout(boxes)[2]
    copies = []
    for k in range(AHEAD + BACK):
        pair, row = ((prev_low, prev_high), k) if k < AHEAD else ((next_low, next_high), k - AHEAD)
        slot = tab_ref[slots + k]
        copy = pltpu.make_async_copy(form_ref.at[k], out_ref.at[jnp.minimum(slot, CAP - 1)], sems.at[k])

        @pl.when(slot < CAP)
        def _():
            interleave(form_ref.at[k], both_ref, lambda spin: pair[spin][row].astype(F32))
            copy.start()

        copies.append((slot, copy))
    for slot, copy in copies:
        @pl.when(slot < CAP)
        def _():
            copy.wait()


def from_behind(value, steps):
    count = lax.axis_size(AXES)
    initial, last = (max(0, -steps), min(count, count - steps))
    return lax.ppermute(value, AXES, [(source, source + steps) for source in range(initial, last)])


def whole(count):
    return [pl.BlockSpec(memory_space=pltpu.VMEM)] * count


SCALARS = pl.BlockSpec(memory_space=pltpu.SMEM)
ANYWHERE = pl.BlockSpec(memory_space=pltpu.MemorySpace.HBM)


def cost(flops, size):
    return pl.CostEstimate(flops=flops, bytes_accessed=size, transcendentals=0)


def shards(orbitals, dest, partners, anchors):
    boxes = orbitals.shape[1]
    sine, inverse, repeated, tiled = tables()
    partners_t, anchors_t = partners.T, anchors.T

    windows = pl.pallas_call(
        window_kernel,
        out_shape=[jax.ShapeDtypeStruct((FLAT, LANES), BF)] * 4,
        in_specs=[SCALARS, ANYWHERE],
        out_specs=whole(4),
        scratch_shapes=[pltpu.VMEM(orbitals.shape, BF), pltpu.VMEM((FLAT * 8, LANES), F32),
                        pltpu.SemaphoreType.DMA((2,))],
        compiler_params=pltpu.CompilerParams(vmem_limit_bytes=8 << 20),
        name="window",
    )(partners_t, orbitals)
    halos = []
    for spin in range(2):
        ahead = from_behind(windows[2 * spin], 1)
        back = from_behind(windows[2 * spin + 1], -1)
        halos.append((ahead, back))

    own, kron, table = pl.pallas_call(
        prepare_kernel,
        out_shape=[jax.ShapeDtypeStruct((boxes, 2, TILES, EDGE, LANES), F32),
                   jax.ShapeDtypeStruct((WIDE, NWIDE), BF),
                   jax.ShapeDtypeStruct((table_layout(boxes)[-1],), jnp.int32)],
        in_specs=[SCALARS] * 3 + whole(3),
        out_specs=whole(2) + [SCALARS],
        scratch_shapes=[pltpu.VMEM((FLAT * 8, LANES), F32)],
        compiler_params=pltpu.CompilerParams(vmem_limit_bytes=14 << 20),
        cost_estimate=cost(10_000_000, 10_000_000),
        name="prepare",
    )(dest, partners_t, anchors_t, orbitals, repeated, tiled)

    held = 2 if boxes % 2 == 0 else 1
    diag = np.kron(np.eye(held * PARTNERS, dtype=np.float32), sine).astype(jnp.bfloat16)
    cubes = boxes * PARTNERS
    terms, arrived = [], []
    for spin in range(2):
        solve = pl.pallas_call(
            lambda *refs, spin=spin: pair_kernel(spin, *refs),
            out_shape=[jax.ShapeDtypeStruct((boxes, FLAT, LANES), F32),
                       jax.ShapeDtypeStruct((AHEAD, FLAT, LANES), BF),
                       jax.ShapeDtypeStruct((BACK, FLAT, LANES), BF)],
            in_specs=[SCALARS] + whole(6),
            out_specs=whole(3),
            scratch_shapes=[
                pltpu.VMEM((boxes + 2, TILES, ROWS, LANES), F32),
                pltpu.VMEM((boxes, PARTNERS, TILES, EDGE, LANES), F32),
                pltpu.VMEM((cubes * EDGE, NWIDE), BF),
                pltpu.VMEM((cubes * EDGE, NWIDE), BF),
                pltpu.VMEM((FLAT, LANES), F32),
                pltpu.VMEM((held, TILES, EDGE, LANES), F32),
            ],
            compiler_params=pltpu.CompilerParams(vmem_limit_bytes=24 << 20),
            cost_estimate=cost(4 * cubes * EDGE * FACE * FACE, 10_000_000),
        )
        mine, sent_ahead, sent_back = solve(table, own, kron, *halos[spin], diag, inverse)
        terms.append(mine)
        ahead = from_behind(sent_ahead, 1)
        back = from_behind(sent_back, -1)
        arrived += [ahead, back]

    shape = jax.ShapeDtypeStruct((CAP, 2, FLAT * LANES), F32)
    kept = pl.pallas_call(
        keep_kernel,
        out_shape=shape,
        grid=(CAP,),
        in_specs=[SCALARS] + whole(2),
        out_specs=pl.BlockSpec((1, 2, FLAT * LANES), lambda i: (i, 0, 0)),
        scratch_shapes=[pltpu.VMEM((2 * FLAT, LANES), F32)],
        compiler_params=pltpu.CompilerParams(vmem_limit_bytes=8 << 20),
        cost_estimate=cost(1_000_000, 8_000_000),
        name="keep",
    )(table, *terms)
    placed = pl.pallas_call(
        lambda *refs: place_kernel(boxes, *refs),
        out_shape=shape,
        in_specs=[SCALARS] + whole(4) + [ANYWHERE],
        out_specs=ANYWHERE,
        scratch_shapes=[pltpu.VMEM((AHEAD + BACK, 2, FLAT * LANES), F32), pltpu.VMEM((2 * FLAT, LANES), F32),
                        pltpu.SemaphoreType.DMA((AHEAD + BACK,))],
        input_output_aliases={5: 0},
        compiler_params=pltpu.CompilerParams(vmem_limit_bytes=8 << 20),
        cost_estimate=cost(1_000_000, 4_000_000),
        name="place",
    )(table, *arrived, kept)
    return jnp.transpose(placed, (1, 0, 2))


def solution(mesh):
    return jax.shard_map(
        shards,
        mesh=mesh,
        in_specs=(P(None, AXES, None), P(), P(), P()),
        out_specs=P(None, AXES, None),
        check_vma=False,
    )
```

```python
import jax
import jax.numpy as jnp
import numpy as np
from jax import lax
from jax.experimental import pallas as pl
from jax.experimental.pallas import tpu as pltpu
from jax.sharding import PartitionSpec as P


EDGE = 40
PARTNERS = 2
GRID_X = 768
GRID_Y = 384
GRID_Z = 384
BACK = 2
AHEAD = 1
CAP = 7
SCREEN = 0.001

AXES = ("gx", "gy", "gz")
LANES = 128
FACE = EDGE * EDGE
TILES = -(-FACE // LANES)
WIDE = TILES * LANES
NCHUNK = 256
NSTEPS = -(-FACE // NCHUNK)
NWIDE = NSTEPS * NCHUNK
FLAT = EDGE ** 3 // LANES
HALF = EDGE // 2
PAIRT = 2 * FACE // LANES
PAD = 24
ROWS = EDGE + 2 * PAD
ZERO_TILES = 7
BF = jnp.bfloat16
F32 = jnp.float32


def tables():
    counter = np.arange(EDGE, dtype=np.float32) + 1.0
    angles = np.float32(np.pi) * counter[:, None] * counter[None, :] / np.float32(EDGE + 1.0)
    sine = (np.sqrt(np.float32(2.0 / (EDGE + 1.0))) * np.sin(angles)).astype(jnp.bfloat16)
    sine = sine.astype(np.float32)
    levels = 2.0 - 2.0 * np.cos(np.pi * counter.astype(np.float64) / (EDGE + 1.0))
    lam = levels[:, None, None] + levels[None, :, None] + levels[None, None, :] + SCREEN
    inverse = np.zeros((EDGE, NWIDE), np.float32)
    inverse[:, :FACE] = (1.0 / lam).reshape(EDGE, FACE)
    repeated = np.zeros((EDGE, NWIDE), np.float32)
    repeated[:, :FACE] = np.repeat(sine, EDGE, axis=1)
    tiled = np.zeros((EDGE, NWIDE), np.float32)
    tiled[:, :FACE] = np.tile(sine, (1, EDGE))
    return sine, inverse, repeated, tiled


def lane_iota():
    return lax.broadcasted_iota(jnp.int32, (1, LANES), 1)


def split_boxes(orb_ref, flat_ref, spin, boxes):
    def step(i, _):
        base = pl.multiple_of(i * PAIRT * LANES, LANES)
        x = orb_ref[spin, :, pl.ds(base, PAIRT * LANES)].astype(F32)
        for j in range(PAIRT):
            flat_ref[pl.ds(pl.multiple_of((i * PAIRT + j) * 8, 8), boxes), :] = x[:, j * LANES:(j + 1) * LANES]
        return 0

    lax.fori_loop(0, HALF, step, 0)


def flat_to_slabs(load, store):
    low = lane_iota() < LANES // 2
    rolled = None
    for t in range(PAIRT):
        x = load(t)
        if t < TILES:
            store(t, 0, x)
        if t >= TILES - 1:
            turned = pltpu.roll(x, LANES // 2, 1)
            if rolled is not None:
                store(t - TILES, 1, jnp.where(low, rolled, turned))
            rolled = turned
    store(TILES - 1, 1, rolled)


def slabs_to_flat(load, store):
    low = lane_iota() < LANES // 2
    for t in range(TILES - 1):
        store(t, load(t, 0))
    before = load(TILES - 1, 0)
    for v in range(TILES):
        turned = pltpu.roll(load(v, 1), LANES // 2, 1)
        store(TILES - 1 + v, jnp.where(low, before, turned))
        before = turned


def window_kernel(part_ref, orb_ref, *refs):
    outs, (orb, flat_ref, sems) = refs[:2], refs[2:]
    boxes = orb_ref.shape[1]
    total = part_ref.shape[1]
    device = lax.axis_index(AXES)
    copies = [pltpu.make_async_copy(orb_ref.at[spin], orb.at[spin], sems.at[spin]) for spin in range(2)]
    for copy in copies:
        copy.start()
    wanted = []
    for step in (1, -1):
        found = jnp.int32(0)
        for k in range(boxes):
            other = (device + step) * boxes + k
            inside = (other >= 0) & (other < total)
            for number in range(PARTNERS):
                local = part_ref[number, jnp.clip(other, 0, total - 1)] - device * boxes
                found = jnp.where(inside & (local >= 0) & (local < boxes), local, found)
        wanted.append(found)
    for spin in range(2):
        copies[spin].wait()
        split_boxes(orb, flat_ref, spin, boxes)
        for side in range(2):
            outs[side][spin] = flat_ref[pl.ds(wanted[side], FLAT, stride=8), :].astype(BF)


def table_layout(boxes):
    pairs = 0
    codes = pairs + boxes * PARTNERS * 4
    slots = codes + CAP + 1
    leaves = slots + AHEAD + BACK + 1
    order = leaves + AHEAD + BACK + 1
    return pairs, codes, slots, leaves, order, order + boxes


def prepare_kernel(dest_ref, part_ref, anc_ref, orb_ref, rep_ref, pad_ref, kron_ref, tab_ref, flat_ref):
    boxes = orb_ref.shape[1]
    total = part_ref.shape[1]
    device = lax.axis_index(AXES)
    pairs, codes, slots, leaves, order, _ = table_layout(boxes)
    one, none = jnp.int32(1), jnp.int32(0)
    for k in range(CAP + 1):
        tab_ref[codes + k] = boxes + AHEAD + BACK
    for k in range(AHEAD + BACK + 1):
        tab_ref[slots + k] = CAP
        tab_ref[leaves + k] = 0
    goes = [dest_ref[device * boxes + k] for k in range(boxes)]
    ahead_all, back_all = none, none
    for k in range(boxes):
        ahead_all = ahead_all + jnp.where(goes[k] == device + 1, one, none)
        back_all = back_all + jnp.where(goes[k] == device - 1, one, none)
    ahead, back, stay = none, none, none
    spots = []
    for k in range(boxes):
        is_ahead, is_back = goes[k] == device + 1, goes[k] == device - 1
        spot = jnp.where(is_ahead, ahead, jnp.where(is_back, ahead_all + back, ahead_all + back_all + stay))
        spots.append(spot)
        tab_ref[order + spot] = k
        spare = leaves + AHEAD + BACK
        tab_ref[jnp.where(is_ahead, leaves + jnp.minimum(ahead, AHEAD - 1), spare)] = spot
        tab_ref[jnp.where(is_back, leaves + AHEAD + jnp.minimum(back, BACK - 1), spare)] = spot
        ahead = ahead + jnp.where(is_ahead, one, none)
        back = back + jnp.where(is_back, one, none)
        stay = stay + jnp.where(is_ahead | is_back, none, one)
    count = none
    for block in range(3):
        arrived = none
        for k in range(boxes):
            box = (device + (block - 1)) * boxes + k
            hit = (box >= 0) & (box < total) & (dest_ref[jnp.clip(box, 0, total - 1)] == device)
            if block == 1:
                code = spots[k]
            else:
                first, most = (0, AHEAD) if block == 0 else (AHEAD, BACK)
                where = first + jnp.minimum(arrived, most - 1)
                code = boxes + where
                tab_ref[jnp.where(hit, slots + where, slots + AHEAD + BACK)] = count
                arrived = arrived + jnp.where(hit, one, none)
            tab_ref[jnp.where(hit, codes + jnp.minimum(count, CAP - 1), codes + CAP)] = code
            count = count + jnp.where(hit, one, none)
    for box in range(boxes):
        me = device * boxes + box
        for number in range(PARTNERS):
            other = part_ref[number, me]
            local = other - device * boxes
            base = pairs + (box * PARTNERS + number) * 4
            tab_ref[base] = jnp.where(local < 0, boxes, jnp.where(local >= boxes, boxes + 1, local))
            for axis, extent in enumerate((GRID_X, GRID_Y, GRID_Z)):
                moved = anc_ref[axis, other] - anc_ref[axis, me] + extent // 2
                moved = jnp.where(moved < 0, moved + extent, jnp.where(moved >= extent, moved - extent, moved))
                tab_ref[base + 1 + axis] = jnp.clip(moved - extent // 2, -(PAD - 4), PAD - 4)

    for spin in range(2):
        split_boxes(orb_ref, flat_ref, spin, boxes)

        def slabs(box, _):
            flat_to_slabs(
                lambda t: flat_ref[pl.ds(box + 8 * t, HALF, stride=8 * PAIRT), :],
                lambda u, parity, x: pad_ref.__setitem__(
                    (box, spin, u, pl.ds(PAD + parity, HALF, stride=2), slice(None)), x),
            )
            return 0

        lax.fori_loop(0, boxes, slabs, 0)

    def build(i, _):
        row = pl.multiple_of(i * 2 * EDGE, 16)
        for c in range(NSTEPS):
            cols = slice(c * NCHUNK, (c + 1) * NCHUNK)
            til = rep_ref[1, :, cols]
            first = rep_ref[0, pl.ds(2 * i, 1), cols] * til
            second = rep_ref[0, pl.ds(2 * i + 1, 1), cols] * til
            kron_ref[pl.ds(row, 2 * EDGE), cols] = jnp.concatenate([first, second], axis=0).astype(BF)
        return 0

    lax.fori_loop(0, HALF, build, 0)
    kron_ref[FACE:, :] = jnp.zeros((WIDE - FACE, NWIDE), BF)


def fill_kernel(old_ref, prev_ref, next_ref, pad_ref, flat_ref):
    boxes = pad_ref.shape[0] - 2
    for side, ref in ((0, prev_ref), (1, next_ref)):
        for spin in range(2):
            flat_ref[...] = ref[spin].astype(F32)
            flat_to_slabs(
                lambda t: flat_ref[pl.ds(t, HALF, stride=PAIRT), :],
                lambda u, parity, x: pad_ref.__setitem__(
                    (boxes + side, spin, u, pl.ds(PAD + parity, HALF, stride=2), slice(None)), x),
            )


def pair_kernel(start, held, spins, tab_ref, pad_ref, kron_ref, diag_ref, inv_ref, out_ref, *refs):
    sends, (mov_ref, x_ref, y_ref, res_ref) = refs[:-4], refs[-4:]
    boxes = pad_ref.shape[0] - 2
    pairs, _, _, leaves, order, _ = table_layout(boxes)
    lanes = lane_iota()
    rows = lax.broadcasted_iota(jnp.int32, (EDGE, 1), 0)

    def dense(index, _):
        box = tab_ref[order + start + index]
        places = []
        for number in range(PARTNERS):
            base = pairs + (box * PARTNERS + number) * 4
            source = tab_ref[base]
            da, db, dc = tab_ref[base + 1], tab_ref[base + 2], tab_ref[base + 3]
            offset = ZERO_TILES * LANES - (db * EDGE + dc)
            row_ok = jnp.abs(2 * (rows - da) - (EDGE - 1)) < EDGE
            places.append((source, da, db, dc, offset // LANES, offset % LANES, row_ok))
        last = [[None] * PARTNERS for _ in spins]
        for u in range(TILES + 1):
            keep = []
            for number in range(PARTNERS):
                source, da, db, dc, quotient, rest, row_ok = places[number]
                if u > 0:
                    cell = lanes + (u - 1) * LANES
                    b = (cell * 52429) >> 21
                    c = cell - b * EDGE
                    ok = (jnp.abs(2 * (b - db) - (EDGE - 1)) < EDGE) & (jnp.abs(2 * (c - dc) - (EDGE - 1)) < EDGE)
                    if u == TILES:
                        ok = ok & (lanes < FACE - (TILES - 1) * LANES)
                    keep.append(row_ok & ok)
            for at, spin in enumerate(spins):
                values = []
                for number in range(PARTNERS):
                    source, da, db, dc, quotient, rest, row_ok = places[number]
                    tile = jnp.clip(quotient + (u - ZERO_TILES), 0, TILES - 1)
                    x = pad_ref[source, spin, tile, pl.ds(PAD - da, EDGE), :]
                    turned = pltpu.roll(x, (LANES - rest) % LANES, 1)
                    if u > 0:
                        moved = jnp.where(keep[number], jnp.where(lanes < LANES - rest, last[at][number], turned), 0.0)
                        mov_ref[index, at, number, u - 1] = moved
                        values.append(pad_ref[box, spin, u - 1, pl.ds(PAD, EDGE), :] * moved)
                    last[at][number] = turned
                if u > 0:
                    both = jnp.concatenate(values, axis=0)
                    if u == TILES:
                        both = jnp.where(lanes < FACE - (TILES - 1) * LANES, both, 0.0)
                    first = (index * len(spins) + at) * PARTNERS * EDGE
                    x_ref[pl.ds(pl.multiple_of(first, 16), PARTNERS * EDGE),
                          (u - 1) * LANES:u * LANES] = both.astype(BF)
        return 0

    lax.fori_loop(0, held, dense, 0)

    cubes = held * len(spins) * PARTNERS
    diag = diag_ref[...]
    for c in range(NSTEPS):
        cols = slice(c * NCHUNK, min((c + 1) * NCHUNK, WIDE))
        y_ref[:, cols] = jnp.dot(diag, x_ref[:, cols], preferred_element_type=F32).astype(BF)

    def forward(n, _):
        cols = pl.ds(pl.multiple_of(n * NCHUNK, NCHUNK), NCHUNK)
        z = jnp.dot(y_ref[:, :WIDE], kron_ref[:, cols], preferred_element_type=F32)
        z = z.reshape(cubes, EDGE, NCHUNK) * inv_ref[:, cols][None]
        x_ref[:, cols] = z.reshape(cubes * EDGE, NCHUNK).astype(BF)
        return 0

    lax.fori_loop(0, NSTEPS, forward, 0)

    def backward(n, _):
        cols = pl.ds(pl.multiple_of(n * NCHUNK, NCHUNK), NCHUNK)
        y_ref[:, cols] = jnp.dot(x_ref[:, :WIDE], kron_ref[:, cols], preferred_element_type=F32).astype(BF)
        return 0

    lax.fori_loop(0, NSTEPS, backward, 0)

    for u in range(TILES):
        potential = jnp.dot(diag, y_ref[:, u * LANES:(u + 1) * LANES], preferred_element_type=F32)
        for index in range(held):
            for at in range(len(spins)):
                total = 0.0
                for number in range(PARTNERS):
                    first = ((index * len(spins) + at) * PARTNERS + number) * EDGE
                    total = total + potential[first:first + EDGE] * mov_ref[index, at, number, u]
                res_ref[index * len(spins) + at, u] = total

    def flatten(row, _):
        slabs_to_flat(
            lambda u, parity: res_ref[row, u, pl.ds(parity, HALF, stride=2), :],
            lambda t, x: out_ref.__setitem__((row, pl.ds(t, HALF, stride=PAIRT), slice(None)), x),
        )
        return 0

    lax.fori_loop(0, held * len(spins), flatten, 0)
    if sends:
        for k in range(AHEAD):
            sends[0][k] = out_ref[tab_ref[leaves + k]].astype(BF)
        for k in range(BACK):
            sends[1][k] = out_ref[tab_ref[leaves + AHEAD + k]].astype(BF)


def interleave(out, both_ref, load):
    for spin in range(2):
        both_ref[pl.ds(spin, FLAT, stride=2), :] = load(spin)

    def step(i, _):
        base = pl.multiple_of(i * PAIRT * LANES, LANES)
        chunk = both_ref[pl.ds(pl.multiple_of(i * 2 * PAIRT, 2), 2 * PAIRT), :]
        for j in range(PAIRT):
            out[:, pl.ds(pl.multiple_of(base + j * LANES, LANES), LANES)] = chunk[2 * j:2 * j + 2]
        return 0

    lax.fori_loop(0, HALF, step, 0)


def keep_kernel(tab_ref, low_ref, high_ref, rest_ref, out_ref, both_ref):
    first = low_ref.shape[0]
    boxes = first + rest_ref.shape[0] // 2
    code = tab_ref[table_layout(boxes)[1] + pl.program_id(0)]

    @pl.when(code < first)
    def _():
        spot = jnp.minimum(code, first - 1)
        interleave(out_ref.at[0], both_ref, lambda spin: (low_ref, high_ref)[spin][spot])

    @pl.when((code >= first) & (code < boxes))
    def _():
        spot = jnp.clip(code - first, 0, boxes - first - 1)
        interleave(out_ref.at[0], both_ref, lambda spin: rest_ref[2 * spot + spin])

    @pl.when(code >= boxes + AHEAD + BACK)
    def _():
        out_ref[...] = jnp.zeros_like(out_ref)


def place_kernel(boxes, tab_ref, prev_low, next_low, prev_high, next_high, kept_ref, out_ref, form_ref, both_ref, sems):
    slots = table_layout(boxes)[2]
    copies = []
    for k in range(AHEAD + BACK):
        pair, row = ((prev_low, prev_high), k) if k < AHEAD else ((next_low, next_high), k - AHEAD)
        slot = tab_ref[slots + k]
        copy = pltpu.make_async_copy(form_ref.at[k], out_ref.at[jnp.minimum(slot, CAP - 1)], sems.at[k])

        @pl.when(slot < CAP)
        def _():
            interleave(form_ref.at[k], both_ref, lambda spin: pair[spin][row].astype(F32))
            copy.start()

        copies.append((slot, copy))
    for slot, copy in copies:
        @pl.when(slot < CAP)
        def _():
            copy.wait()


def from_behind(value, steps):
    count = lax.axis_size(AXES)
    return lax.ppermute(value, AXES, [(source, (source + steps) % count) for source in range(count)])


def whole(count):
    return [pl.BlockSpec(memory_space=pltpu.VMEM)] * count


SCALARS = pl.BlockSpec(memory_space=pltpu.SMEM)
ANYWHERE = pl.BlockSpec(memory_space=pltpu.MemorySpace.HBM)


def cost(flops, size):
    return pl.CostEstimate(flops=flops, bytes_accessed=size, transcendentals=0)


def shards(orbitals, dest, partners, anchors):
    boxes = orbitals.shape[1]
    sine, inverse, repeated, tiled = tables()
    partners_t, anchors_t = partners.T, anchors.T

    windows = pl.pallas_call(
        window_kernel,
        out_shape=[jax.ShapeDtypeStruct((2, FLAT, LANES), BF)] * 2,
        in_specs=[SCALARS, ANYWHERE],
        out_specs=whole(2),
        scratch_shapes=[pltpu.VMEM(orbitals.shape, BF), pltpu.VMEM((FLAT * 8, LANES), F32),
                        pltpu.SemaphoreType.DMA((2,))],
        compiler_params=pltpu.CompilerParams(vmem_limit_bytes=66_300_000),
        name="window",
    )(partners_t, orbitals)
    from_prev = from_behind(windows[0], 1)
    from_next = from_behind(windows[1], -1)

    slabs = jax.ShapeDtypeStruct((boxes + 2, 2, TILES, ROWS, LANES), F32)
    pad, kron, table = pl.pallas_call(
        prepare_kernel,
        out_shape=[slabs,
                   jax.ShapeDtypeStruct((WIDE, NWIDE), BF),
                   jax.ShapeDtypeStruct((table_layout(boxes)[-1],), jnp.int32)],
        in_specs=[SCALARS] * 3 + whole(2),
        out_specs=whole(2) + [SCALARS],
        scratch_shapes=[pltpu.VMEM((FLAT * 8, LANES), F32)],
        compiler_params=pltpu.CompilerParams(vmem_limit_bytes=20 << 20),
        cost_estimate=cost(10_000_000, 10_000_000),
        name="prepare",
    )(dest, partners_t, anchors_t, orbitals, np.stack([repeated, tiled]))
    pad = pl.pallas_call(
        fill_kernel,
        out_shape=slabs,
        in_specs=whole(3),
        out_specs=pl.BlockSpec(memory_space=pltpu.VMEM),
        scratch_shapes=[pltpu.VMEM((FLAT, LANES), F32)],
        input_output_aliases={0: 0},
        compiler_params=pltpu.CompilerParams(vmem_limit_bytes=12 << 20),
        cost_estimate=cost(1_000_000, 2_000_000),
        name="fill",
    )(pad, from_prev, from_next)

    moving = AHEAD + BACK

    def solve(start, held, spins, send):
        cubes = held * len(spins) * PARTNERS
        diag = np.kron(np.eye(cubes, dtype=np.float32), sine).astype(jnp.bfloat16)
        shapes = [jax.ShapeDtypeStruct((held * len(spins), FLAT, LANES), F32)]
        if send:
            shapes += [jax.ShapeDtypeStruct((count, FLAT, LANES), BF) for count in (AHEAD, BACK)]
        return pl.pallas_call(
            lambda *refs: pair_kernel(start, held, spins, *refs),
            out_shape=shapes,
            in_specs=[SCALARS] + whole(4),
            out_specs=whole(len(shapes)),
            scratch_shapes=[
                pltpu.VMEM((held, len(spins), PARTNERS, TILES, EDGE, LANES), F32),
                pltpu.VMEM((cubes * EDGE, NWIDE), BF),
                pltpu.VMEM((cubes * EDGE, NWIDE), BF),
                pltpu.VMEM((held * len(spins), TILES, EDGE, LANES), F32),
            ],
            compiler_params=pltpu.CompilerParams(vmem_limit_bytes=20 << 20),
            cost_estimate=cost(4 * cubes * EDGE * FACE * FACE, 10_000_000),
        )(table, pad, kron, diag, inverse)

    terms, arrived = [], []
    for spin in range(2):
        mine, sent_ahead, sent_back = solve(0, moving, (spin,), True)
        terms.append(mine)
        ahead = from_behind(sent_ahead, 1)
        back = from_behind(sent_back, -1)
        arrived += [ahead, back]
    terms += solve(moving, boxes - moving, (0, 1), False)

    shape = jax.ShapeDtypeStruct((CAP, 2, FLAT * LANES), F32)
    kept = pl.pallas_call(
        keep_kernel,
        out_shape=shape,
        grid=(CAP,),
        in_specs=[SCALARS] + whole(3),
        out_specs=pl.BlockSpec((1, 2, FLAT * LANES), lambda i: (i, 0, 0)),
        scratch_shapes=[pltpu.VMEM((2 * FLAT, LANES), F32)],
        compiler_params=pltpu.CompilerParams(vmem_limit_bytes=8 << 20),
        cost_estimate=cost(1_000_000, 8_000_000),
        name="keep",
    )(table, *terms)
    placed = pl.pallas_call(
        lambda *refs: place_kernel(boxes, *refs),
        out_shape=shape,
        in_specs=[SCALARS] + whole(4) + [ANYWHERE],
        out_specs=ANYWHERE,
        scratch_shapes=[pltpu.VMEM((AHEAD + BACK, 2, FLAT * LANES), F32), pltpu.VMEM((2 * FLAT, LANES), F32),
                        pltpu.SemaphoreType.DMA((AHEAD + BACK,))],
        input_output_aliases={5: 0},
        compiler_params=pltpu.CompilerParams(vmem_limit_bytes=8 << 20),
        cost_estimate=cost(1_000_000, 4_000_000),
        name="place",
    )(table, *arrived, kept)
    return jnp.transpose(placed, (1, 0, 2))


def solution(mesh):
    return jax.shard_map(
        shards,
        mesh=mesh,
        in_specs=(P(None, AXES, None), P(), P(), P()),
        out_specs=P(None, AXES, None),
        check_vma=False,
    )
```

```python
import jax
import jax.numpy as jnp
import numpy as np
from jax import lax
from jax.experimental import pallas as pl
from jax.experimental.pallas import tpu as pltpu
from jax.sharding import PartitionSpec as P


EDGE = 40
PARTNERS = 2
GRID_X = 768
GRID_Y = 384
GRID_Z = 384
BACK = 2
AHEAD = 1
CAP = 7
SCREEN = 0.001

AXES = ("gx", "gy", "gz")
LANES = 128
FACE = EDGE * EDGE
TILES = -(-FACE // LANES)
WIDE = TILES * LANES
NCHUNK = 256
NSTEPS = -(-FACE // NCHUNK)
NWIDE = NSTEPS * NCHUNK
FLAT = EDGE ** 3 // LANES
HALF = EDGE // 2
PAIRT = 2 * FACE // LANES
PAD = 24
ROWS = EDGE + 2 * PAD
ZERO_TILES = 7
BF = jnp.bfloat16
F32 = jnp.float32


def tables():
    counter = np.arange(EDGE, dtype=np.float32) + 1.0
    angles = np.float32(np.pi) * counter[:, None] * counter[None, :] / np.float32(EDGE + 1.0)
    sine = (np.sqrt(np.float32(2.0 / (EDGE + 1.0))) * np.sin(angles)).astype(jnp.bfloat16)
    sine = sine.astype(np.float32)
    levels = 2.0 - 2.0 * np.cos(np.pi * counter.astype(np.float64) / (EDGE + 1.0))
    lam = levels[:, None, None] + levels[None, :, None] + levels[None, None, :] + SCREEN
    inverse = np.zeros((EDGE, NWIDE), np.float32)
    inverse[:, :FACE] = (1.0 / lam).reshape(EDGE, FACE)
    repeated = np.zeros((EDGE, NWIDE), np.float32)
    repeated[:, :FACE] = np.repeat(sine, EDGE, axis=1)
    tiled = np.zeros((EDGE, NWIDE), np.float32)
    tiled[:, :FACE] = np.tile(sine, (1, EDGE))
    return sine, inverse, repeated, tiled


def lane_iota():
    return lax.broadcasted_iota(jnp.int32, (1, LANES), 1)


def split_boxes(orb_ref, flat_ref, boxes):
    def step(i, _):
        base = pl.multiple_of(i * PAIRT * LANES, LANES)
        x = orb_ref[:, pl.ds(base, PAIRT * LANES)].astype(F32)
        for j in range(PAIRT):
            flat_ref[pl.ds(pl.multiple_of((i * PAIRT + j) * 8, 8), boxes), :] = x[:, j * LANES:(j + 1) * LANES]
        return 0

    lax.fori_loop(0, HALF, step, 0)


def flat_to_slabs(load, store):
    low = lane_iota() < LANES // 2
    rolled = None
    for t in range(PAIRT):
        x = load(t)
        if t < TILES:
            store(t, 0, x)
        if t >= TILES - 1:
            turned = pltpu.roll(x, LANES // 2, 1)
            if rolled is not None:
                store(t - TILES, 1, jnp.where(low, rolled, turned))
            rolled = turned
    store(TILES - 1, 1, rolled)


def slabs_to_flat(load, store):
    low = lane_iota() < LANES // 2
    for t in range(TILES - 1):
        store(t, load(t, 0))
    before = load(TILES - 1, 0)
    for v in range(TILES):
        turned = pltpu.roll(load(v, 1), LANES // 2, 1)
        store(TILES - 1 + v, jnp.where(low, before, turned))
        before = turned


def wanted_boxes(part_ref, boxes):
    total = part_ref.shape[1]
    device = lax.axis_index(AXES)
    wanted = []
    for step in (1, -1):
        found = jnp.int32(0)
        for k in range(boxes):
            other = (device + step) * boxes + k
            inside = (other >= 0) & (other < total)
            for number in range(PARTNERS):
                local = part_ref[number, jnp.clip(other, 0, total - 1)] - device * boxes
                found = jnp.where(inside & (local >= 0) & (local < boxes), local, found)
        wanted.append(found)
    return wanted


def window_kernel(dest_hbm, part_hbm, anc_hbm, orb_hbm, ahead_low, back_low, ahead_high, back_high, tab_ref,
                  dest_ref, part_ref, anc_ref, orb_ref, flat_ref, sems):
    boxes = orb_ref.shape[1]
    small = [pltpu.make_async_copy(source, target, sems.at[k]) for k, (source, target) in enumerate(
        ((part_hbm, part_ref), (dest_hbm, dest_ref), (anc_hbm, anc_ref)))]
    large = [pltpu.make_async_copy(orb_hbm.at[spin], orb_ref.at[spin], sems.at[3 + spin]) for spin in range(2)]
    for copy in (small[0], large[0], small[1], small[2], large[1]):
        copy.start()
    for copy in small:
        copy.wait()
    wanted = wanted_boxes(part_ref, boxes)
    build_tables(dest_ref, part_ref, anc_ref, tab_ref, boxes)
    for spin, refs in enumerate(((ahead_low, back_low), (ahead_high, back_high))):
        large[spin].wait()
        split_boxes(orb_ref.at[spin], flat_ref, boxes)
        for side, ref in enumerate(refs):
            ref[...] = flat_ref[pl.ds(wanted[side], FLAT, stride=8), :].astype(BF)


def table_layout(boxes):
    pairs = 0
    codes = pairs + boxes * PARTNERS * 4
    slots = codes + CAP + 1
    leaves = slots + AHEAD + BACK + 1
    order = leaves + AHEAD + BACK + 1
    return pairs, codes, slots, leaves, order, order + boxes


def build_tables(dest_ref, part_ref, anc_ref, tab_ref, boxes):
    total = part_ref.shape[1]
    device = lax.axis_index(AXES)
    pairs, codes, slots, leaves, order, _ = table_layout(boxes)
    one, none = jnp.int32(1), jnp.int32(0)
    for k in range(CAP + 1):
        tab_ref[codes + k] = boxes + AHEAD + BACK
    for k in range(AHEAD + BACK + 1):
        tab_ref[slots + k] = CAP
        tab_ref[leaves + k] = 0
    goes = [dest_ref[device * boxes + k] for k in range(boxes)]
    ahead_all, back_all = none, none
    for k in range(boxes):
        ahead_all = ahead_all + jnp.where(goes[k] == device + 1, one, none)
        back_all = back_all + jnp.where(goes[k] == device - 1, one, none)
    ahead, back, stay = none, none, none
    spots = []
    for k in range(boxes):
        is_ahead, is_back = goes[k] == device + 1, goes[k] == device - 1
        spot = jnp.where(is_ahead, ahead, jnp.where(is_back, ahead_all + back, ahead_all + back_all + stay))
        spots.append(spot)
        tab_ref[order + spot] = k
        spare = leaves + AHEAD + BACK
        tab_ref[jnp.where(is_ahead, leaves + jnp.minimum(ahead, AHEAD - 1), spare)] = spot
        tab_ref[jnp.where(is_back, leaves + AHEAD + jnp.minimum(back, BACK - 1), spare)] = spot
        ahead = ahead + jnp.where(is_ahead, one, none)
        back = back + jnp.where(is_back, one, none)
        stay = stay + jnp.where(is_ahead | is_back, none, one)
    count = none
    for block in range(3):
        arrived = none
        for k in range(boxes):
            box = (device + (block - 1)) * boxes + k
            hit = (box >= 0) & (box < total) & (dest_ref[jnp.clip(box, 0, total - 1)] == device)
            if block == 1:
                code = spots[k]
            else:
                first, most = (0, AHEAD) if block == 0 else (AHEAD, BACK)
                where = first + jnp.minimum(arrived, most - 1)
                code = boxes + where
                tab_ref[jnp.where(hit, slots + where, slots + AHEAD + BACK)] = count
                arrived = arrived + jnp.where(hit, one, none)
            tab_ref[jnp.where(hit, codes + jnp.minimum(count, CAP - 1), codes + CAP)] = code
            count = count + jnp.where(hit, one, none)
    for box in range(boxes):
        me = device * boxes + box
        for number in range(PARTNERS):
            other = part_ref[number, me]
            local = other - device * boxes
            base = pairs + (box * PARTNERS + number) * 4
            tab_ref[base] = jnp.where(local < 0, boxes, jnp.where(local >= boxes, boxes + 1, local))
            for axis, extent in enumerate((GRID_X, GRID_Y, GRID_Z)):
                moved = anc_ref[axis, other] - anc_ref[axis, me] + extent // 2
                moved = jnp.where(moved < 0, moved + extent, jnp.where(moved >= extent, moved - extent, moved))
                tab_ref[base + 1 + axis] = jnp.clip(moved - extent // 2, -(PAD - 4), PAD - 4)


def prepare_kernel(orb_hbm, rep_hbm, low_ref, high_ref, kron_ref, orb_ref, rep_ref, flat_ref, sems):
    boxes = orb_ref.shape[1]
    copies = [pltpu.make_async_copy(orb_hbm.at[spin], orb_ref.at[spin], sems.at[spin]) for spin in range(2)]
    copies.append(pltpu.make_async_copy(rep_hbm, rep_ref, sems.at[2]))
    for copy in copies:
        copy.start()
    for spin, pad_ref in enumerate((low_ref, high_ref)):
        copies[spin].wait()
        split_boxes(orb_ref.at[spin], flat_ref, boxes)

        def slabs(box, _):
            flat_to_slabs(
                lambda t: flat_ref[pl.ds(box + 8 * t, HALF, stride=8 * PAIRT), :],
                lambda u, parity, x: pad_ref.__setitem__(
                    (box, u, pl.ds(PAD + parity, HALF, stride=2), slice(None)), x),
            )
            return 0

        lax.fori_loop(0, boxes, slabs, 0)

    copies[2].wait()

    def build(i, _):
        row = pl.multiple_of(i * 2 * EDGE, 16)
        for c in range(NSTEPS):
            cols = slice(c * NCHUNK, (c + 1) * NCHUNK)
            til = rep_ref[1, :, cols]
            first = rep_ref[0, pl.ds(2 * i, 1), cols] * til
            second = rep_ref[0, pl.ds(2 * i + 1, 1), cols] * til
            kron_ref[pl.ds(row, 2 * EDGE), cols] = jnp.concatenate([first, second], axis=0).astype(BF)
        return 0

    lax.fori_loop(0, HALF, build, 0)
    kron_ref[FACE:, :] = jnp.zeros((WIDE - FACE, NWIDE), BF)


def fill_kernel(old_ref, prev_ref, next_ref, pad_ref, flat_ref):
    boxes = pad_ref.shape[0] - 2
    for side, ref in ((0, prev_ref), (1, next_ref)):
        flat_ref[...] = ref[...].astype(F32)
        flat_to_slabs(
            lambda t: flat_ref[pl.ds(t, HALF, stride=PAIRT), :],
            lambda u, parity, x: pad_ref.__setitem__(
                (boxes + side, u, pl.ds(PAD + parity, HALF, stride=2), slice(None)), x),
        )


def pair_kernel(start, held, spins, tab_ref, kron_ref, diag_ref, inv_ref, *refs):
    pads, out_ref, sends = refs[:len(spins)], refs[len(spins)], refs[len(spins) + 1:-4]
    mov_ref, x_ref, y_ref, res_ref = refs[-4:]
    boxes = pads[0].shape[0] - 2
    pairs, _, _, leaves, order, _ = table_layout(boxes)
    lanes = lane_iota()
    rows = lax.broadcasted_iota(jnp.int32, (EDGE, 1), 0)

    def dense(index, _):
        box = tab_ref[order + start + index]
        places = []
        for number in range(PARTNERS):
            base = pairs + (box * PARTNERS + number) * 4
            source = tab_ref[base]
            da, db, dc = tab_ref[base + 1], tab_ref[base + 2], tab_ref[base + 3]
            offset = ZERO_TILES * LANES - (db * EDGE + dc)
            row_ok = jnp.abs(2 * (rows - da) - (EDGE - 1)) < EDGE
            places.append((source, da, db, dc, offset // LANES, offset % LANES, row_ok))
        last = [[None] * PARTNERS for _ in spins]
        for u in range(TILES + 1):
            keep = []
            for number in range(PARTNERS):
                source, da, db, dc, quotient, rest, row_ok = places[number]
                if u > 0:
                    cell = lanes + (u - 1) * LANES
                    b = (cell * 52429) >> 21
                    c = cell - b * EDGE
                    ok = (jnp.abs(2 * (b - db) - (EDGE - 1)) < EDGE) & (jnp.abs(2 * (c - dc) - (EDGE - 1)) < EDGE)
                    if u == TILES:
                        ok = ok & (lanes < FACE - (TILES - 1) * LANES)
                    keep.append(row_ok & ok)
            for at, pad_ref in enumerate(pads):
                values = []
                for number in range(PARTNERS):
                    source, da, db, dc, quotient, rest, row_ok = places[number]
                    tile = jnp.clip(quotient + (u - ZERO_TILES), 0, TILES - 1)
                    x = pad_ref[source, tile, pl.ds(PAD - da, EDGE), :]
                    turned = pltpu.roll(x, (LANES - rest) % LANES, 1)
                    if u > 0:
                        moved = jnp.where(keep[number], jnp.where(lanes < LANES - rest, last[at][number], turned), 0.0)
                        mov_ref[index, at, number, u - 1] = moved
                        values.append(pad_ref[box, u - 1, pl.ds(PAD, EDGE), :] * moved)
                    last[at][number] = turned
                if u > 0:
                    both = jnp.concatenate(values, axis=0)
                    if u == TILES:
                        both = jnp.where(lanes < FACE - (TILES - 1) * LANES, both, 0.0)
                    first = (index * len(spins) + at) * PARTNERS * EDGE
                    x_ref[pl.ds(pl.multiple_of(first, 16), PARTNERS * EDGE),
                          (u - 1) * LANES:u * LANES] = both.astype(BF)
        return 0

    lax.fori_loop(0, held, dense, 0)

    cubes = held * len(spins) * PARTNERS
    diag = diag_ref[...]
    for c in range(NSTEPS):
        cols = slice(c * NCHUNK, min((c + 1) * NCHUNK, WIDE))
        y_ref[:, cols] = jnp.dot(diag, x_ref[:, cols], preferred_element_type=F32).astype(BF)

    def forward(n, _):
        cols = pl.ds(pl.multiple_of(n * NCHUNK, NCHUNK), NCHUNK)
        z = jnp.dot(y_ref[:, :WIDE], kron_ref[:, cols], preferred_element_type=F32)
        z = z.reshape(cubes, EDGE, NCHUNK) * inv_ref[:, cols][None]
        x_ref[:, cols] = z.reshape(cubes * EDGE, NCHUNK).astype(BF)
        return 0

    lax.fori_loop(0, NSTEPS, forward, 0)

    def backward(n, _):
        cols = pl.ds(pl.multiple_of(n * NCHUNK, NCHUNK), NCHUNK)
        y_ref[:, cols] = jnp.dot(x_ref[:, :WIDE], kron_ref[:, cols], preferred_element_type=F32).astype(BF)
        return 0

    lax.fori_loop(0, NSTEPS, backward, 0)

    for u in range(TILES):
        potential = jnp.dot(diag, y_ref[:, u * LANES:(u + 1) * LANES], preferred_element_type=F32)
        for index in range(held):
            for at in range(len(spins)):
                total = 0.0
                for number in range(PARTNERS):
                    first = ((index * len(spins) + at) * PARTNERS + number) * EDGE
                    total = total + potential[first:first + EDGE] * mov_ref[index, at, number, u]
                res_ref[index * len(spins) + at, u] = total

    def flatten(row, _):
        slabs_to_flat(
            lambda u, parity: res_ref[row, u, pl.ds(parity, HALF, stride=2), :],
            lambda t, x: out_ref.__setitem__((row, pl.ds(t, HALF, stride=PAIRT), slice(None)), x),
        )
        return 0

    lax.fori_loop(0, held * len(spins), flatten, 0)
    if sends:
        for k in range(AHEAD):
            sends[0][k] = out_ref[tab_ref[leaves + k]].astype(BF)
        for k in range(BACK):
            sends[1][k] = out_ref[tab_ref[leaves + AHEAD + k]].astype(BF)


def keep_kernel(tab_ref, low_ref, high_ref, rest_ref, out_ref):
    first = low_ref.shape[0]
    boxes = first + rest_ref.shape[0] // 2
    code = tab_ref[table_layout(boxes)[1] + pl.program_id(0)]

    @pl.when(code < first)
    def _():
        spot = jnp.minimum(code, first - 1)
        for spin, ref in enumerate((low_ref, high_ref)):
            out_ref[0, pl.ds(spin, FLAT, stride=2), :] = ref[spot]

    @pl.when((code >= first) & (code < boxes))
    def _():
        spot = jnp.clip(code - first, 0, boxes - first - 1)
        for spin in range(2):
            out_ref[0, pl.ds(spin, FLAT, stride=2), :] = rest_ref[2 * spot + spin]

    @pl.when(code >= boxes + AHEAD + BACK)
    def _():
        out_ref[...] = jnp.zeros_like(out_ref)


def place_kernel(boxes, tab_ref, prev_low, next_low, prev_high, next_high, kept_ref, out_ref, form_ref, sems):
    slots = table_layout(boxes)[2]
    copies = []
    for k in range(AHEAD + BACK):
        pair, row = ((prev_low, prev_high), k) if k < AHEAD else ((next_low, next_high), k - AHEAD)
        slot = tab_ref[slots + k]
        copy = pltpu.make_async_copy(form_ref.at[k], out_ref.at[jnp.minimum(slot, CAP - 1)], sems.at[k])

        @pl.when(slot < CAP)
        def _():
            for spin, ref in enumerate(pair):
                form_ref[k, pl.ds(spin, FLAT, stride=2), :] = ref[row].astype(F32)
            copy.start()

        copies.append((slot, copy))
    for slot, copy in copies:
        @pl.when(slot < CAP)
        def _():
            copy.wait()


def from_behind(value, steps):
    count = lax.axis_size(AXES)
    return lax.ppermute(value, AXES, [(source, (source + steps) % count) for source in range(count)])


def whole(count):
    return [pl.BlockSpec(memory_space=pltpu.VMEM)] * count


SCALARS = pl.BlockSpec(memory_space=pltpu.SMEM)
ANYWHERE = pl.BlockSpec(memory_space=pltpu.MemorySpace.HBM)


def in_place(value):
    return pltpu.with_memory_space_constraint(jnp.asarray(value), pltpu.HBM)


def cost(flops, size):
    return pl.CostEstimate(flops=flops, bytes_accessed=size, transcendentals=0)


def shards(orbitals, dest, partners, anchors):
    boxes = orbitals.shape[1]
    sine, inverse, repeated, tiled = tables()
    partners_t, anchors_t = partners.T, anchors.T

    box = jax.ShapeDtypeStruct((FLAT, LANES), BF)
    splitter = pltpu.VMEM((FLAT * 8, LANES), F32)
    ahead_low, back_low, ahead_high, back_high, table = pl.pallas_call(
        window_kernel,
        out_shape=[box] * 4 + [jax.ShapeDtypeStruct((table_layout(boxes)[-1],), jnp.int32)],
        in_specs=[ANYWHERE] * 4,
        out_specs=whole(4) + [SCALARS],
        scratch_shapes=[pltpu.SMEM(dest.shape, jnp.int32), pltpu.SMEM(partners_t.shape, jnp.int32),
                        pltpu.SMEM(anchors_t.shape, jnp.int32), pltpu.VMEM(orbitals.shape, BF),
                        splitter, pltpu.SemaphoreType.DMA((5,))],
        compiler_params=pltpu.CompilerParams(vmem_limit_bytes=12 << 20),
        name="window",
    )(*map(in_place, (dest, partners_t, anchors_t, orbitals)))
    prev_low = from_behind(ahead_low, 1)
    next_low = from_behind(back_low, -1)
    prev_high = from_behind(ahead_high, 1)
    next_high = from_behind(back_high, -1)

    slabs = jax.ShapeDtypeStruct((boxes + 2, TILES, ROWS, LANES), F32)
    constants = np.stack([repeated, tiled])
    *pads, kron = pl.pallas_call(
        prepare_kernel,
        out_shape=[slabs, slabs, jax.ShapeDtypeStruct((WIDE, NWIDE), BF)],
        in_specs=[ANYWHERE] * 2,
        out_specs=whole(3),
        scratch_shapes=[pltpu.VMEM(orbitals.shape, BF), pltpu.VMEM(constants.shape, F32), splitter,
                        pltpu.SemaphoreType.DMA((3,))],
        compiler_params=pltpu.CompilerParams(vmem_limit_bytes=20 << 20),
        cost_estimate=cost(10_000_000, 10_000_000),
        name="prepare",
    )(in_place(orbitals), in_place(constants))
    for spin, halo in enumerate(((prev_low, next_low), (prev_high, next_high))):
        pads[spin] = pl.pallas_call(
            fill_kernel,
            out_shape=slabs,
            in_specs=whole(3),
            out_specs=pl.BlockSpec(memory_space=pltpu.VMEM),
            scratch_shapes=[pltpu.VMEM((FLAT, LANES), F32)],
            input_output_aliases={0: 0},
            compiler_params=pltpu.CompilerParams(vmem_limit_bytes=12 << 20),
            cost_estimate=cost(1_000_000, 2_000_000),
        )(pads[spin], *halo)

    moving = AHEAD + BACK

    def solve(start, held, spins, send):
        cubes = held * len(spins) * PARTNERS
        diag = np.kron(np.eye(cubes, dtype=np.float32), sine).astype(jnp.bfloat16)
        shapes = [jax.ShapeDtypeStruct((held * len(spins), FLAT, LANES), F32)]
        if send:
            shapes += [jax.ShapeDtypeStruct((count, FLAT, LANES), BF) for count in (AHEAD, BACK)]
        return pl.pallas_call(
            lambda *refs: pair_kernel(start, held, spins, *refs),
            out_shape=shapes,
            in_specs=[SCALARS] + whole(3 + len(spins)),
            out_specs=whole(len(shapes)),
            scratch_shapes=[
                pltpu.VMEM((held, len(spins), PARTNERS, TILES, EDGE, LANES), F32),
                pltpu.VMEM((cubes * EDGE, NWIDE), BF),
                pltpu.VMEM((cubes * EDGE, NWIDE), BF),
                pltpu.VMEM((held * len(spins), TILES, EDGE, LANES), F32),
            ],
            compiler_params=pltpu.CompilerParams(vmem_limit_bytes=20 << 20),
            cost_estimate=cost(4 * cubes * EDGE * FACE * FACE, 10_000_000),
        )(table, kron, diag, inverse, *[pads[spin] for spin in spins])

    terms, arrived = [], []
    for spin in range(2):
        mine, sent_ahead, sent_back = solve(0, moving, (spin,), True)
        terms.append(mine)
        ahead = from_behind(sent_ahead, 1)
        back = from_behind(sent_back, -1)
        arrived += [ahead, back]
    terms += solve(moving, boxes - moving, (0, 1), False)

    shape = jax.ShapeDtypeStruct((CAP, 2 * FLAT, LANES), F32)
    kept = pl.pallas_call(
        keep_kernel,
        out_shape=shape,
        grid=(CAP,),
        in_specs=[SCALARS] + whole(3),
        out_specs=pl.BlockSpec((1, 2 * FLAT, LANES), lambda i: (i, 0, 0)),
        compiler_params=pltpu.CompilerParams(vmem_limit_bytes=8 << 20),
        cost_estimate=cost(1_000_000, 8_000_000),
        name="keep",
    )(table, *terms)
    placed = pl.pallas_call(
        lambda *refs: place_kernel(boxes, *refs),
        out_shape=shape,
        in_specs=[SCALARS] + whole(4) + [ANYWHERE],
        out_specs=ANYWHERE,
        scratch_shapes=[pltpu.VMEM((AHEAD + BACK, 2 * FLAT, LANES), F32),
                        pltpu.SemaphoreType.DMA((AHEAD + BACK,))],
        input_output_aliases={5: 0},
        compiler_params=pltpu.CompilerParams(vmem_limit_bytes=8 << 20),
        cost_estimate=cost(1_000_000, 4_000_000),
        name="place",
    )(table, *arrived, kept)
    placed = placed.reshape(-1).reshape(CAP, FLAT, 2, LANES).transpose(0, 2, 1, 3)
    return placed.reshape(CAP, 2, FLAT * LANES).transpose(1, 0, 2)


def solution(mesh):
    return jax.shard_map(
        shards,
        mesh=mesh,
        in_specs=(P(None, AXES, None), P(), P(), P()),
        out_specs=P(None, AXES, None),
        check_vma=False,
    )
```

```python
import jax
import jax.numpy as jnp
import numpy as np
from jax import lax
from jax.experimental import pallas as pl
from jax.experimental.pallas import tpu as pltpu
from jax.sharding import PartitionSpec as P


EDGE = 40
PARTNERS = 2
GRID_X = 768
GRID_Y = 384
GRID_Z = 384
BACK = 2
AHEAD = 1
CAP = 7
SCREEN = 0.001

AXES = ("gx", "gy", "gz")
LANES = 128
FACE = EDGE * EDGE
TILES = -(-FACE // LANES)
WIDE = TILES * LANES
NCHUNK = 256
NSTEPS = -(-FACE // NCHUNK)
NWIDE = NSTEPS * NCHUNK
FLAT = EDGE ** 3 // LANES
HALF = EDGE // 2
PAIRT = 2 * FACE // LANES
PAD = 24
ROWS = EDGE + 2 * PAD
ZERO_TILES = 7
BF = jnp.bfloat16
F32 = jnp.float32


def tables():
    counter = np.arange(EDGE, dtype=np.float32) + 1.0
    angles = np.float32(np.pi) * counter[:, None] * counter[None, :] / np.float32(EDGE + 1.0)
    sine = (np.sqrt(np.float32(2.0 / (EDGE + 1.0))) * np.sin(angles)).astype(jnp.bfloat16)
    sine = sine.astype(np.float32)
    levels = 2.0 - 2.0 * np.cos(np.pi * counter.astype(np.float64) / (EDGE + 1.0))
    lam = levels[:, None, None] + levels[None, :, None] + levels[None, None, :] + SCREEN
    inverse = np.zeros((EDGE, NWIDE), np.float32)
    inverse[:, :FACE] = (1.0 / lam).reshape(EDGE, FACE)
    repeated = np.zeros((EDGE, NWIDE), np.float32)
    repeated[:, :FACE] = np.repeat(sine, EDGE, axis=1)
    tiled = np.zeros((EDGE, NWIDE), np.float32)
    tiled[:, :FACE] = np.tile(sine, (1, EDGE))
    return sine, inverse, repeated, tiled


def lane_iota():
    return lax.broadcasted_iota(jnp.int32, (1, LANES), 1)


def split_boxes(orb_ref, flat_ref, boxes):
    def step(i, _):
        base = pl.multiple_of(i * PAIRT * LANES, LANES)
        x = orb_ref[:, pl.ds(base, PAIRT * LANES)].astype(F32)
        for j in range(PAIRT):
            flat_ref[pl.ds(pl.multiple_of((i * PAIRT + j) * 8, 8), boxes), :] = x[:, j * LANES:(j + 1) * LANES]
        return 0

    lax.fori_loop(0, HALF, step, 0)


def flat_to_slabs(load, store):
    low = lane_iota() < LANES // 2
    rolled = None
    for t in range(PAIRT):
        x = load(t)
        if t < TILES:
            store(t, 0, x)
        if t >= TILES - 1:
            turned = pltpu.roll(x, LANES // 2, 1)
            if rolled is not None:
                store(t - TILES, 1, jnp.where(low, rolled, turned))
            rolled = turned
    store(TILES - 1, 1, rolled)


def slabs_to_flat(load, store):
    low = lane_iota() < LANES // 2
    for t in range(TILES - 1):
        store(t, load(t, 0))
    before = load(TILES - 1, 0)
    for v in range(TILES):
        turned = pltpu.roll(load(v, 1), LANES // 2, 1)
        store(TILES - 1 + v, jnp.where(low, before, turned))
        before = turned


def wanted_boxes(part_ref, boxes):
    total = part_ref.shape[1]
    device = lax.axis_index(AXES)
    wanted = []
    for step in (1, -1):
        found = jnp.int32(0)
        for k in range(boxes):
            other = (device + step) * boxes + k
            inside = (other >= 0) & (other < total)
            for number in range(PARTNERS):
                local = part_ref[number, jnp.clip(other, 0, total - 1)] - device * boxes
                found = jnp.where(inside & (local >= 0) & (local < boxes), local, found)
        wanted.append(found)
    return wanted


def window_kernel(dest_hbm, part_hbm, anc_hbm, orb_hbm, ahead_low, back_low, ahead_high, back_high, tab_ref,
                  dest_ref, part_ref, anc_ref, orb_ref, flat_ref, sems):
    boxes = orb_ref.shape[1]
    small = [pltpu.make_async_copy(source, target, sems.at[k]) for k, (source, target) in enumerate(
        ((part_hbm, part_ref), (dest_hbm, dest_ref), (anc_hbm, anc_ref)))]
    large = [pltpu.make_async_copy(orb_hbm.at[spin], orb_ref.at[spin], sems.at[3 + spin]) for spin in range(2)]
    for copy in (small[0], large[0], small[1], small[2], large[1]):
        copy.start()
    for copy in small:
        copy.wait()
    wanted = wanted_boxes(part_ref, boxes)
    build_tables(dest_ref, part_ref, anc_ref, tab_ref, boxes)
    for spin, refs in enumerate(((ahead_low, back_low), (ahead_high, back_high))):
        large[spin].wait()
        split_boxes(orb_ref.at[spin], flat_ref, boxes)
        for side, ref in enumerate(refs):
            ref[...] = flat_ref[pl.ds(wanted[side], FLAT, stride=8), :].astype(BF)


def table_layout(boxes):
    pairs = 0
    codes = pairs + boxes * PARTNERS * 4
    slots = codes + CAP + 1
    leaves = slots + AHEAD + BACK + 1
    order = leaves + AHEAD + BACK + 1
    return pairs, codes, slots, leaves, order, order + boxes


def build_tables(dest_ref, part_ref, anc_ref, tab_ref, boxes):
    total = part_ref.shape[1]
    device = lax.axis_index(AXES)
    pairs, codes, slots, leaves, order, _ = table_layout(boxes)
    one, none = jnp.int32(1), jnp.int32(0)
    for k in range(CAP + 1):
        tab_ref[codes + k] = boxes + AHEAD + BACK
    for k in range(AHEAD + BACK + 1):
        tab_ref[slots + k] = CAP
        tab_ref[leaves + k] = 0
    goes = [dest_ref[device * boxes + k] for k in range(boxes)]
    ahead_all, back_all = none, none
    for k in range(boxes):
        ahead_all = ahead_all + jnp.where(goes[k] == device + 1, one, none)
        back_all = back_all + jnp.where(goes[k] == device - 1, one, none)
    ahead, back, stay = none, none, none
    spots = []
    for k in range(boxes):
        is_ahead, is_back = goes[k] == device + 1, goes[k] == device - 1
        spot = jnp.where(is_ahead, ahead, jnp.where(is_back, ahead_all + back, ahead_all + back_all + stay))
        spots.append(spot)
        tab_ref[order + spot] = k
        spare = leaves + AHEAD + BACK
        tab_ref[jnp.where(is_ahead, leaves + jnp.minimum(ahead, AHEAD - 1), spare)] = spot
        tab_ref[jnp.where(is_back, leaves + AHEAD + jnp.minimum(back, BACK - 1), spare)] = spot
        ahead = ahead + jnp.where(is_ahead, one, none)
        back = back + jnp.where(is_back, one, none)
        stay = stay + jnp.where(is_ahead | is_back, none, one)
    count = none
    for block in range(3):
        arrived = none
        for k in range(boxes):
            box = (device + (block - 1)) * boxes + k
            hit = (box >= 0) & (box < total) & (dest_ref[jnp.clip(box, 0, total - 1)] == device)
            if block == 1:
                code = spots[k]
            else:
                first, most = (0, AHEAD) if block == 0 else (AHEAD, BACK)
                where = first + jnp.minimum(arrived, most - 1)
                code = boxes + where
                tab_ref[jnp.where(hit, slots + where, slots + AHEAD + BACK)] = count
                arrived = arrived + jnp.where(hit, one, none)
            tab_ref[jnp.where(hit, codes + jnp.minimum(count, CAP - 1), codes + CAP)] = code
            count = count + jnp.where(hit, one, none)
    for box in range(boxes):
        me = device * boxes + box
        for number in range(PARTNERS):
            other = part_ref[number, me]
            local = other - device * boxes
            base = pairs + (box * PARTNERS + number) * 4
            tab_ref[base] = jnp.where(local < 0, boxes, jnp.where(local >= boxes, boxes + 1, local))
            for axis, extent in enumerate((GRID_X, GRID_Y, GRID_Z)):
                moved = anc_ref[axis, other] - anc_ref[axis, me] + extent // 2
                moved = jnp.where(moved < 0, moved + extent, jnp.where(moved >= extent, moved - extent, moved))
                tab_ref[base + 1 + axis] = jnp.clip(moved - extent // 2, -(PAD - 4), PAD - 4)


def prepare_kernel(orb_hbm, rep_hbm, low_ref, high_ref, kron_ref, orb_ref, rep_ref, flat_ref, sems):
    boxes = orb_ref.shape[1]
    copies = [pltpu.make_async_copy(orb_hbm.at[spin], orb_ref.at[spin], sems.at[spin]) for spin in range(2)]
    copies.append(pltpu.make_async_copy(rep_hbm, rep_ref, sems.at[2]))
    for copy in copies:
        copy.start()
    for spin, pad_ref in enumerate((low_ref, high_ref)):
        copies[spin].wait()
        split_boxes(orb_ref.at[spin], flat_ref, boxes)

        def slabs(box, _):
            flat_to_slabs(
                lambda t: flat_ref[pl.ds(box + 8 * t, HALF, stride=8 * PAIRT), :],
                lambda u, parity, x: pad_ref.__setitem__(
                    (box, u, pl.ds(PAD + parity, HALF, stride=2), slice(None)), x),
            )
            return 0

        lax.fori_loop(0, boxes, slabs, 0)

    copies[2].wait()

    def build(i, _):
        row = pl.multiple_of(i * 2 * EDGE, 16)
        for c in range(NSTEPS):
            cols = slice(c * NCHUNK, (c + 1) * NCHUNK)
            til = rep_ref[1, :, cols]
            first = rep_ref[0, pl.ds(2 * i, 1), cols] * til
            second = rep_ref[0, pl.ds(2 * i + 1, 1), cols] * til
            kron_ref[pl.ds(row, 2 * EDGE), cols] = jnp.concatenate([first, second], axis=0).astype(BF)
        return 0

    lax.fori_loop(0, HALF, build, 0)
    kron_ref[FACE:, :] = jnp.zeros((WIDE - FACE, NWIDE), BF)


def fill_kernel(old_ref, prev_ref, next_ref, pad_ref, flat_ref):
    boxes = pad_ref.shape[0] - 2
    for side, ref in ((0, prev_ref), (1, next_ref)):
        flat_ref[...] = ref[...].astype(F32)
        flat_to_slabs(
            lambda t: flat_ref[pl.ds(t, HALF, stride=PAIRT), :],
            lambda u, parity, x: pad_ref.__setitem__(
                (boxes + side, u, pl.ds(PAD + parity, HALF, stride=2), slice(None)), x),
        )


def pair_kernel(start, held, spins, tab_ref, kron_ref, diag_ref, inv_ref, *refs):
    pads, out_ref, sends = refs[:len(spins)], refs[len(spins)], refs[len(spins) + 1:-4]
    mov_ref, x_ref, y_ref, res_ref = refs[-4:]
    boxes = pads[0].shape[0] - 2
    pairs, _, _, leaves, order, _ = table_layout(boxes)
    lanes = lane_iota()
    rows = lax.broadcasted_iota(jnp.int32, (EDGE, 1), 0)

    def dense(index, _):
        box = tab_ref[order + start + index]
        places = []
        for number in range(PARTNERS):
            base = pairs + (box * PARTNERS + number) * 4
            source = tab_ref[base]
            da, db, dc = tab_ref[base + 1], tab_ref[base + 2], tab_ref[base + 3]
            offset = ZERO_TILES * LANES - (db * EDGE + dc)
            row_ok = jnp.abs(2 * (rows - da) - (EDGE - 1)) < EDGE
            places.append((source, da, db, dc, offset // LANES, offset % LANES, row_ok))
        last = [[None] * PARTNERS for _ in spins]
        for u in range(TILES + 1):
            keep = []
            for number in range(PARTNERS):
                source, da, db, dc, quotient, rest, row_ok = places[number]
                if u > 0:
                    cell = lanes + (u - 1) * LANES
                    b = (cell * 52429) >> 21
                    c = cell - b * EDGE
                    ok = (jnp.abs(2 * (b - db) - (EDGE - 1)) < EDGE) & (jnp.abs(2 * (c - dc) - (EDGE - 1)) < EDGE)
                    if u == TILES:
                        ok = ok & (lanes < FACE - (TILES - 1) * LANES)
                    keep.append(row_ok & ok)
            for at, pad_ref in enumerate(pads):
                values = []
                for number in range(PARTNERS):
                    source, da, db, dc, quotient, rest, row_ok = places[number]
                    tile = jnp.clip(quotient + (u - ZERO_TILES), 0, TILES - 1)
                    x = pad_ref[source, tile, pl.ds(PAD - da, EDGE), :]
                    turned = pltpu.roll(x, (LANES - rest) % LANES, 1)
                    if u > 0:
                        moved = jnp.where(keep[number], jnp.where(lanes < LANES - rest, last[at][number], turned), 0.0)
                        mov_ref[index, at, number, u - 1] = moved
                        values.append(pad_ref[box, u - 1, pl.ds(PAD, EDGE), :] * moved)
                    last[at][number] = turned
                if u > 0:
                    both = jnp.concatenate(values, axis=0)
                    if u == TILES:
                        both = jnp.where(lanes < FACE - (TILES - 1) * LANES, both, 0.0)
                    first = (index * len(spins) + at) * PARTNERS * EDGE
                    x_ref[pl.ds(pl.multiple_of(first, 16), PARTNERS * EDGE),
                          (u - 1) * LANES:u * LANES] = both.astype(BF)
        return 0

    lax.fori_loop(0, held, dense, 0)

    cubes = held * len(spins) * PARTNERS
    diag = diag_ref[...]
    for c in range(NSTEPS):
        cols = slice(c * NCHUNK, min((c + 1) * NCHUNK, WIDE))
        y_ref[:, cols] = jnp.dot(diag, x_ref[:, cols], preferred_element_type=F32).astype(BF)

    def forward(n, _):
        cols = pl.ds(pl.multiple_of(n * NCHUNK, NCHUNK), NCHUNK)
        z = jnp.dot(y_ref[:, :WIDE], kron_ref[:, cols], preferred_element_type=F32)
        z = z.reshape(cubes, EDGE, NCHUNK) * inv_ref[:, cols][None]
        x_ref[:, cols] = z.reshape(cubes * EDGE, NCHUNK).astype(BF)
        return 0

    lax.fori_loop(0, NSTEPS, forward, 0)

    def backward(n, _):
        cols = pl.ds(pl.multiple_of(n * NCHUNK, NCHUNK), NCHUNK)
        y_ref[:, cols] = jnp.dot(x_ref[:, :WIDE], kron_ref[:, cols], preferred_element_type=F32).astype(BF)
        return 0

    lax.fori_loop(0, NSTEPS, backward, 0)

    for u in range(TILES):
        potential = jnp.dot(diag, y_ref[:, u * LANES:(u + 1) * LANES], preferred_element_type=F32)
        for index in range(held):
            for at in range(len(spins)):
                total = 0.0
                for number in range(PARTNERS):
                    first = ((index * len(spins) + at) * PARTNERS + number) * EDGE
                    total = total + potential[first:first + EDGE] * mov_ref[index, at, number, u]
                res_ref[index * len(spins) + at, u] = total

    def flatten(row, _):
        slabs_to_flat(
            lambda u, parity: res_ref[row, u, pl.ds(parity, HALF, stride=2), :],
            lambda t, x: out_ref.__setitem__((row, pl.ds(t, HALF, stride=PAIRT), slice(None)), x),
        )
        return 0

    lax.fori_loop(0, held * len(spins), flatten, 0)
    if sends:
        for k in range(AHEAD):
            sends[0][k] = out_ref[tab_ref[leaves + k]].astype(BF)
        for k in range(BACK):
            sends[1][k] = out_ref[tab_ref[leaves + AHEAD + k]].astype(BF)


def keep_kernel(tab_ref, low_ref, high_ref, rest_ref, out_ref, form_ref, sems):
    first = low_ref.shape[0]
    boxes = first + rest_ref.shape[0] // 2
    codes = table_layout(boxes)[1]

    def copy(slot):
        return pltpu.make_async_copy(form_ref.at[slot], out_ref.at[slot], sems.at[slot])

    def arrives(slot):
        code = tab_ref[codes + slot]
        return (code >= boxes) & (code < boxes + AHEAD + BACK)

    def make(slot, _):
        code = tab_ref[codes + slot]

        @pl.when(code < first)
        def _():
            spot = jnp.minimum(code, first - 1)
            for spin, ref in enumerate((low_ref, high_ref)):
                form_ref[slot, pl.ds(spin, FLAT, stride=2), :] = ref[spot]

        @pl.when((code >= first) & (code < boxes))
        def _():
            spot = jnp.clip(code - first, 0, boxes - first - 1)
            for spin in range(2):
                form_ref[slot, pl.ds(spin, FLAT, stride=2), :] = rest_ref[2 * spot + spin]

        @pl.when(code >= boxes + AHEAD + BACK)
        def _():
            form_ref[slot] = jnp.zeros(form_ref.shape[1:], F32)

        @pl.when(jnp.logical_not(arrives(slot)))
        def _():
            copy(slot).start()

        return 0

    lax.fori_loop(0, CAP, make, 0)

    def finish(slot, _):
        @pl.when(jnp.logical_not(arrives(slot)))
        def _():
            copy(slot).wait()

        return 0

    lax.fori_loop(0, CAP, finish, 0)


def place_kernel(boxes, tab_ref, prev_low, next_low, prev_high, next_high, kept_ref, out_ref, form_ref, sems):
    slots = table_layout(boxes)[2]
    copies = []
    for k in range(AHEAD + BACK):
        pair, row = ((prev_low, prev_high), k) if k < AHEAD else ((next_low, next_high), k - AHEAD)
        slot = tab_ref[slots + k]
        copy = pltpu.make_async_copy(form_ref.at[k], out_ref.at[jnp.minimum(slot, CAP - 1)], sems.at[k])

        @pl.when(slot < CAP)
        def _():
            for spin, ref in enumerate(pair):
                form_ref[k, pl.ds(spin, FLAT, stride=2), :] = ref[row].astype(F32)
            copy.start()

        copies.append((slot, copy))
    for slot, copy in copies:
        @pl.when(slot < CAP)
        def _():
            copy.wait()


def from_behind(value, steps):
    count = lax.axis_size(AXES)
    return lax.ppermute(value, AXES, [(source, (source + steps) % count) for source in range(count)])


def whole(count):
    return [pl.BlockSpec(memory_space=pltpu.VMEM)] * count


SCALARS = pl.BlockSpec(memory_space=pltpu.SMEM)
ANYWHERE = pl.BlockSpec(memory_space=pltpu.MemorySpace.HBM)


def in_place(value):
    return pltpu.with_memory_space_constraint(jnp.asarray(value), pltpu.HBM)


def cost(flops, size):
    return pl.CostEstimate(flops=flops, bytes_accessed=size, transcendentals=0)


def shards(orbitals, dest, partners, anchors):
    boxes = orbitals.shape[1]
    sine, inverse, repeated, tiled = tables()
    partners_t, anchors_t = partners.T, anchors.T

    box = jax.ShapeDtypeStruct((FLAT, LANES), BF)
    splitter = pltpu.VMEM((FLAT * 8, LANES), F32)
    ahead_low, back_low, ahead_high, back_high, table = pl.pallas_call(
        window_kernel,
        out_shape=[box] * 4 + [jax.ShapeDtypeStruct((table_layout(boxes)[-1],), jnp.int32)],
        in_specs=[ANYWHERE] * 4,
        out_specs=whole(4) + [SCALARS],
        scratch_shapes=[pltpu.SMEM(dest.shape, jnp.int32), pltpu.SMEM(partners_t.shape, jnp.int32),
                        pltpu.SMEM(anchors_t.shape, jnp.int32), pltpu.VMEM(orbitals.shape, BF),
                        splitter, pltpu.SemaphoreType.DMA((5,))],
        compiler_params=pltpu.CompilerParams(vmem_limit_bytes=12 << 20),
        name="window",
    )(*map(in_place, (dest, partners_t, anchors_t, orbitals)))
    prev_low = from_behind(ahead_low, 1)
    next_low = from_behind(back_low, -1)
    prev_high = from_behind(ahead_high, 1)
    next_high = from_behind(back_high, -1)

    slabs = jax.ShapeDtypeStruct((boxes + 2, TILES, ROWS, LANES), F32)
    constants = np.stack([repeated, tiled])
    prepare = pl.pallas_call(
        prepare_kernel,
        out_shape=[slabs, slabs, jax.ShapeDtypeStruct((WIDE, NWIDE), BF)],
        in_specs=[ANYWHERE] * 2,
        out_specs=whole(3),
        scratch_shapes=[pltpu.VMEM(orbitals.shape, BF), pltpu.VMEM(constants.shape, F32), splitter,
                        pltpu.SemaphoreType.DMA((3,))],
        compiler_params=pltpu.CompilerParams(vmem_limit_bytes=20 << 20),
        cost_estimate=cost(10_000_000, 10_000_000),
        name="prepare",
    )
    *pads, kron = prepare(in_place(orbitals), in_place(constants))
    for spin, halo in enumerate(((prev_low, next_low), (prev_high, next_high))):
        pads[spin] = pl.pallas_call(
            fill_kernel,
            out_shape=slabs,
            in_specs=whole(3),
            out_specs=pl.BlockSpec(memory_space=pltpu.VMEM),
            scratch_shapes=[pltpu.VMEM((FLAT, LANES), F32)],
            input_output_aliases={0: 0},
            compiler_params=pltpu.CompilerParams(vmem_limit_bytes=12 << 20),
            cost_estimate=cost(1_000_000, 2_000_000),
        )(pads[spin], *halo)

    moving = AHEAD + BACK

    def solve(start, held, spins, send):
        cubes = held * len(spins) * PARTNERS
        diag = np.kron(np.eye(cubes, dtype=np.float32), sine).astype(jnp.bfloat16)
        shapes = [jax.ShapeDtypeStruct((held * len(spins), FLAT, LANES), F32)]
        if send:
            shapes += [jax.ShapeDtypeStruct((count, FLAT, LANES), BF) for count in (AHEAD, BACK)]
        return pl.pallas_call(
            lambda *refs: pair_kernel(start, held, spins, *refs),
            out_shape=shapes,
            in_specs=[SCALARS] + whole(3 + len(spins)),
            out_specs=whole(len(shapes)),
            scratch_shapes=[
                pltpu.VMEM((held, len(spins), PARTNERS, TILES, EDGE, LANES), F32),
                pltpu.VMEM((cubes * EDGE, NWIDE), BF),
                pltpu.VMEM((cubes * EDGE, NWIDE), BF),
                pltpu.VMEM((held * len(spins), TILES, EDGE, LANES), F32),
            ],
            compiler_params=pltpu.CompilerParams(vmem_limit_bytes=20 << 20),
            cost_estimate=cost(4 * cubes * EDGE * FACE * FACE, 10_000_000),
        )(table, kron, diag, inverse, *[pads[spin] for spin in spins])

    terms, arrived = [], []
    for spin in range(2):
        mine, sent_ahead, sent_back = solve(0, moving, (spin,), True)
        terms.append(mine)
        ahead = from_behind(sent_ahead, 1)
        back = from_behind(sent_back, -1)
        arrived += [ahead, back]
    terms += solve(moving, boxes - moving, (0, 1), False)

    shape = jax.ShapeDtypeStruct((CAP, 2 * FLAT, LANES), F32)
    kept = pl.pallas_call(
        keep_kernel,
        out_shape=shape,
        in_specs=[SCALARS] + whole(3),
        out_specs=ANYWHERE,
        scratch_shapes=[pltpu.VMEM((CAP, 2 * FLAT, LANES), F32), pltpu.SemaphoreType.DMA((CAP,))],
        compiler_params=pltpu.CompilerParams(vmem_limit_bytes=8 << 20),
        cost_estimate=cost(1_000_000, 8_000_000),
        name="keep",
    )(table, *terms)
    placed = pl.pallas_call(
        lambda *refs: place_kernel(boxes, *refs),
        out_shape=shape,
        in_specs=[SCALARS] + whole(4) + [ANYWHERE],
        out_specs=ANYWHERE,
        scratch_shapes=[pltpu.VMEM((AHEAD + BACK, 2 * FLAT, LANES), F32),
                        pltpu.SemaphoreType.DMA((AHEAD + BACK,))],
        input_output_aliases={5: 0},
        compiler_params=pltpu.CompilerParams(vmem_limit_bytes=8 << 20),
        cost_estimate=cost(1_000_000, 4_000_000),
        name="place",
    )(table, *arrived, kept)
    placed = placed.reshape(-1).reshape(CAP, FLAT, 2, LANES).transpose(0, 2, 1, 3)
    return placed.reshape(CAP, 2, FLAT * LANES).transpose(1, 0, 2)


def solution(mesh):
    return jax.shard_map(
        shards,
        mesh=mesh,
        in_specs=(P(None, AXES, None), P(), P(), P()),
        out_specs=P(None, AXES, None),
        check_vma=False,
    )
```

```python
import jax
import jax.numpy as jnp
import numpy as np
from jax import lax
from jax.experimental import pallas as pl
from jax.experimental.pallas import tpu as pltpu
from jax.sharding import PartitionSpec as P


EDGE = 40
PARTNERS = 2
GRID_X = 768
GRID_Y = 384
GRID_Z = 384
BACK = 2
AHEAD = 1
CAP = 7
SCREEN = 0.001

AXES = ("gx", "gy", "gz")
LANES = 128
FACE = EDGE * EDGE
TILES = -(-FACE // LANES)
WIDE = TILES * LANES
NCHUNK = 256
NSTEPS = -(-FACE // NCHUNK)
NWIDE = NSTEPS * NCHUNK
FLAT = EDGE ** 3 // LANES
HALF = EDGE // 2
PAIRT = 2 * FACE // LANES
PAD = 24
ROWS = EDGE + 2 * PAD
ZERO_TILES = 7
BF = jnp.bfloat16
F32 = jnp.float32


def tables():
    counter = np.arange(EDGE, dtype=np.float32) + 1.0
    angles = np.float32(np.pi) * counter[:, None] * counter[None, :] / np.float32(EDGE + 1.0)
    sine = (np.sqrt(np.float32(2.0 / (EDGE + 1.0))) * np.sin(angles)).astype(jnp.bfloat16)
    sine = sine.astype(np.float32)
    levels = 2.0 - 2.0 * np.cos(np.pi * counter.astype(np.float64) / (EDGE + 1.0))
    lam = levels[:, None, None] + levels[None, :, None] + levels[None, None, :] + SCREEN
    inverse = np.zeros((EDGE, NWIDE), np.float32)
    inverse[:, :FACE] = (1.0 / lam).reshape(EDGE, FACE)
    repeated = np.zeros((EDGE, NWIDE), np.float32)
    repeated[:, :FACE] = np.repeat(sine, EDGE, axis=1)
    tiled = np.zeros((EDGE, NWIDE), np.float32)
    tiled[:, :FACE] = np.tile(sine, (1, EDGE))
    return sine, inverse, repeated, tiled


def lane_iota():
    return lax.broadcasted_iota(jnp.int32, (1, LANES), 1)


def split_boxes(orb_ref, flat_ref, boxes):
    def step(i, _):
        base = pl.multiple_of(i * PAIRT * LANES, LANES)
        x = orb_ref[:, pl.ds(base, PAIRT * LANES)].astype(F32)
        for j in range(PAIRT):
            flat_ref[pl.ds(pl.multiple_of((i * PAIRT + j) * 8, 8), boxes), :] = x[:, j * LANES:(j + 1) * LANES]
        return 0

    lax.fori_loop(0, HALF, step, 0)


def flat_to_slabs(load, store):
    low = lane_iota() < LANES // 2
    rolled = None
    for t in range(PAIRT):
        x = load(t)
        if t < TILES:
            store(t, 0, x)
        if t >= TILES - 1:
            turned = pltpu.roll(x, LANES // 2, 1)
            if rolled is not None:
                store(t - TILES, 1, jnp.where(low, rolled, turned))
            rolled = turned
    store(TILES - 1, 1, rolled)


def slabs_to_flat(load, store):
    low = lane_iota() < LANES // 2
    for t in range(TILES - 1):
        store(t, load(t, 0))
    before = load(TILES - 1, 0)
    for v in range(TILES):
        turned = pltpu.roll(load(v, 1), LANES // 2, 1)
        store(TILES - 1 + v, jnp.where(low, before, turned))
        before = turned


def wanted_boxes(part_ref, boxes):
    total = part_ref.shape[1]
    device = lax.axis_index(AXES)
    wanted = []
    for step in (1, -1):
        found = jnp.int32(0)
        for k in range(boxes):
            other = (device + step) * boxes + k
            inside = (other >= 0) & (other < total)
            for number in range(PARTNERS):
                local = part_ref[number, jnp.clip(other, 0, total - 1)] - device * boxes
                found = jnp.where(inside & (local >= 0) & (local < boxes), local, found)
        wanted.append(found)
    return wanted


def window_kernel(dest_hbm, part_hbm, anc_hbm, orb_hbm, ahead_low, back_low, ahead_high, back_high, tab_ref,
                  dest_ref, part_ref, anc_ref, orb_ref, flat_ref, sems):
    boxes = orb_ref.shape[1]
    small = [pltpu.make_async_copy(source, target, sems.at[k]) for k, (source, target) in enumerate(
        ((part_hbm, part_ref), (dest_hbm, dest_ref), (anc_hbm, anc_ref)))]
    large = [pltpu.make_async_copy(orb_hbm.at[spin], orb_ref.at[spin], sems.at[3 + spin]) for spin in range(2)]
    for copy in (small[0], large[0], small[1], small[2], large[1]):
        copy.start()
    for copy in small:
        copy.wait()
    wanted = wanted_boxes(part_ref, boxes)
    build_tables(dest_ref, part_ref, anc_ref, tab_ref, boxes)
    for spin, refs in enumerate(((ahead_low, back_low), (ahead_high, back_high))):
        large[spin].wait()
        split_boxes(orb_ref.at[spin], flat_ref, boxes)
        for side, ref in enumerate(refs):
            ref[...] = flat_ref[pl.ds(wanted[side], FLAT, stride=8), :].astype(BF)


def table_layout(boxes):
    pairs = 0
    codes = pairs + boxes * PARTNERS * 4
    slots = codes + CAP + 1
    leaves = slots + AHEAD + BACK + 1
    order = leaves + AHEAD + BACK + 1
    homes = order + boxes
    return pairs, codes, slots, leaves, order, homes, homes + boxes + 1


def build_tables(dest_ref, part_ref, anc_ref, tab_ref, boxes):
    total = part_ref.shape[1]
    device = lax.axis_index(AXES)
    pairs, codes, slots, leaves, order, homes, _ = table_layout(boxes)
    one, none = jnp.int32(1), jnp.int32(0)
    for k in range(CAP + 1):
        tab_ref[codes + k] = boxes + AHEAD + BACK
    for k in range(boxes + 1):
        tab_ref[homes + k] = 0
    for k in range(AHEAD + BACK + 1):
        tab_ref[slots + k] = CAP
        tab_ref[leaves + k] = 0
    goes = [dest_ref[device * boxes + k] for k in range(boxes)]
    ahead_all, back_all = none, none
    for k in range(boxes):
        ahead_all = ahead_all + jnp.where(goes[k] == device + 1, one, none)
        back_all = back_all + jnp.where(goes[k] == device - 1, one, none)
    ahead, back, stay = none, none, none
    spots = []
    for k in range(boxes):
        is_ahead, is_back = goes[k] == device + 1, goes[k] == device - 1
        spot = jnp.where(is_ahead, ahead, jnp.where(is_back, ahead_all + back, ahead_all + back_all + stay))
        spots.append(spot)
        tab_ref[order + spot] = k
        spare = leaves + AHEAD + BACK
        tab_ref[jnp.where(is_ahead, leaves + jnp.minimum(ahead, AHEAD - 1), spare)] = spot
        tab_ref[jnp.where(is_back, leaves + AHEAD + jnp.minimum(back, BACK - 1), spare)] = spot
        ahead = ahead + jnp.where(is_ahead, one, none)
        back = back + jnp.where(is_back, one, none)
        stay = stay + jnp.where(is_ahead | is_back, none, one)
    count = none
    for block in range(3):
        arrived = none
        for k in range(boxes):
            box = (device + (block - 1)) * boxes + k
            hit = (box >= 0) & (box < total) & (dest_ref[jnp.clip(box, 0, total - 1)] == device)
            if block == 1:
                code = spots[k]
                tab_ref[jnp.where(hit, homes + code, homes + boxes)] = jnp.minimum(count, CAP - 1)
            else:
                first, most = (0, AHEAD) if block == 0 else (AHEAD, BACK)
                where = first + jnp.minimum(arrived, most - 1)
                code = boxes + where
                tab_ref[jnp.where(hit, slots + where, slots + AHEAD + BACK)] = count
                arrived = arrived + jnp.where(hit, one, none)
            tab_ref[jnp.where(hit, codes + jnp.minimum(count, CAP - 1), codes + CAP)] = code
            count = count + jnp.where(hit, one, none)
    for box in range(boxes):
        me = device * boxes + box
        for number in range(PARTNERS):
            other = part_ref[number, me]
            local = other - device * boxes
            base = pairs + (box * PARTNERS + number) * 4
            tab_ref[base] = jnp.where(local < 0, boxes, jnp.where(local >= boxes, boxes + 1, local))
            for axis, extent in enumerate((GRID_X, GRID_Y, GRID_Z)):
                moved = anc_ref[axis, other] - anc_ref[axis, me] + extent // 2
                moved = jnp.where(moved < 0, moved + extent, jnp.where(moved >= extent, moved - extent, moved))
                tab_ref[base + 1 + axis] = jnp.clip(moved - extent // 2, -(PAD - 4), PAD - 4)


def prepare_kernel(orb_hbm, rep_hbm, inv_hbm, diag_hbm, rest_hbm, low_ref, high_ref, kron_ref, inv_ref, diag_ref, rest_ref,
                   orb_ref, rep_ref, flat_ref, sems):
    boxes = orb_ref.shape[1]
    copies = [pltpu.make_async_copy(orb_hbm.at[spin], orb_ref.at[spin], sems.at[spin]) for spin in range(2)]
    copies += [pltpu.make_async_copy(source, target, sems.at[2 + k]) for k, (source, target) in enumerate(
        ((rep_hbm, rep_ref), (inv_hbm, inv_ref), (diag_hbm, diag_ref), (rest_hbm, rest_ref)))]
    for copy in copies:
        copy.start()
    for spin, pad_ref in enumerate((low_ref, high_ref)):
        copies[spin].wait()
        split_boxes(orb_ref.at[spin], flat_ref, boxes)

        def slabs(box, _):
            flat_to_slabs(
                lambda t: flat_ref[pl.ds(box + 8 * t, HALF, stride=8 * PAIRT), :],
                lambda u, parity, x: pad_ref.__setitem__(
                    (box, u, pl.ds(PAD + parity, HALF, stride=2), slice(None)), x),
            )
            return 0

        lax.fori_loop(0, boxes, slabs, 0)

    copies[2].wait()

    def build(i, _):
        row = pl.multiple_of(i * 2 * EDGE, 16)
        for c in range(NSTEPS):
            cols = slice(c * NCHUNK, (c + 1) * NCHUNK)
            til = rep_ref[1, :, cols]
            first = rep_ref[0, pl.ds(2 * i, 1), cols] * til
            second = rep_ref[0, pl.ds(2 * i + 1, 1), cols] * til
            kron_ref[pl.ds(row, 2 * EDGE), cols] = jnp.concatenate([first, second], axis=0).astype(BF)
        return 0

    lax.fori_loop(0, HALF, build, 0)
    kron_ref[FACE:, :] = jnp.zeros((WIDE - FACE, NWIDE), BF)
    for copy in copies[3:]:
        copy.wait()


def fill_kernel(old_ref, prev_ref, next_ref, pad_ref, flat_ref):
    boxes = pad_ref.shape[0] - 2
    for side, ref in ((0, prev_ref), (1, next_ref)):
        flat_ref[...] = ref[...].astype(F32)
        flat_to_slabs(
            lambda t: flat_ref[pl.ds(t, HALF, stride=PAIRT), :],
            lambda u, parity, x: pad_ref.__setitem__(
                (boxes + side, u, pl.ds(PAD + parity, HALF, stride=2), slice(None)), x),
        )


def pair_kernel(start, held, spins, final, tab_ref, kron_ref, diag_ref, inv_ref, *refs):
    pads, (mov_ref, x_ref, y_ref, res_ref) = refs[:len(spins)], refs[-4:]
    boxes = pads[0].shape[0] - 2
    pairs, codes, _, leaves, order, homes, _ = table_layout(boxes)
    if final:
        low_ref, high_ref, out_ref, form_ref, sems = refs[len(spins):-4]

        def copy(slot):
            return pltpu.make_async_copy(form_ref.at[slot], out_ref.at[slot], sems.at[slot])

        def early(slot, _):
            code = tab_ref[codes + slot]

            @pl.when(code < start)
            def _():
                spot = jnp.minimum(code, start - 1)
                for spin, ref in enumerate((low_ref, high_ref)):
                    form_ref[slot, pl.ds(spin, FLAT, stride=2), :] = ref[spot]
                copy(slot).start()

            @pl.when(code >= boxes + AHEAD + BACK)
            def _():
                form_ref[slot] = jnp.zeros(form_ref.shape[1:], F32)
                copy(slot).start()

            return 0

        lax.fori_loop(0, CAP, early, 0)
    else:
        out_ref, sends = refs[len(spins)], refs[len(spins) + 1:-4]
    lanes = lane_iota()
    rows = lax.broadcasted_iota(jnp.int32, (EDGE, 1), 0)

    def dense(index, _):
        box = tab_ref[order + start + index]
        places = []
        for number in range(PARTNERS):
            base = pairs + (box * PARTNERS + number) * 4
            source = tab_ref[base]
            da, db, dc = tab_ref[base + 1], tab_ref[base + 2], tab_ref[base + 3]
            offset = ZERO_TILES * LANES - (db * EDGE + dc)
            row_ok = jnp.abs(2 * (rows - da) - (EDGE - 1)) < EDGE
            places.append((source, da, db, dc, offset // LANES, offset % LANES, row_ok))
        last = [[None] * PARTNERS for _ in spins]
        for u in range(TILES + 1):
            keep = []
            for number in range(PARTNERS):
                source, da, db, dc, quotient, rest, row_ok = places[number]
                if u > 0:
                    cell = lanes + (u - 1) * LANES
                    b = (cell * 52429) >> 21
                    c = cell - b * EDGE
                    ok = (jnp.abs(2 * (b - db) - (EDGE - 1)) < EDGE) & (jnp.abs(2 * (c - dc) - (EDGE - 1)) < EDGE)
                    if u == TILES:
                        ok = ok & (lanes < FACE - (TILES - 1) * LANES)
                    keep.append(row_ok & ok)
            for at, pad_ref in enumerate(pads):
                values = []
                for number in range(PARTNERS):
                    source, da, db, dc, quotient, rest, row_ok = places[number]
                    tile = jnp.clip(quotient + (u - ZERO_TILES), 0, TILES - 1)
                    x = pad_ref[source, tile, pl.ds(PAD - da, EDGE), :]
                    turned = pltpu.roll(x, (LANES - rest) % LANES, 1)
                    if u > 0:
                        moved = jnp.where(keep[number], jnp.where(lanes < LANES - rest, last[at][number], turned), 0.0)
                        mov_ref[index, at, number, u - 1] = moved
                        values.append(pad_ref[box, u - 1, pl.ds(PAD, EDGE), :] * moved)
                    last[at][number] = turned
                if u > 0:
                    both = jnp.concatenate(values, axis=0)
                    if u == TILES:
                        both = jnp.where(lanes < FACE - (TILES - 1) * LANES, both, 0.0)
                    first = (index * len(spins) + at) * PARTNERS * EDGE
                    x_ref[pl.ds(pl.multiple_of(first, 16), PARTNERS * EDGE),
                          (u - 1) * LANES:u * LANES] = both.astype(BF)
        return 0

    lax.fori_loop(0, held, dense, 0)

    cubes = held * len(spins) * PARTNERS
    diag = diag_ref[...]
    for c in range(NSTEPS):
        cols = slice(c * NCHUNK, min((c + 1) * NCHUNK, WIDE))
        y_ref[:, cols] = jnp.dot(diag, x_ref[:, cols], preferred_element_type=F32).astype(BF)

    def forward(n, _):
        cols = pl.ds(pl.multiple_of(n * NCHUNK, NCHUNK), NCHUNK)
        z = jnp.dot(y_ref[:, :WIDE], kron_ref[:, cols], preferred_element_type=F32)
        z = z.reshape(cubes, EDGE, NCHUNK) * inv_ref[:, cols][None]
        x_ref[:, cols] = z.reshape(cubes * EDGE, NCHUNK).astype(BF)
        return 0

    lax.fori_loop(0, NSTEPS, forward, 0)

    def backward(n, _):
        cols = pl.ds(pl.multiple_of(n * NCHUNK, NCHUNK), NCHUNK)
        y_ref[:, cols] = jnp.dot(x_ref[:, :WIDE], kron_ref[:, cols], preferred_element_type=F32).astype(BF)
        return 0

    lax.fori_loop(0, NSTEPS, backward, 0)

    for u in range(TILES):
        potential = jnp.dot(diag, y_ref[:, u * LANES:(u + 1) * LANES], preferred_element_type=F32)
        for index in range(held):
            for at in range(len(spins)):
                total = 0.0
                for number in range(PARTNERS):
                    first = ((index * len(spins) + at) * PARTNERS + number) * EDGE
                    total = total + potential[first:first + EDGE] * mov_ref[index, at, number, u]
                res_ref[index * len(spins) + at, u] = total

    if final:
        for index in range(held):
            home = tab_ref[homes + start + index]
            for at in range(len(spins)):
                slabs_to_flat(
                    lambda u, parity: res_ref[index * len(spins) + at, u, pl.ds(parity, HALF, stride=2), :],
                    lambda t, x: form_ref.__setitem__(
                        (home, pl.ds(2 * t + at, HALF, stride=2 * PAIRT), slice(None)), x),
                )
            copy(home).start()

        def finish(slot, _):
            code = tab_ref[codes + slot]

            @pl.when((code < boxes) | (code >= boxes + AHEAD + BACK))
            def _():
                copy(slot).wait()

            return 0

        lax.fori_loop(0, CAP, finish, 0)
        return

    def flatten(row, _):
        slabs_to_flat(
            lambda u, parity: res_ref[row, u, pl.ds(parity, HALF, stride=2), :],
            lambda t, x: out_ref.__setitem__((row, pl.ds(t, HALF, stride=PAIRT), slice(None)), x),
        )
        return 0

    lax.fori_loop(0, held * len(spins), flatten, 0)
    for k in range(AHEAD):
        sends[0][k] = out_ref[tab_ref[leaves + k]].astype(BF)
    for k in range(BACK):
        sends[1][k] = out_ref[tab_ref[leaves + AHEAD + k]].astype(BF)


def place_kernel(boxes, tab_ref, prev_low, next_low, prev_high, next_high, kept_ref, out_ref, form_ref, sems):
    slots = table_layout(boxes)[2]
    copies = []
    for k in range(AHEAD + BACK):
        pair, row = ((prev_low, prev_high), k) if k < AHEAD else ((next_low, next_high), k - AHEAD)
        slot = tab_ref[slots + k]
        copy = pltpu.make_async_copy(form_ref.at[k], out_ref.at[jnp.minimum(slot, CAP - 1)], sems.at[k])

        @pl.when(slot < CAP)
        def _():
            for spin, ref in enumerate(pair):
                form_ref[k, pl.ds(spin, FLAT, stride=2), :] = ref[row].astype(F32)
            copy.start()

        copies.append((slot, copy))
    for slot, copy in copies:
        @pl.when(slot < CAP)
        def _():
            copy.wait()


def from_behind(value, steps):
    count = lax.axis_size(AXES)
    return lax.ppermute(value, AXES, [(source, (source + steps) % count) for source in range(count)])


def whole(count):
    return [pl.BlockSpec(memory_space=pltpu.VMEM)] * count


SCALARS = pl.BlockSpec(memory_space=pltpu.SMEM)
ANYWHERE = pl.BlockSpec(memory_space=pltpu.MemorySpace.HBM)


def in_place(value):
    return pltpu.with_memory_space_constraint(jnp.asarray(value), pltpu.HBM)


def cost(flops, size):
    return pl.CostEstimate(flops=flops, bytes_accessed=size, transcendentals=0)


def shards(orbitals, dest, partners, anchors):
    boxes = orbitals.shape[1]
    sine, inverse, repeated, tiled = tables()
    partners_t, anchors_t = partners.T, anchors.T

    box = jax.ShapeDtypeStruct((FLAT, LANES), BF)
    splitter = pltpu.VMEM((FLAT * 8, LANES), F32)
    ahead_low, back_low, ahead_high, back_high, table = pl.pallas_call(
        window_kernel,
        out_shape=[box] * 4 + [jax.ShapeDtypeStruct((table_layout(boxes)[-1],), jnp.int32)],
        in_specs=[ANYWHERE] * 4,
        out_specs=whole(4) + [SCALARS],
        scratch_shapes=[pltpu.SMEM(dest.shape, jnp.int32), pltpu.SMEM(partners_t.shape, jnp.int32),
                        pltpu.SMEM(anchors_t.shape, jnp.int32), pltpu.VMEM(orbitals.shape, BF),
                        splitter, pltpu.SemaphoreType.DMA((5,))],
        compiler_params=pltpu.CompilerParams(vmem_limit_bytes=12 << 20),
        name="window",
    )(*map(in_place, (dest, partners_t, anchors_t, orbitals)))
    prev_low = from_behind(ahead_low, 1)
    next_low = from_behind(back_low, -1)
    prev_high = from_behind(ahead_high, 1)
    next_high = from_behind(back_high, -1)

    moving = AHEAD + BACK
    slabs = jax.ShapeDtypeStruct((boxes + 2, TILES, ROWS, LANES), F32)
    constants = np.stack([repeated, tiled])
    diags = [np.kron(np.eye(cubes, dtype=np.float32), sine).astype(jnp.bfloat16)
             for cubes in (moving * PARTNERS, (boxes - moving) * 2 * PARTNERS)]
    handed = (inverse, *diags)
    prepare = pl.pallas_call(
        prepare_kernel,
        out_shape=[slabs, slabs, jax.ShapeDtypeStruct((WIDE, NWIDE), BF)]
        + [jax.ShapeDtypeStruct(value.shape, value.dtype) for value in handed],
        in_specs=[ANYWHERE] * 5,
        out_specs=whole(6),
        scratch_shapes=[pltpu.VMEM(orbitals.shape, BF), pltpu.VMEM(constants.shape, F32), splitter,
                        pltpu.SemaphoreType.DMA((6,))],
        compiler_params=pltpu.CompilerParams(vmem_limit_bytes=20 << 20),
        cost_estimate=cost(10_000_000, 10_000_000),
        name="prepare",
    )
    low, high, kron, inverse, *diags = prepare(*map(in_place, (orbitals, constants, *handed)))
    pads = [low, high]
    for spin, halo in enumerate(((prev_low, next_low), (prev_high, next_high))):
        pads[spin] = pl.pallas_call(
            fill_kernel,
            out_shape=slabs,
            in_specs=whole(3),
            out_specs=pl.BlockSpec(memory_space=pltpu.VMEM),
            scratch_shapes=[pltpu.VMEM((FLAT, LANES), F32)],
            input_output_aliases={0: 0},
            compiler_params=pltpu.CompilerParams(vmem_limit_bytes=12 << 20),
            cost_estimate=cost(1_000_000, 2_000_000),
        )(pads[spin], *halo)

    shape = jax.ShapeDtypeStruct((CAP, 2 * FLAT, LANES), F32)

    def solve(start, held, spins, terms=None):
        cubes = held * len(spins) * PARTNERS
        final = terms is not None
        if final:
            shapes, specs = [shape], [ANYWHERE]
            extra = [pltpu.VMEM(shape.shape, F32), pltpu.SemaphoreType.DMA((CAP,))]
        else:
            shapes = [jax.ShapeDtypeStruct((held * len(spins), FLAT, LANES), F32)]
            shapes += [jax.ShapeDtypeStruct((count, FLAT, LANES), BF) for count in (AHEAD, BACK)]
            specs, extra = whole(3), []
        operands = [table, kron, diags[final], inverse] + [pads[spin] for spin in spins] + (terms or [])
        return pl.pallas_call(
            lambda *refs: pair_kernel(start, held, spins, final, *refs),
            out_shape=shapes,
            in_specs=[SCALARS] + whole(len(operands) - 1),
            out_specs=specs,
            scratch_shapes=extra + [
                pltpu.VMEM((held, len(spins), PARTNERS, TILES, EDGE, LANES), F32),
                pltpu.VMEM((cubes * EDGE, NWIDE), BF),
                pltpu.VMEM((cubes * EDGE, NWIDE), BF),
                pltpu.VMEM((held * len(spins), TILES, EDGE, LANES), F32),
            ],
            compiler_params=pltpu.CompilerParams(vmem_limit_bytes=20 << 20),
            cost_estimate=cost(4 * cubes * EDGE * FACE * FACE, 10_000_000),
        )(*operands)

    terms, arrived = [], []
    for spin in range(2):
        mine, sent_ahead, sent_back = solve(0, moving, (spin,))
        terms.append(mine)
        ahead = from_behind(sent_ahead, 1)
        back = from_behind(sent_back, -1)
        arrived += [ahead, back]
    kept, = solve(moving, boxes - moving, (0, 1), terms)
    placed = pl.pallas_call(
        lambda *refs: place_kernel(boxes, *refs),
        out_shape=shape,
        in_specs=[SCALARS] + whole(4) + [ANYWHERE],
        out_specs=ANYWHERE,
        scratch_shapes=[pltpu.VMEM((AHEAD + BACK, 2 * FLAT, LANES), F32),
                        pltpu.SemaphoreType.DMA((AHEAD + BACK,))],
        input_output_aliases={5: 0},
        compiler_params=pltpu.CompilerParams(vmem_limit_bytes=8 << 20),
        cost_estimate=cost(1_000_000, 4_000_000),
        name="place",
    )(table, *arrived, kept)
    placed = placed.reshape(-1).reshape(CAP, FLAT, 2, LANES).transpose(0, 2, 1, 3)
    return placed.reshape(CAP, 2, FLAT * LANES).transpose(1, 0, 2)


def solution(mesh):
    return jax.shard_map(
        shards,
        mesh=mesh,
        in_specs=(P(None, AXES, None), P(), P(), P()),
        out_specs=P(None, AXES, None),
        check_vma=False,
    )
```

```python
import jax
import jax.numpy as jnp
import numpy as np
from jax import lax
from jax.experimental import pallas as pl
from jax.experimental.pallas import tpu as pltpu
from jax.sharding import PartitionSpec as P


EDGE = 40
PARTNERS = 2
GRID_X = 768
GRID_Y = 384
GRID_Z = 384
BACK = 2
AHEAD = 1
CAP = 7
SCREEN = 0.001

AXES = ("gx", "gy", "gz")
LANES = 128
FACE = EDGE * EDGE
TILES = -(-FACE // LANES)
NCHUNK = 256
FOLD = FACE // 2
FTILES = -(-FOLD // LANES)
FWIDE = FTILES * LANES
CHUNKS = [(min(first, FWIDE - NCHUNK), NCHUNK) for first in range(0, FWIDE, NCHUNK)]
FLAT = EDGE ** 3 // LANES
HALF = EDGE // 2
PAIRT = 2 * FACE // LANES
PAD = 24
ROWS = EDGE + 2 * PAD
ZERO_TILES = 7
BF = jnp.bfloat16
F32 = jnp.float32


def tables():
    counter = np.arange(EDGE, dtype=np.float32) + 1.0
    angles = np.float32(np.pi) * counter[:, None] * counter[None, :] / np.float32(EDGE + 1.0)
    sine = (np.sqrt(np.float32(2.0 / (EDGE + 1.0))) * np.sin(angles)).astype(jnp.bfloat16)
    sine = sine.astype(np.float32)
    levels = 2.0 - 2.0 * np.cos(np.pi * counter.astype(np.float64) / (EDGE + 1.0))
    number = np.arange(FOLD)
    second, step = number // HALF, number % HALF
    thirds = [2 * step + second % 2, 2 * step + 1 - second % 2]
    inverse = np.zeros((EDGE, 2 * FWIDE), np.float32)
    for part, third in enumerate(thirds):
        lam = levels[:, None] + levels[second] + levels[third] + SCREEN
        inverse[:, part * FWIDE:part * FWIDE + FOLD] = 1.0 / lam
    factors = np.zeros((6, EDGE, FWIDE), np.float32)
    factors[0, :HALF, :FOLD] = sine[:HALF][:, second]
    for part, third in enumerate(thirds):
        factors[1 + part, :, :FOLD] = sine[:, third]
    factors[3, :, :FOLD] = np.repeat(sine[:HALF], EDGE, axis=0).T
    lines = np.tile(sine, (HALF, 1)).T
    factors[4, :, :FOLD] = np.concatenate([lines[0::2], lines[1::2]])
    factors[5, :, :FOLD] = np.concatenate([lines[1::2], lines[0::2]])
    return sine, inverse, factors


def lane_iota():
    return lax.broadcasted_iota(jnp.int32, (1, LANES), 1)


def split_boxes(orb_ref, flat_ref, boxes):
    def step(i, _):
        base = pl.multiple_of(i * PAIRT * LANES, LANES)
        x = orb_ref[:, pl.ds(base, PAIRT * LANES)].astype(F32)
        for j in range(PAIRT):
            flat_ref[pl.ds(pl.multiple_of((i * PAIRT + j) * 8, 8), boxes), :] = x[:, j * LANES:(j + 1) * LANES]
        return 0

    lax.fori_loop(0, HALF, step, 0)


def flat_to_slabs(load, store):
    low = lane_iota() < LANES // 2
    rolled = None
    for t in range(PAIRT):
        x = load(t)
        if t < TILES:
            store(t, 0, x)
        if t >= TILES - 1:
            turned = pltpu.roll(x, LANES // 2, 1)
            if rolled is not None:
                store(t - TILES, 1, jnp.where(low, rolled, turned))
            rolled = turned
    store(TILES - 1, 1, rolled)


def turn(x):
    source = (LANES // 2 - 1 - lax.broadcasted_iota(jnp.int32, x.shape, 1)) & (LANES - 1)
    return jnp.take_along_axis(x, source, axis=1)


def reverse_slabs(load, store, first, count):
    low = lane_iota() < LANES // 2
    turned = [turn(load(v)) for v in range(count)]
    for u in range(first, TILES):
        v = TILES - 1 - u
        store(u, jnp.where(low, turned[v], turned[v - 1]) if v > 0 else turned[v])


def slabs_to_flat(load, store):
    low = lane_iota() < LANES // 2
    for t in range(TILES - 1):
        store(t, load(t, 0))
    before = load(TILES - 1, 0)
    for v in range(TILES):
        turned = pltpu.roll(load(v, 1), LANES // 2, 1)
        store(TILES - 1 + v, jnp.where(low, before, turned))
        before = turned


def wanted_boxes(part_ref, boxes):
    total = part_ref.shape[1]
    device = lax.axis_index(AXES)
    wanted = []
    for step in (1, -1):
        found = jnp.int32(0)
        for k in range(boxes):
            other = (device + step) * boxes + k
            inside = (other >= 0) & (other < total)
            for number in range(PARTNERS):
                local = part_ref[number, jnp.clip(other, 0, total - 1)] - device * boxes
                found = jnp.where(inside & (local >= 0) & (local < boxes), local, found)
        wanted.append(found)
    return wanted


def window_kernel(dest_hbm, part_hbm, anc_hbm, orb_hbm, ahead_low, back_low, ahead_high, back_high, tab_ref,
                  dest_ref, part_ref, anc_ref, orb_ref, flat_ref, sems):
    boxes = orb_ref.shape[1]
    small = [pltpu.make_async_copy(source, target, sems.at[k]) for k, (source, target) in enumerate(
        ((part_hbm, part_ref), (dest_hbm, dest_ref), (anc_hbm, anc_ref)))]
    large = [pltpu.make_async_copy(orb_hbm.at[spin], orb_ref.at[spin], sems.at[3 + spin]) for spin in range(2)]
    for copy in (small[0], large[0], small[1], small[2], large[1]):
        copy.start()
    for copy in small:
        copy.wait()
    wanted = wanted_boxes(part_ref, boxes)
    build_tables(dest_ref, part_ref, anc_ref, tab_ref, boxes)
    for spin, refs in enumerate(((ahead_low, back_low), (ahead_high, back_high))):
        large[spin].wait()
        split_boxes(orb_ref.at[spin], flat_ref, boxes)
        for side, ref in enumerate(refs):
            ref[...] = flat_ref[pl.ds(wanted[side], FLAT, stride=8), :].astype(BF)


def table_layout(boxes):
    pairs = 0
    codes = pairs + boxes * PARTNERS * 4
    slots = codes + CAP + 1
    leaves = slots + AHEAD + BACK + 1
    order = leaves + AHEAD + BACK + 1
    homes = order + boxes
    return pairs, codes, slots, leaves, order, homes, homes + boxes + 1


def build_tables(dest_ref, part_ref, anc_ref, tab_ref, boxes):
    total = part_ref.shape[1]
    device = lax.axis_index(AXES)
    pairs, codes, slots, leaves, order, homes, _ = table_layout(boxes)
    one, none = jnp.int32(1), jnp.int32(0)
    for k in range(CAP + 1):
        tab_ref[codes + k] = boxes + AHEAD + BACK
    for k in range(boxes + 1):
        tab_ref[homes + k] = 0
    for k in range(AHEAD + BACK + 1):
        tab_ref[slots + k] = CAP
        tab_ref[leaves + k] = 0
    goes = [dest_ref[device * boxes + k] for k in range(boxes)]
    ahead_all, back_all = none, none
    for k in range(boxes):
        ahead_all = ahead_all + jnp.where(goes[k] == device + 1, one, none)
        back_all = back_all + jnp.where(goes[k] == device - 1, one, none)
    ahead, back, stay = none, none, none
    spots = []
    for k in range(boxes):
        is_ahead, is_back = goes[k] == device + 1, goes[k] == device - 1
        spot = jnp.where(is_ahead, ahead, jnp.where(is_back, ahead_all + back, ahead_all + back_all + stay))
        spots.append(spot)
        tab_ref[order + spot] = k
        spare = leaves + AHEAD + BACK
        tab_ref[jnp.where(is_ahead, leaves + jnp.minimum(ahead, AHEAD - 1), spare)] = spot
        tab_ref[jnp.where(is_back, leaves + AHEAD + jnp.minimum(back, BACK - 1), spare)] = spot
        ahead = ahead + jnp.where(is_ahead, one, none)
        back = back + jnp.where(is_back, one, none)
        stay = stay + jnp.where(is_ahead | is_back, none, one)
    count = none
    for block in range(3):
        arrived = none
        for k in range(boxes):
            box = (device + (block - 1)) * boxes + k
            hit = (box >= 0) & (box < total) & (dest_ref[jnp.clip(box, 0, total - 1)] == device)
            if block == 1:
                code = spots[k]
                tab_ref[jnp.where(hit, homes + code, homes + boxes)] = jnp.minimum(count, CAP - 1)
            else:
                first, most = (0, AHEAD) if block == 0 else (AHEAD, BACK)
                where = first + jnp.minimum(arrived, most - 1)
                code = boxes + where
                tab_ref[jnp.where(hit, slots + where, slots + AHEAD + BACK)] = count
                arrived = arrived + jnp.where(hit, one, none)
            tab_ref[jnp.where(hit, codes + jnp.minimum(count, CAP - 1), codes + CAP)] = code
            count = count + jnp.where(hit, one, none)
    for box in range(boxes):
        me = device * boxes + box
        for number in range(PARTNERS):
            other = part_ref[number, me]
            local = other - device * boxes
            base = pairs + (box * PARTNERS + number) * 4
            tab_ref[base] = jnp.where(local < 0, boxes, jnp.where(local >= boxes, boxes + 1, local))
            for axis, extent in enumerate((GRID_X, GRID_Y, GRID_Z)):
                moved = anc_ref[axis, other] - anc_ref[axis, me] + extent // 2
                moved = jnp.where(moved < 0, moved + extent, jnp.where(moved >= extent, moved - extent, moved))
                tab_ref[base + 1 + axis] = jnp.clip(moved - extent // 2, -(PAD - 4), PAD - 4)


def reverse_box(pad_ref, box):
    body = pl.ds(PAD, EDGE)
    reverse_slabs(lambda v: pad_ref[0, box, v, body, :],
                  lambda u, x: pad_ref.__setitem__((1, box, u, body, slice(None)), x), 0, TILES)


def prepare_kernel(orb_hbm, fac_hbm, inv_hbm, diag_hbm, rest_hbm, low_ref, high_ref, to_ref, from_ref, inv_ref, diag_ref,
                   rest_ref, orb_ref, fac_ref, flat_ref, sems):
    boxes = orb_ref.shape[1]
    copies = [pltpu.make_async_copy(orb_hbm.at[spin], orb_ref.at[spin], sems.at[spin]) for spin in range(2)]
    copies += [pltpu.make_async_copy(source, target, sems.at[2 + k]) for k, (source, target) in enumerate(
        ((fac_hbm, fac_ref), (inv_hbm, inv_ref), (diag_hbm, diag_ref), (rest_hbm, rest_ref)))]
    for copy in copies:
        copy.start()
    for spin, pad_ref in enumerate((low_ref, high_ref)):
        copies[spin].wait()
        split_boxes(orb_ref.at[spin], flat_ref, boxes)

        def slabs(box, _):
            flat_to_slabs(
                lambda t: flat_ref[pl.ds(box + 8 * t, HALF, stride=8 * PAIRT), :],
                lambda u, parity, x: pad_ref.__setitem__(
                    (0, box, u, pl.ds(PAD + parity, HALF, stride=2), slice(None)), x),
            )
            reverse_box(pad_ref, box)
            return 0

        lax.fori_loop(0, boxes, slabs, 0)

    copies[2].wait()
    front = lax.broadcasted_iota(jnp.int32, (EDGE, 1), 0) < HALF

    def build(i, _):
        where = pl.ds(pl.multiple_of(i * 2 * EDGE, 16), 2 * EDGE)
        for first, size in CHUNKS:
            cols = slice(first, first + size)
            line = [fac_ref[0, pl.ds(2 * i + k, 1), cols] for k in range(2)]
            mode = [fac_ref[3, pl.ds(4 * i + k, 1), cols] for k in range(4)]
            modes = [jnp.where(front, mode[2 * k], mode[2 * k + 1]) for k in range(2)]
            for part in range(2):
                right = fac_ref[1 + part, :, cols]
                to_ref[part, where, cols] = jnp.concatenate([x * right for x in line], axis=0).astype(BF)
                right = fac_ref[4 + part, :, cols]
                from_ref[part, where, cols] = jnp.concatenate([x * right for x in modes], axis=0).astype(BF)
        return 0

    lax.fori_loop(0, HALF // 2, build, 0)
    for part in range(2):
        to_ref[part, FOLD:, :] = jnp.zeros((FWIDE - FOLD, FWIDE), BF)
        from_ref[part, FOLD:, :] = jnp.zeros((FWIDE - FOLD, FWIDE), BF)
    for copy in copies[3:]:
        copy.wait()


def fill_kernel(old_ref, prev_ref, next_ref, pad_ref, flat_ref):
    boxes = pad_ref.shape[1] - 2
    for side, ref in ((0, prev_ref), (1, next_ref)):
        flat_ref[...] = ref[...].astype(F32)
        flat_to_slabs(
            lambda t: flat_ref[pl.ds(t, HALF, stride=PAIRT), :],
            lambda u, parity, x: pad_ref.__setitem__(
                (0, boxes + side, u, pl.ds(PAD + parity, HALF, stride=2), slice(None)), x),
        )
        reverse_box(pad_ref, boxes + side)


def pair_kernel(start, held, spins, final, tab_ref, to_ref, from_ref, diag_ref, inv_ref, *refs):
    pads, (mov_ref, x_ref, y_ref, half_ref, res_ref) = refs[:len(spins)], refs[-5:]
    boxes = pads[0].shape[1] - 2
    pairs, codes, _, leaves, order, homes, _ = table_layout(boxes)
    if final:
        low_ref, high_ref, out_ref, form_ref, sems = refs[len(spins):-5]

        def copy(slot):
            return pltpu.make_async_copy(form_ref.at[slot], out_ref.at[slot], sems.at[slot])

        def early(slot, _):
            code = tab_ref[codes + slot]

            @pl.when(code < start)
            def _():
                spot = jnp.minimum(code, start - 1)
                for spin, ref in enumerate((low_ref, high_ref)):
                    form_ref[slot, pl.ds(spin, FLAT, stride=2), :] = ref[spot]
                copy(slot).start()

            @pl.when(code >= boxes + AHEAD + BACK)
            def _():
                form_ref[slot] = jnp.zeros(form_ref.shape[1:], F32)
                copy(slot).start()

            return 0

        lax.fori_loop(0, CAP, early, 0)
    else:
        out_ref, sends = refs[len(spins)], refs[len(spins) + 1:-5]
    lanes = lane_iota()
    rows = lax.broadcasted_iota(jnp.int32, (EDGE, 1), 0)

    def dense(index, _):
        box = tab_ref[order + start + index]
        places = []
        for number in range(PARTNERS):
            base = pairs + (box * PARTNERS + number) * 4
            source = tab_ref[base]
            da, db, dc = tab_ref[base + 1], tab_ref[base + 2], tab_ref[base + 3]
            row_ok = jnp.abs(2 * (rows - da) - (EDGE - 1)) < EDGE
            for b_by, c_by in ((db, dc), (-db, -dc)):
                offset = ZERO_TILES * LANES - (b_by * EDGE + c_by)
                places.append((source, da, b_by, c_by, offset // LANES, offset % LANES, row_ok))
        last = [[None] * len(places) for _ in spins]
        for u in range(FTILES + 1):
            keep = []
            for source, da, b_by, c_by, quotient, rest, row_ok in places:
                if u > 0:
                    cell = lanes + (u - 1) * LANES
                    b = (cell * 52429) >> 21
                    c = cell - b * EDGE
                    ok = (jnp.abs(2 * (b - b_by) - (EDGE - 1)) < EDGE) & (jnp.abs(2 * (c - c_by) - (EDGE - 1)) < EDGE)
                    if u == FTILES:
                        ok = ok & (lanes < FOLD - (FTILES - 1) * LANES)
                    keep.append(row_ok & ok)
            for at, pad_ref in enumerate(pads):
                values = []
                for which, (source, da, b_by, c_by, quotient, rest, row_ok) in enumerate(places):
                    part = which % 2
                    tile = jnp.clip(quotient + (u - ZERO_TILES), 0, TILES - 1)
                    x = pad_ref[part, source, tile, pl.ds(PAD - da, EDGE), :]
                    turned = pltpu.roll(x, (LANES - rest) % LANES, 1)
                    if u > 0:
                        moved = jnp.where(keep[which], jnp.where(lanes < LANES - rest, last[at][which], turned), 0.0)
                        mov_ref[index, at, which // 2, part, u - 1] = moved
                        values.append(pad_ref[part, box, u - 1, pl.ds(PAD, EDGE), :] * moved)
                    last[at][which] = turned
                if u > 0:
                    where = pl.ds(pl.multiple_of((index * len(spins) + at) * PARTNERS * EDGE, 16), PARTNERS * EDGE)
                    front = jnp.concatenate(values[0::2], axis=0)
                    behind = jnp.concatenate(values[1::2], axis=0)
                    x_ref[where, (u - 1) * LANES:u * LANES] = (front + behind).astype(BF)
                    x_ref[where, FWIDE + (u - 1) * LANES:FWIDE + u * LANES] = (front - behind).astype(BF)
        return 0

    lax.fori_loop(0, held, dense, 0)

    cubes = held * len(spins) * PARTNERS
    diag = diag_ref[...]
    for first in range(0, 2 * FWIDE, NCHUNK):
        cols = slice(first, first + NCHUNK)
        y_ref[:, cols] = jnp.dot(diag, x_ref[:, cols], preferred_element_type=F32).astype(BF)

    def forward(first, size):
        for part in range(2):
            z = jnp.dot(y_ref[:, part * FWIDE:(part + 1) * FWIDE], to_ref[part, :, pl.ds(first, size)],
                        preferred_element_type=F32)
            cols = pl.ds(pl.multiple_of(part * FWIDE + first, LANES), size)
            z = z.reshape(cubes, EDGE, size) * inv_ref[:, cols][None]
            x_ref[:, cols] = z.reshape(cubes * EDGE, size).astype(BF)

    def backward(first, size):
        even, odd = [jnp.dot(x_ref[:, part * FWIDE:(part + 1) * FWIDE], from_ref[part, :, pl.ds(first, size)],
                             preferred_element_type=F32) for part in range(2)]
        y_ref[:, pl.ds(first, size)] = (even + odd).astype(BF)
        y_ref[:, pl.ds(pl.multiple_of(FWIDE + first, LANES), size)] = (even - odd).astype(BF)

    for step in (forward, backward):
        whole_steps = FWIDE // NCHUNK

        def looped(n, _):
            step(pl.multiple_of(n * NCHUNK, NCHUNK), NCHUNK)
            return 0

        lax.fori_loop(0, whole_steps, looped, 0)
        if FWIDE % NCHUNK:
            step(whole_steps * NCHUNK, FWIDE % NCHUNK)

    for first in range(0, 2 * FTILES, 2):
        potential = jnp.dot(diag, y_ref[:, first * LANES:(first + 2) * LANES], preferred_element_type=F32)
        for u in (first, first + 1):
            side = slice((u - first) * LANES, (u - first + 1) * LANES)
            for index in range(held):
                for at in range(len(spins)):
                    total = 0.0
                    for number in range(PARTNERS):
                        row = ((index * len(spins) + at) * PARTNERS + number) * EDGE
                        total = total + potential[row:row + EDGE, side] * mov_ref[index, at, number, u // FTILES, u % FTILES]
                    if u < FTILES:
                        res_ref[index * len(spins) + at, u] = total
                    else:
                        half_ref[index * len(spins) + at, u - FTILES] = total

    def unfold(row, _):
        middle = FTILES - 1

        def store(u, x):
            if u == middle:
                x = jnp.where(lanes < FOLD - middle * LANES, res_ref[row, middle], x)
            res_ref[row, u] = x

        reverse_slabs(lambda v: half_ref[row, v], store, middle, FTILES)
        return 0

    lax.fori_loop(0, held * len(spins), unfold, 0)

    if final:
        for index in range(held):
            home = tab_ref[homes + start + index]
            for at in range(len(spins)):
                slabs_to_flat(
                    lambda u, parity: res_ref[index * len(spins) + at, u, pl.ds(parity, HALF, stride=2), :],
                    lambda t, x: form_ref.__setitem__(
                        (home, pl.ds(2 * t + at, HALF, stride=2 * PAIRT), slice(None)), x),
                )
            copy(home).start()

        def finish(slot, _):
            code = tab_ref[codes + slot]

            @pl.when((code < boxes) | (code >= boxes + AHEAD + BACK))
            def _():
                copy(slot).wait()

            return 0

        lax.fori_loop(0, CAP, finish, 0)
        return

    def flatten(row, _):
        slabs_to_flat(
            lambda u, parity: res_ref[row, u, pl.ds(parity, HALF, stride=2), :],
            lambda t, x: out_ref.__setitem__((row, pl.ds(t, HALF, stride=PAIRT), slice(None)), x),
        )
        return 0

    lax.fori_loop(0, held * len(spins), flatten, 0)
    for k in range(AHEAD):
        sends[0][k] = out_ref[tab_ref[leaves + k]].astype(BF)
    for k in range(BACK):
        sends[1][k] = out_ref[tab_ref[leaves + AHEAD + k]].astype(BF)


def place_kernel(boxes, tab_ref, prev_low, next_low, prev_high, next_high, kept_ref, out_ref, form_ref, sems):
    slots = table_layout(boxes)[2]
    copies = []
    for k in range(AHEAD + BACK):
        pair, row = ((prev_low, prev_high), k) if k < AHEAD else ((next_low, next_high), k - AHEAD)
        slot = tab_ref[slots + k]
        copy = pltpu.make_async_copy(form_ref.at[k], out_ref.at[jnp.minimum(slot, CAP - 1)], sems.at[k])

        @pl.when(slot < CAP)
        def _():
            for spin, ref in enumerate(pair):
                form_ref[k, pl.ds(spin, FLAT, stride=2), :] = ref[row].astype(F32)
            copy.start()

        copies.append((slot, copy))
    for slot, copy in copies:
        @pl.when(slot < CAP)
        def _():
            copy.wait()


def from_behind(value, steps):
    count = lax.axis_size(AXES)
    return lax.ppermute(value, AXES, [(source, (source + steps) % count) for source in range(count)])


def whole(count):
    return [pl.BlockSpec(memory_space=pltpu.VMEM)] * count


SCALARS = pl.BlockSpec(memory_space=pltpu.SMEM)
ANYWHERE = pl.BlockSpec(memory_space=pltpu.MemorySpace.HBM)


def in_place(value):
    return pltpu.with_memory_space_constraint(jnp.asarray(value), pltpu.HBM)


def cost(flops, size):
    return pl.CostEstimate(flops=flops, bytes_accessed=size, transcendentals=0)


def shards(orbitals, dest, partners, anchors):
    boxes = orbitals.shape[1]
    sine, inverse, factors = tables()
    partners_t, anchors_t = partners.T, anchors.T

    box = jax.ShapeDtypeStruct((FLAT, LANES), BF)
    splitter = pltpu.VMEM((FLAT * 8, LANES), F32)
    ahead_low, back_low, ahead_high, back_high, table = pl.pallas_call(
        window_kernel,
        out_shape=[box] * 4 + [jax.ShapeDtypeStruct((table_layout(boxes)[-1],), jnp.int32)],
        in_specs=[ANYWHERE] * 4,
        out_specs=whole(4) + [SCALARS],
        scratch_shapes=[pltpu.SMEM(dest.shape, jnp.int32), pltpu.SMEM(partners_t.shape, jnp.int32),
                        pltpu.SMEM(anchors_t.shape, jnp.int32), pltpu.VMEM(orbitals.shape, BF),
                        splitter, pltpu.SemaphoreType.DMA((5,))],
        compiler_params=pltpu.CompilerParams(vmem_limit_bytes=12 << 20),
        name="window",
    )(*map(in_place, (dest, partners_t, anchors_t, orbitals)))
    prev_low = from_behind(ahead_low, 1)
    next_low = from_behind(back_low, -1)
    prev_high = from_behind(ahead_high, 1)
    next_high = from_behind(back_high, -1)

    moving = AHEAD + BACK
    slabs = jax.ShapeDtypeStruct((2, boxes + 2, TILES, ROWS, LANES), F32)
    folded = jax.ShapeDtypeStruct((2, FWIDE, FWIDE), BF)
    diags = [np.kron(np.eye(cubes, dtype=np.float32), sine).astype(jnp.bfloat16)
             for cubes in (moving * PARTNERS, (boxes - moving) * 2 * PARTNERS)]
    handed = (inverse, *diags)
    prepare = pl.pallas_call(
        prepare_kernel,
        out_shape=[slabs, slabs, folded, folded]
        + [jax.ShapeDtypeStruct(value.shape, value.dtype) for value in handed],
        in_specs=[ANYWHERE] * 5,
        out_specs=whole(7),
        scratch_shapes=[pltpu.VMEM(orbitals.shape, BF), pltpu.VMEM(factors.shape, F32), splitter,
                        pltpu.SemaphoreType.DMA((6,))],
        compiler_params=pltpu.CompilerParams(vmem_limit_bytes=20 << 20),
        cost_estimate=cost(10_000_000, 10_000_000),
        name="prepare",
    )
    low, high, to_modes, from_modes, inverse, *diags = prepare(*map(in_place, (orbitals, factors, *handed)))
    pads = [low, high]
    for spin, halo in enumerate(((prev_low, next_low), (prev_high, next_high))):
        pads[spin] = pl.pallas_call(
            fill_kernel,
            out_shape=slabs,
            in_specs=whole(3),
            out_specs=pl.BlockSpec(memory_space=pltpu.VMEM),
            scratch_shapes=[pltpu.VMEM((FLAT, LANES), F32)],
            input_output_aliases={0: 0},
            compiler_params=pltpu.CompilerParams(vmem_limit_bytes=12 << 20),
            cost_estimate=cost(1_000_000, 2_000_000),
        )(pads[spin], *halo)

    shape = jax.ShapeDtypeStruct((CAP, 2 * FLAT, LANES), F32)

    def solve(start, held, spins, terms=None):
        cubes = held * len(spins) * PARTNERS
        final = terms is not None
        if final:
            shapes, specs = [shape], [ANYWHERE]
            extra = [pltpu.VMEM(shape.shape, F32), pltpu.SemaphoreType.DMA((CAP,))]
        else:
            shapes = [jax.ShapeDtypeStruct((held * len(spins), FLAT, LANES), F32)]
            shapes += [jax.ShapeDtypeStruct((count, FLAT, LANES), BF) for count in (AHEAD, BACK)]
            specs, extra = whole(3), []
        operands = [table, to_modes, from_modes, diags[final], inverse] + [pads[spin] for spin in spins] + (terms or [])
        return pl.pallas_call(
            lambda *refs: pair_kernel(start, held, spins, final, *refs),
            out_shape=shapes,
            in_specs=[SCALARS] + whole(len(operands) - 1),
            out_specs=specs,
            scratch_shapes=extra + [
                pltpu.VMEM((held, len(spins), PARTNERS, 2, FTILES, EDGE, LANES), F32),
                pltpu.VMEM((cubes * EDGE, 2 * FWIDE), BF),
                pltpu.VMEM((cubes * EDGE, 2 * FWIDE), BF),
                pltpu.VMEM((held * len(spins), FTILES, EDGE, LANES), F32),
                pltpu.VMEM((held * len(spins), TILES, EDGE, LANES), F32),
            ],
            compiler_params=pltpu.CompilerParams(vmem_limit_bytes=20 << 20),
            cost_estimate=cost(2 * cubes * EDGE * FACE * FACE, 10_000_000),
        )(*operands)

    terms, arrived = [], []
    for spin in range(2):
        mine, sent_ahead, sent_back = solve(0, moving, (spin,))
        terms.append(mine)
        ahead = from_behind(sent_ahead, 1)
        back = from_behind(sent_back, -1)
        arrived += [ahead, back]
    kept, = solve(moving, boxes - moving, (0, 1), terms)
    placed = pl.pallas_call(
        lambda *refs: place_kernel(boxes, *refs),
        out_shape=shape,
        in_specs=[SCALARS] + whole(4) + [ANYWHERE],
        out_specs=ANYWHERE,
        scratch_shapes=[pltpu.VMEM((AHEAD + BACK, 2 * FLAT, LANES), F32),
                        pltpu.SemaphoreType.DMA((AHEAD + BACK,))],
        input_output_aliases={5: 0},
        compiler_params=pltpu.CompilerParams(vmem_limit_bytes=8 << 20),
        cost_estimate=cost(1_000_000, 4_000_000),
        name="place",
    )(table, *arrived, kept)
    placed = placed.reshape(-1).reshape(CAP, FLAT, 2, LANES).transpose(0, 2, 1, 3)
    return placed.reshape(CAP, 2, FLAT * LANES).transpose(1, 0, 2)


def solution(mesh):
    return jax.shard_map(
        shards,
        mesh=mesh,
        in_specs=(P(None, AXES, None), P(), P(), P()),
        out_specs=P(None, AXES, None),
        check_vma=False,
    )
```

```python
import jax
import jax.numpy as jnp
import numpy as np
from jax import lax
from jax.experimental import pallas as pl
from jax.experimental.pallas import tpu as pltpu
from jax.sharding import PartitionSpec as P


EDGE = 40
PARTNERS = 2
GRID_X = 768
GRID_Y = 384
GRID_Z = 384
BACK = 2
AHEAD = 1
CAP = 7
SCREEN = 0.001

AXES = ("gx", "gy", "gz")
LANES = 128
FACE = EDGE * EDGE
TILES = -(-FACE // LANES)
NCHUNK = 256
FOLD = FACE // 2
FTILES = -(-FOLD // LANES)
FWIDE = FTILES * LANES
CHUNKS = [(min(first, FWIDE - NCHUNK), NCHUNK) for first in range(0, FWIDE, NCHUNK)]
FLAT = EDGE ** 3 // LANES
HALF = EDGE // 2
PAIRT = 2 * FACE // LANES
PAD = 24
ROWS = EDGE + 2 * PAD
ZERO_TILES = 7
BF = jnp.bfloat16
F32 = jnp.float32


def tables():
    counter = np.arange(EDGE) + 1
    turns = np.outer(counter, counter) % (2 * (EDGE + 1))
    sine = (np.sqrt(2.0 / (EDGE + 1.0)) * np.sin(np.pi * turns / (EDGE + 1.0))).astype(np.float32)
    sine = sine.astype(jnp.bfloat16).astype(np.float32)
    flipped = sine[::-1] * np.where(np.arange(EDGE) % 2 == 0, 1.0, -1.0)
    assert np.array_equal(sine, flipped)
    levels = 2.0 - 2.0 * np.cos(np.pi * counter / (EDGE + 1.0))
    number = np.arange(FOLD)
    second, step = number // HALF, number % HALF
    thirds = [2 * step + second % 2, 2 * step + 1 - second % 2]
    inverse = np.zeros((EDGE, 2 * FWIDE), np.float32)
    for part, third in enumerate(thirds):
        lam = levels[:, None] + levels[second] + levels[third] + SCREEN
        inverse[:, part * FWIDE:part * FWIDE + FOLD] = 1.0 / lam
    factors = np.zeros((6, EDGE, FWIDE), np.float32)
    factors[0, :HALF, :FOLD] = sine[:HALF][:, second]
    for part, third in enumerate(thirds):
        factors[1 + part, :, :FOLD] = sine[:, third]
    factors[3, :, :FOLD] = np.repeat(sine[:HALF], EDGE, axis=0).T
    lines = np.tile(sine, (HALF, 1)).T
    factors[4, :, :FOLD] = np.concatenate([lines[0::2], lines[1::2]])
    factors[5, :, :FOLD] = np.concatenate([lines[1::2], lines[0::2]])
    return sine, inverse, factors


def lane_iota():
    return lax.broadcasted_iota(jnp.int32, (1, LANES), 1)


def split_boxes(orb_ref, flat_ref, boxes):
    def step(i, _):
        base = pl.multiple_of(i * PAIRT * LANES, LANES)
        x = orb_ref[:, pl.ds(base, PAIRT * LANES)].astype(F32)
        for j in range(PAIRT):
            flat_ref[pl.ds(pl.multiple_of((i * PAIRT + j) * 8, 8), boxes), :] = x[:, j * LANES:(j + 1) * LANES]
        return 0

    lax.fori_loop(0, HALF, step, 0)


def flat_to_slabs(load, store):
    low = lane_iota() < LANES // 2
    rolled = None
    for t in range(PAIRT):
        x = load(t)
        if t < TILES:
            store(t, 0, x)
        if t >= TILES - 1:
            turned = pltpu.roll(x, LANES // 2, 1)
            if rolled is not None:
                store(t - TILES, 1, jnp.where(low, rolled, turned))
            rolled = turned
    store(TILES - 1, 1, rolled)


def turn(x):
    source = (LANES // 2 - 1 - lax.broadcasted_iota(jnp.int32, x.shape, 1)) & (LANES - 1)
    return jnp.take_along_axis(x, source, axis=1)


def reverse_slabs(load, store, first, count):
    low = lane_iota() < LANES // 2
    turned = [turn(load(v)) for v in range(count)]
    for u in range(first, TILES):
        v = TILES - 1 - u
        store(u, jnp.where(low, turned[v], turned[v - 1]) if v > 0 else turned[v])


def slabs_to_flat(load, store):
    low = lane_iota() < LANES // 2
    for t in range(TILES - 1):
        store(t, load(t, 0))
    before = load(TILES - 1, 0)
    for v in range(TILES):
        turned = pltpu.roll(load(v, 1), LANES // 2, 1)
        store(TILES - 1 + v, jnp.where(low, before, turned))
        before = turned


def wanted_boxes(part_ref, boxes):
    total = part_ref.shape[1]
    device = lax.axis_index(AXES)
    wanted = []
    for step in (1, -1):
        found = jnp.int32(0)
        for k in range(boxes):
            other = (device + step) * boxes + k
            inside = (other >= 0) & (other < total)
            for number in range(PARTNERS):
                local = part_ref[number, jnp.clip(other, 0, total - 1)] - device * boxes
                found = jnp.where(inside & (local >= 0) & (local < boxes), local, found)
        wanted.append(found)
    return wanted


def window_kernel(part_hbm, orb_hbm, ahead_ref, back_ref, part_ref, orb_ref, flat_ref, sems):
    boxes = orb_ref.shape[0]
    small = pltpu.make_async_copy(part_hbm, part_ref, sems.at[0])
    large = pltpu.make_async_copy(orb_hbm.at[0], orb_ref, sems.at[1])
    small.start()
    large.start()
    small.wait()
    wanted = wanted_boxes(part_ref, boxes)
    large.wait()
    split_boxes(orb_ref, flat_ref, boxes)
    for side, ref in enumerate((ahead_ref, back_ref)):
        ref[...] = flat_ref[pl.ds(wanted[side], FLAT, stride=8), :].astype(BF)


def table_layout(boxes):
    pairs = 0
    codes = pairs + boxes * PARTNERS * 4
    slots = codes + CAP + 1
    leaves = slots + AHEAD + BACK + 1
    order = leaves + AHEAD + BACK + 1
    homes = order + boxes
    return pairs, codes, slots, leaves, order, homes, homes + boxes + 1


def build_tables(dest_ref, part_ref, anc_ref, tab_ref, boxes):
    total = part_ref.shape[1]
    device = lax.axis_index(AXES)
    pairs, codes, slots, leaves, order, homes, _ = table_layout(boxes)
    one, none = jnp.int32(1), jnp.int32(0)
    for k in range(CAP + 1):
        tab_ref[codes + k] = boxes + AHEAD + BACK
    for k in range(boxes + 1):
        tab_ref[homes + k] = 0
    for k in range(AHEAD + BACK + 1):
        tab_ref[slots + k] = CAP
        tab_ref[leaves + k] = 0
    goes = [dest_ref[device * boxes + k] for k in range(boxes)]
    ahead_all, back_all = none, none
    for k in range(boxes):
        ahead_all = ahead_all + jnp.where(goes[k] == device + 1, one, none)
        back_all = back_all + jnp.where(goes[k] == device - 1, one, none)
    ahead, back, stay = none, none, none
    spots = []
    for k in range(boxes):
        is_ahead, is_back = goes[k] == device + 1, goes[k] == device - 1
        spot = jnp.where(is_ahead, ahead, jnp.where(is_back, ahead_all + back, ahead_all + back_all + stay))
        spots.append(spot)
        tab_ref[order + spot] = k
        spare = leaves + AHEAD + BACK
        tab_ref[jnp.where(is_ahead, leaves + jnp.minimum(ahead, AHEAD - 1), spare)] = spot
        tab_ref[jnp.where(is_back, leaves + AHEAD + jnp.minimum(back, BACK - 1), spare)] = spot
        ahead = ahead + jnp.where(is_ahead, one, none)
        back = back + jnp.where(is_back, one, none)
        stay = stay + jnp.where(is_ahead | is_back, none, one)
    count = none
    for block in range(3):
        arrived = none
        for k in range(boxes):
            box = (device + (block - 1)) * boxes + k
            hit = (box >= 0) & (box < total) & (dest_ref[jnp.clip(box, 0, total - 1)] == device)
            if block == 1:
                code = spots[k]
                tab_ref[jnp.where(hit, homes + code, homes + boxes)] = jnp.minimum(count, CAP - 1)
            else:
                first, most = (0, AHEAD) if block == 0 else (AHEAD, BACK)
                where = first + jnp.minimum(arrived, most - 1)
                code = boxes + where
                tab_ref[jnp.where(hit, slots + where, slots + AHEAD + BACK)] = count
                arrived = arrived + jnp.where(hit, one, none)
            tab_ref[jnp.where(hit, codes + jnp.minimum(count, CAP - 1), codes + CAP)] = code
            count = count + jnp.where(hit, one, none)
    for box in range(boxes):
        me = device * boxes + box
        for number in range(PARTNERS):
            other = part_ref[number, me]
            local = other - device * boxes
            base = pairs + (box * PARTNERS + number) * 4
            tab_ref[base] = jnp.where(local < 0, boxes, jnp.where(local >= boxes, boxes + 1, local))
            for axis, extent in enumerate((GRID_X, GRID_Y, GRID_Z)):
                moved = anc_ref[axis, other] - anc_ref[axis, me] + extent // 2
                moved = jnp.where(moved < 0, moved + extent, jnp.where(moved >= extent, moved - extent, moved))
                tab_ref[base + 1 + axis] = jnp.clip(moved - extent // 2, -(PAD - 4), PAD - 4)


def reverse_box(pad_ref, box):
    body = pl.ds(PAD, EDGE)
    reverse_slabs(lambda v: pad_ref[0, box, v, body, :],
                  lambda u, x: pad_ref.__setitem__((1, box, u, body, slice(None)), x), 0, TILES)


def prepare_kernel(dest_hbm, part_hbm, anc_hbm, orb_hbm, inv_hbm, diag_hbm, rest_hbm,
                   low_ref, high_ref, ahead_ref, back_ref, tab_ref, inv_ref, diag_ref, rest_ref,
                   dest_ref, part_ref, anc_ref, orb_ref, flat_ref, sems):
    boxes = orb_ref.shape[1]
    pieces = [(part_hbm, part_ref), (dest_hbm, dest_ref), (anc_hbm, anc_ref)]
    pieces += [(orb_hbm.at[spin], orb_ref.at[spin]) for spin in range(2)]
    pieces += [(inv_hbm, inv_ref), (diag_hbm, diag_ref), (rest_hbm, rest_ref)]
    copies = [pltpu.make_async_copy(source, target, sems.at[k]) for k, (source, target) in enumerate(pieces)]
    for copy in copies:
        copy.start()
    for copy in copies[:3]:
        copy.wait()
    build_tables(dest_ref, part_ref, anc_ref, tab_ref, boxes)
    wanted = wanted_boxes(part_ref, boxes)
    for spin, pad_ref in enumerate((low_ref, high_ref)):
        copies[3 + spin].wait()
        split_boxes(orb_ref.at[spin], flat_ref, boxes)
        if spin == 1:
            for side, ref in enumerate((ahead_ref, back_ref)):
                ref[...] = flat_ref[pl.ds(wanted[side], FLAT, stride=8), :].astype(BF)

        def slabs(box, _):
            flat_to_slabs(
                lambda t: flat_ref[pl.ds(box + 8 * t, HALF, stride=8 * PAIRT), :],
                lambda u, parity, x: pad_ref.__setitem__(
                    (0, box, u, pl.ds(PAD + parity, HALF, stride=2), slice(None)), x),
            )
            reverse_box(pad_ref, box)
            return 0

        lax.fori_loop(0, boxes, slabs, 0)
    for copy in copies[5:]:
        copy.wait()


def modes_kernel(early, fac_hbm, *refs):
    to_ref, from_ref, fac_ref, sem = refs[-4:]
    first = lax.axis_index(AXES[-1]) == 0

    @pl.when(first if early else jnp.logical_not(first))
    def _():
        copy = pltpu.make_async_copy(fac_hbm, fac_ref, sem)
        copy.start()
        for part in range(2):
            to_ref[part, FOLD:, :] = jnp.zeros((FWIDE - FOLD, FWIDE), BF)
            from_ref[part, FOLD:, :] = jnp.zeros((FWIDE - FOLD, FWIDE), BF)
        front = lax.broadcasted_iota(jnp.int32, (EDGE, 1), 0) < HALF
        copy.wait()

        def build(i, _):
            where = pl.ds(pl.multiple_of(i * 2 * EDGE, 16), 2 * EDGE)
            for start, size in CHUNKS:
                cols = slice(start, start + size)
                line = [fac_ref[0, pl.ds(2 * i + k, 1), cols] for k in range(2)]
                mode = [fac_ref[3, pl.ds(4 * i + k, 1), cols] for k in range(4)]
                modes = [jnp.where(front, mode[2 * k], mode[2 * k + 1]) for k in range(2)]
                for part in range(2):
                    right = fac_ref[1 + part, :, cols]
                    to_ref[part, where, cols] = jnp.concatenate([x * right for x in line], axis=0).astype(BF)
                    right = fac_ref[4 + part, :, cols]
                    from_ref[part, where, cols] = jnp.concatenate([x * right for x in modes], axis=0).astype(BF)
            return 0

        lax.fori_loop(0, HALF // 2, build, 0)


def fill_kernel(old_ref, prev_ref, next_ref, pad_ref, flat_ref):
    boxes = pad_ref.shape[1] - 2
    for side, ref in ((0, prev_ref), (1, next_ref)):
        flat_ref[...] = ref[...].astype(F32)
        flat_to_slabs(
            lambda t: flat_ref[pl.ds(t, HALF, stride=PAIRT), :],
            lambda u, parity, x: pad_ref.__setitem__(
                (0, boxes + side, u, pl.ds(PAD + parity, HALF, stride=2), slice(None)), x),
        )
        reverse_box(pad_ref, boxes + side)


def pair_kernel(start, held, spins, final, tab_ref, to_ref, from_ref, diag_ref, inv_ref, *refs):
    pads, (mov_ref, x_ref, y_ref, half_ref, res_ref) = refs[:len(spins)], refs[-5:]
    boxes = pads[0].shape[1] - 2
    pairs, codes, _, leaves, order, homes, _ = table_layout(boxes)
    if final:
        low_ref, high_ref, out_ref, form_ref, sems = refs[len(spins):-5]

        def copy(slot):
            return pltpu.make_async_copy(form_ref.at[slot], out_ref.at[slot], sems.at[slot])

        def early(slot, _):
            code = tab_ref[codes + slot]

            @pl.when(code < start)
            def _():
                spot = jnp.minimum(code, start - 1)
                for spin, ref in enumerate((low_ref, high_ref)):
                    form_ref[slot, pl.ds(spin, FLAT, stride=2), :] = ref[spot]
                copy(slot).start()

            @pl.when(code >= boxes + AHEAD + BACK)
            def _():
                form_ref[slot] = jnp.zeros(form_ref.shape[1:], F32)
                copy(slot).start()

            return 0

        lax.fori_loop(0, CAP, early, 0)
    else:
        out_ref, sends = refs[len(spins)], refs[len(spins) + 1:-5]
    lanes = lane_iota()
    rows = lax.broadcasted_iota(jnp.int32, (EDGE, 1), 0)

    def dense(index, _):
        box = tab_ref[order + start + index]
        places = []
        for number in range(PARTNERS):
            base = pairs + (box * PARTNERS + number) * 4
            source = tab_ref[base]
            da, db, dc = tab_ref[base + 1], tab_ref[base + 2], tab_ref[base + 3]
            row_ok = jnp.abs(2 * (rows - da) - (EDGE - 1)) < EDGE
            for b_by, c_by in ((db, dc), (-db, -dc)):
                offset = ZERO_TILES * LANES - (b_by * EDGE + c_by)
                places.append((source, da, b_by, c_by, offset // LANES, offset % LANES, row_ok))
        last = [[None] * len(places) for _ in spins]
        for u in range(FTILES + 1):
            keep = []
            for source, da, b_by, c_by, quotient, rest, row_ok in places:
                if u > 0:
                    cell = lanes + (u - 1) * LANES
                    b = (cell * 52429) >> 21
                    c = cell - b * EDGE
                    ok = (jnp.abs(2 * (b - b_by) - (EDGE - 1)) < EDGE) & (jnp.abs(2 * (c - c_by) - (EDGE - 1)) < EDGE)
                    if u == FTILES:
                        ok = ok & (lanes < FOLD - (FTILES - 1) * LANES)
                    keep.append(row_ok & ok)
            for at, pad_ref in enumerate(pads):
                values = []
                for which, (source, da, b_by, c_by, quotient, rest, row_ok) in enumerate(places):
                    part = which % 2
                    tile = jnp.clip(quotient + (u - ZERO_TILES), 0, TILES - 1)
                    x = pad_ref[part, source, tile, pl.ds(PAD - da, EDGE), :]
                    turned = pltpu.roll(x, (LANES - rest) % LANES, 1)
                    if u > 0:
                        moved = jnp.where(keep[which], jnp.where(lanes < LANES - rest, last[at][which], turned), 0.0)
                        mov_ref[index, at, which // 2, part, u - 1] = moved
                        values.append(pad_ref[part, box, u - 1, pl.ds(PAD, EDGE), :] * moved)
                    last[at][which] = turned
                if u > 0:
                    where = pl.ds(pl.multiple_of((index * len(spins) + at) * PARTNERS * EDGE, 16), PARTNERS * EDGE)
                    front = jnp.concatenate(values[0::2], axis=0)
                    behind = jnp.concatenate(values[1::2], axis=0)
                    x_ref[where, (u - 1) * LANES:u * LANES] = (front + behind).astype(BF)
                    x_ref[where, FWIDE + (u - 1) * LANES:FWIDE + u * LANES] = (front - behind).astype(BF)
        return 0

    lax.fori_loop(0, held, dense, 0)

    cubes = held * len(spins) * PARTNERS
    diag = diag_ref[...]
    for first in range(0, 2 * FWIDE, NCHUNK):
        cols = slice(first, first + NCHUNK)
        y_ref[:, cols] = jnp.dot(diag, x_ref[:, cols], preferred_element_type=F32).astype(BF)

    def forward(first, size):
        for part in range(2):
            z = jnp.dot(y_ref[:, part * FWIDE:(part + 1) * FWIDE], to_ref[part, :, pl.ds(first, size)],
                        preferred_element_type=F32)
            cols = pl.ds(pl.multiple_of(part * FWIDE + first, LANES), size)
            z = z.reshape(cubes, EDGE, size) * inv_ref[:, cols][None]
            x_ref[:, cols] = z.reshape(cubes * EDGE, size).astype(BF)

    def backward(first, size):
        even, odd = [jnp.dot(x_ref[:, part * FWIDE:(part + 1) * FWIDE], from_ref[part, :, pl.ds(first, size)],
                             preferred_element_type=F32) for part in range(2)]
        y_ref[:, pl.ds(first, size)] = (even + odd).astype(BF)
        y_ref[:, pl.ds(pl.multiple_of(FWIDE + first, LANES), size)] = (even - odd).astype(BF)

    for step in (forward, backward):
        whole_steps = FWIDE // NCHUNK

        def looped(n, _):
            step(pl.multiple_of(n * NCHUNK, NCHUNK), NCHUNK)
            return 0

        lax.fori_loop(0, whole_steps, looped, 0)
        if FWIDE % NCHUNK:
            step(whole_steps * NCHUNK, FWIDE % NCHUNK)

    for first in range(0, 2 * FTILES, 2):
        potential = jnp.dot(diag, y_ref[:, first * LANES:(first + 2) * LANES], preferred_element_type=F32)
        for u in (first, first + 1):
            side = slice((u - first) * LANES, (u - first + 1) * LANES)
            for index in range(held):
                for at in range(len(spins)):
                    total = 0.0
                    for number in range(PARTNERS):
                        row = ((index * len(spins) + at) * PARTNERS + number) * EDGE
                        total = total + potential[row:row + EDGE, side] * mov_ref[index, at, number, u // FTILES, u % FTILES]
                    if u < FTILES:
                        res_ref[index * len(spins) + at, u] = total
                    else:
                        half_ref[index * len(spins) + at, u - FTILES] = total

    def unfold(row, _):
        middle = FTILES - 1

        def store(u, x):
            if u == middle:
                x = jnp.where(lanes < FOLD - middle * LANES, res_ref[row, middle], x)
            res_ref[row, u] = x

        reverse_slabs(lambda v: half_ref[row, v], store, middle, FTILES)
        return 0

    lax.fori_loop(0, held * len(spins), unfold, 0)

    if final:
        for index in range(held):
            home = tab_ref[homes + start + index]
            for at in range(len(spins)):
                slabs_to_flat(
                    lambda u, parity: res_ref[index * len(spins) + at, u, pl.ds(parity, HALF, stride=2), :],
                    lambda t, x: form_ref.__setitem__(
                        (home, pl.ds(2 * t + at, HALF, stride=2 * PAIRT), slice(None)), x),
                )
            copy(home).start()

        def finish(slot, _):
            code = tab_ref[codes + slot]

            @pl.when((code < boxes) | (code >= boxes + AHEAD + BACK))
            def _():
                copy(slot).wait()

            return 0

        lax.fori_loop(0, CAP, finish, 0)
        return

    def flatten(row, _):
        slabs_to_flat(
            lambda u, parity: res_ref[row, u, pl.ds(parity, HALF, stride=2), :],
            lambda t, x: out_ref.__setitem__((row, pl.ds(t, HALF, stride=PAIRT), slice(None)), x),
        )
        return 0

    lax.fori_loop(0, held * len(spins), flatten, 0)
    for k in range(AHEAD):
        sends[0][k] = out_ref[tab_ref[leaves + k]].astype(BF)
    for k in range(BACK):
        sends[1][k] = out_ref[tab_ref[leaves + AHEAD + k]].astype(BF)


def place_kernel(boxes, tab_ref, prev_low, next_low, prev_high, next_high, kept_ref, out_ref, form_ref, sems):
    slots = table_layout(boxes)[2]
    copies = []
    for k in range(AHEAD + BACK):
        pair, row = ((prev_low, prev_high), k) if k < AHEAD else ((next_low, next_high), k - AHEAD)
        slot = tab_ref[slots + k]
        copy = pltpu.make_async_copy(form_ref.at[k], out_ref.at[jnp.minimum(slot, CAP - 1)], sems.at[k])

        @pl.when(slot < CAP)
        def _():
            for spin, ref in enumerate(pair):
                form_ref[k, pl.ds(spin, FLAT, stride=2), :] = ref[row].astype(F32)
            copy.start()

        copies.append((slot, copy))
    for slot, copy in copies:
        @pl.when(slot < CAP)
        def _():
            copy.wait()


def from_behind(value, steps):
    count = lax.axis_size(AXES)
    return lax.ppermute(value, AXES, [(source, (source + steps) % count) for source in range(count)])


def whole(count):
    return [pl.BlockSpec(memory_space=pltpu.VMEM)] * count


SCALARS = pl.BlockSpec(memory_space=pltpu.SMEM)
ANYWHERE = pl.BlockSpec(memory_space=pltpu.MemorySpace.HBM)


def in_place(value):
    return pltpu.with_memory_space_constraint(jnp.asarray(value), pltpu.HBM)


def cost(flops, size):
    return pl.CostEstimate(flops=flops, bytes_accessed=size, transcendentals=0)


def shards(orbitals, dest, partners, anchors):
    boxes = orbitals.shape[1]
    sine, inverse, factors = tables()
    partners_t, anchors_t = partners.T, anchors.T

    box = jax.ShapeDtypeStruct((FLAT, LANES), BF)
    splitter = pltpu.VMEM((FLAT * 8, LANES), F32)
    ahead, back = pl.pallas_call(
        window_kernel,
        out_shape=[box] * 2,
        in_specs=[ANYWHERE] * 2,
        out_specs=whole(2),
        scratch_shapes=[pltpu.SMEM(partners_t.shape, jnp.int32), pltpu.VMEM(orbitals.shape[1:], BF),
                        splitter, pltpu.SemaphoreType.DMA((2,))],
        compiler_params=pltpu.CompilerParams(vmem_limit_bytes=12 << 20),
        name="window",
    )(*map(in_place, (partners_t, orbitals)))
    prev_low = from_behind(ahead, 1)
    next_low = from_behind(back, -1)

    folded = jax.ShapeDtypeStruct((2, FWIDE, FWIDE), BF)

    def build_modes(early, *before):
        return pl.pallas_call(
            lambda *refs: modes_kernel(early, *refs),
            out_shape=[folded] * 2,
            in_specs=[ANYWHERE] + whole(len(before)),
            out_specs=whole(2),
            scratch_shapes=[pltpu.VMEM(factors.shape, F32), pltpu.SemaphoreType.DMA],
            input_output_aliases={1: 0, 2: 1} if before else {},
            compiler_params=pltpu.CompilerParams(vmem_limit_bytes=12 << 20),
            cost_estimate=cost(4_000_000, 4_000_000),
        )(in_place(factors), *before)

    modes = build_modes(True)
    moving = AHEAD + BACK
    slabs = jax.ShapeDtypeStruct((2, boxes + 2, TILES, ROWS, LANES), F32)
    diags = [np.kron(np.eye(cubes, dtype=np.float32), sine).astype(jnp.bfloat16)
             for cubes in (moving * PARTNERS, (boxes - moving) * 2 * PARTNERS)]
    handed = (inverse, *diags)
    prepare = pl.pallas_call(
        prepare_kernel,
        out_shape=[slabs, slabs, box, box, jax.ShapeDtypeStruct((table_layout(boxes)[-1],), jnp.int32)]
        + [jax.ShapeDtypeStruct(value.shape, value.dtype) for value in handed],
        in_specs=[ANYWHERE] * 7,
        out_specs=whole(4) + [SCALARS] + whole(3),
        scratch_shapes=[pltpu.SMEM(dest.shape, jnp.int32), pltpu.SMEM(partners_t.shape, jnp.int32),
                        pltpu.SMEM(anchors_t.shape, jnp.int32), pltpu.VMEM(orbitals.shape, BF), splitter,
                        pltpu.SemaphoreType.DMA((8,))],
        compiler_params=pltpu.CompilerParams(vmem_limit_bytes=20 << 20),
        cost_estimate=cost(10_000_000, 10_000_000),
        name="prepare",
    )
    low, high, ahead, back, table, inverse, *diags = prepare(
        *map(in_place, (dest, partners_t, anchors_t, orbitals, *handed)))
    prev_high = from_behind(ahead, 1)
    next_high = from_behind(back, -1)
    to_modes, from_modes = build_modes(False, *modes)
    pads = [low, high]
    for spin, halo in enumerate(((prev_low, next_low), (prev_high, next_high))):
        pads[spin] = pl.pallas_call(
            fill_kernel,
            out_shape=slabs,
            in_specs=whole(3),
            out_specs=pl.BlockSpec(memory_space=pltpu.VMEM),
            scratch_shapes=[pltpu.VMEM((FLAT, LANES), F32)],
            input_output_aliases={0: 0},
            compiler_params=pltpu.CompilerParams(vmem_limit_bytes=12 << 20),
            cost_estimate=cost(1_000_000, 2_000_000),
        )(pads[spin], *halo)

    shape = jax.ShapeDtypeStruct((CAP, 2 * FLAT, LANES), F32)

    def solve(start, held, spins, terms=None):
        cubes = held * len(spins) * PARTNERS
        final = terms is not None
        if final:
            shapes, specs = [shape], [ANYWHERE]
            extra = [pltpu.VMEM(shape.shape, F32), pltpu.SemaphoreType.DMA((CAP,))]
        else:
            shapes = [jax.ShapeDtypeStruct((held * len(spins), FLAT, LANES), F32)]
            shapes += [jax.ShapeDtypeStruct((count, FLAT, LANES), BF) for count in (AHEAD, BACK)]
            specs, extra = whole(3), []
        operands = [table, to_modes, from_modes, diags[final], inverse] + [pads[spin] for spin in spins] + (terms or [])
        return pl.pallas_call(
            lambda *refs: pair_kernel(start, held, spins, final, *refs),
            out_shape=shapes,
            in_specs=[SCALARS] + whole(len(operands) - 1),
            out_specs=specs,
            scratch_shapes=extra + [
                pltpu.VMEM((held, len(spins), PARTNERS, 2, FTILES, EDGE, LANES), F32),
                pltpu.VMEM((cubes * EDGE, 2 * FWIDE), BF),
                pltpu.VMEM((cubes * EDGE, 2 * FWIDE), BF),
                pltpu.VMEM((held * len(spins), FTILES, EDGE, LANES), F32),
                pltpu.VMEM((held * len(spins), TILES, EDGE, LANES), F32),
            ],
            compiler_params=pltpu.CompilerParams(vmem_limit_bytes=20 << 20),
            cost_estimate=cost(2 * cubes * EDGE * FACE * FACE, 10_000_000),
        )(*operands)

    terms, arrived = [], []
    for spin in range(2):
        mine, sent_ahead, sent_back = solve(0, moving, (spin,))
        terms.append(mine)
        ahead = from_behind(sent_ahead, 1)
        back = from_behind(sent_back, -1)
        arrived += [ahead, back]
    kept, = solve(moving, boxes - moving, (0, 1), terms)
    placed = pl.pallas_call(
        lambda *refs: place_kernel(boxes, *refs),
        out_shape=shape,
        in_specs=[SCALARS] + whole(4) + [ANYWHERE],
        out_specs=ANYWHERE,
        scratch_shapes=[pltpu.VMEM((AHEAD + BACK, 2 * FLAT, LANES), F32),
                        pltpu.SemaphoreType.DMA((AHEAD + BACK,))],
        input_output_aliases={5: 0},
        compiler_params=pltpu.CompilerParams(vmem_limit_bytes=8 << 20),
        cost_estimate=cost(1_000_000, 4_000_000),
        name="place",
    )(table, *arrived, kept)
    placed = placed.reshape(-1).reshape(CAP, FLAT, 2, LANES).transpose(0, 2, 1, 3)
    return placed.reshape(CAP, 2, FLAT * LANES).transpose(1, 0, 2)


def solution(mesh):
    return jax.shard_map(
        shards,
        mesh=mesh,
        in_specs=(P(None, AXES, None), P(), P(), P()),
        out_specs=P(None, AXES, None),
        check_vma=False,
    )
```

```python
import jax
import jax.numpy as jnp
import numpy as np
from jax import lax
from jax.experimental import pallas as pl
from jax.experimental.pallas import tpu as pltpu
from jax.sharding import PartitionSpec as P


EDGE = 40
PARTNERS = 2
GRID_X = 768
GRID_Y = 384
GRID_Z = 384
BACK = 2
AHEAD = 1
CAP = 7
SCREEN = 0.001

AXES = ("gx", "gy", "gz")
LANES = 128
FACE = EDGE * EDGE
TILES = -(-FACE // LANES)
NCHUNK = 256
FOLD = FACE // 2
FTILES = -(-FOLD // LANES)
FWIDE = FTILES * LANES
CHUNKS = [(min(first, FWIDE - NCHUNK), NCHUNK) for first in range(0, FWIDE, NCHUNK)]
FLAT = EDGE ** 3 // LANES
HALF = EDGE // 2
PAIRT = 2 * FACE // LANES
PAD = 24
ROWS = EDGE + 2 * PAD
ZERO_TILES = 7
BF = jnp.bfloat16
F32 = jnp.float32


def tables():
    counter = np.arange(EDGE) + 1
    turns = np.outer(counter, counter) % (2 * (EDGE + 1))
    sine = (np.sqrt(2.0 / (EDGE + 1.0)) * np.sin(np.pi * turns / (EDGE + 1.0))).astype(np.float32)
    sine = sine.astype(jnp.bfloat16).astype(np.float32)
    flipped = sine[::-1] * np.where(np.arange(EDGE) % 2 == 0, 1.0, -1.0)
    assert np.array_equal(sine, flipped)
    levels = 2.0 - 2.0 * np.cos(np.pi * counter / (EDGE + 1.0))
    number = np.arange(FOLD)
    second, step = number // HALF, number % HALF
    thirds = [2 * step + second % 2, 2 * step + 1 - second % 2]
    inverse = np.zeros((EDGE, 2 * FWIDE), np.float32)
    for part, third in enumerate(thirds):
        lam = levels[:, None] + levels[second] + levels[third] + SCREEN
        inverse[:, part * FWIDE:part * FWIDE + FOLD] = 1.0 / lam
    factors = np.zeros((6, EDGE, FWIDE), np.float32)
    factors[0, :HALF, :FOLD] = sine[:HALF][:, second]
    for part, third in enumerate(thirds):
        factors[1 + part, :, :FOLD] = sine[:, third]
    factors[3, :, :FOLD] = np.repeat(sine[:HALF], EDGE, axis=0).T
    lines = np.tile(sine, (HALF, 1)).T
    factors[4, :, :FOLD] = np.concatenate([lines[0::2], lines[1::2]])
    factors[5, :, :FOLD] = np.concatenate([lines[1::2], lines[0::2]])
    return sine, inverse, factors


def lane_iota():
    return lax.broadcasted_iota(jnp.int32, (1, LANES), 1)


def split_boxes(orb_ref, flat_ref, boxes):
    def step(i, _):
        base = pl.multiple_of(i * PAIRT * LANES, LANES)
        x = orb_ref[:, pl.ds(base, PAIRT * LANES)].astype(F32)
        for j in range(PAIRT):
            flat_ref[pl.ds(pl.multiple_of((i * PAIRT + j) * 8, 8), boxes), :] = x[:, j * LANES:(j + 1) * LANES]
        return 0

    lax.fori_loop(0, HALF, step, 0)


def flat_to_slabs(load, store):
    low = lane_iota() < LANES // 2
    rolled = None
    for t in range(PAIRT):
        x = load(t)
        if t < TILES:
            store(t, 0, x)
        if t >= TILES - 1:
            turned = pltpu.roll(x, LANES // 2, 1)
            if rolled is not None:
                store(t - TILES, 1, jnp.where(low, rolled, turned))
            rolled = turned
    store(TILES - 1, 1, rolled)


def turn(x):
    source = (LANES // 2 - 1 - lax.broadcasted_iota(jnp.int32, x.shape, 1)) & (LANES - 1)
    return jnp.take_along_axis(x, source, axis=1)


def reverse_slabs(load, store, first, count):
    low = lane_iota() < LANES // 2
    turned = [turn(load(v)) for v in range(count)]
    for u in range(first, TILES):
        v = TILES - 1 - u
        store(u, jnp.where(low, turned[v], turned[v - 1]) if v > 0 else turned[v])


def slabs_to_flat(load, store):
    low = lane_iota() < LANES // 2
    for t in range(TILES - 1):
        store(t, load(t, 0))
    before = load(TILES - 1, 0)
    for v in range(TILES):
        turned = pltpu.roll(load(v, 1), LANES // 2, 1)
        store(TILES - 1 + v, jnp.where(low, before, turned))
        before = turned


def wanted_boxes(part_ref, boxes):
    total = part_ref.shape[1]
    device = lax.axis_index(AXES)
    wanted = []
    for step in (1, -1):
        found = jnp.int32(0)
        for k in range(boxes):
            other = (device + step) * boxes + k
            inside = (other >= 0) & (other < total)
            for number in range(PARTNERS):
                local = part_ref[number, jnp.clip(other, 0, total - 1)] - device * boxes
                found = jnp.where(inside & (local >= 0) & (local < boxes), local, found)
        wanted.append(found)
    return wanted


def window_kernel(part_hbm, orb_hbm, ahead_ref, back_ref, part_ref, orb_ref, flat_ref, sems):
    boxes = orb_ref.shape[0]
    small = pltpu.make_async_copy(part_hbm, part_ref, sems.at[0])
    large = pltpu.make_async_copy(orb_hbm.at[0], orb_ref, sems.at[1])
    small.start()
    large.start()
    small.wait()
    wanted = wanted_boxes(part_ref, boxes)
    large.wait()
    split_boxes(orb_ref, flat_ref, boxes)
    for side, ref in enumerate((ahead_ref, back_ref)):
        ref[...] = flat_ref[pl.ds(wanted[side], FLAT, stride=8), :].astype(BF)


def table_layout(boxes):
    pairs = 0
    codes = pairs + boxes * PARTNERS * 4
    slots = codes + CAP + 1
    leaves = slots + AHEAD + BACK + 1
    order = leaves + AHEAD + BACK + 1
    homes = order + boxes
    return pairs, codes, slots, leaves, order, homes, homes + boxes + 1


def build_tables(dest_ref, part_ref, anc_ref, tab_ref, boxes):
    total = part_ref.shape[1]
    device = lax.axis_index(AXES)
    pairs, codes, slots, leaves, order, homes, _ = table_layout(boxes)
    one, none = jnp.int32(1), jnp.int32(0)
    for k in range(CAP + 1):
        tab_ref[codes + k] = boxes + AHEAD + BACK
    for k in range(boxes + 1):
        tab_ref[homes + k] = 0
    for k in range(AHEAD + BACK + 1):
        tab_ref[slots + k] = CAP
        tab_ref[leaves + k] = 0
    goes = [dest_ref[device * boxes + k] for k in range(boxes)]
    ahead_all, back_all = none, none
    for k in range(boxes):
        ahead_all = ahead_all + jnp.where(goes[k] == device + 1, one, none)
        back_all = back_all + jnp.where(goes[k] == device - 1, one, none)
    ahead, back, stay = none, none, none
    spots = []
    for k in range(boxes):
        is_ahead, is_back = goes[k] == device + 1, goes[k] == device - 1
        spot = jnp.where(is_ahead, ahead, jnp.where(is_back, ahead_all + back, ahead_all + back_all + stay))
        spots.append(spot)
        tab_ref[order + spot] = k
        spare = leaves + AHEAD + BACK
        tab_ref[jnp.where(is_ahead, leaves + jnp.minimum(ahead, AHEAD - 1), spare)] = spot
        tab_ref[jnp.where(is_back, leaves + AHEAD + jnp.minimum(back, BACK - 1), spare)] = spot
        ahead = ahead + jnp.where(is_ahead, one, none)
        back = back + jnp.where(is_back, one, none)
        stay = stay + jnp.where(is_ahead | is_back, none, one)
    count = none
    for block in range(3):
        arrived = none
        for k in range(boxes):
            box = (device + (block - 1)) * boxes + k
            hit = (box >= 0) & (box < total) & (dest_ref[jnp.clip(box, 0, total - 1)] == device)
            if block == 1:
                code = spots[k]
                tab_ref[jnp.where(hit, homes + code, homes + boxes)] = jnp.minimum(count, CAP - 1)
            else:
                first, most = (0, AHEAD) if block == 0 else (AHEAD, BACK)
                where = first + jnp.minimum(arrived, most - 1)
                code = boxes + where
                tab_ref[jnp.where(hit, slots + where, slots + AHEAD + BACK)] = count
                arrived = arrived + jnp.where(hit, one, none)
            tab_ref[jnp.where(hit, codes + jnp.minimum(count, CAP - 1), codes + CAP)] = code
            count = count + jnp.where(hit, one, none)
    for box in range(boxes):
        me = device * boxes + box
        for number in range(PARTNERS):
            other = part_ref[number, me]
            local = other - device * boxes
            base = pairs + (box * PARTNERS + number) * 4
            tab_ref[base] = jnp.where(local < 0, boxes, jnp.where(local >= boxes, boxes + 1, local))
            for axis, extent in enumerate((GRID_X, GRID_Y, GRID_Z)):
                moved = anc_ref[axis, other] - anc_ref[axis, me] + extent // 2
                moved = jnp.where(moved < 0, moved + extent, jnp.where(moved >= extent, moved - extent, moved))
                tab_ref[base + 1 + axis] = jnp.clip(moved - extent // 2, -(PAD - 4), PAD - 4)


def reverse_box(pad_ref, box):
    body = pl.ds(PAD, EDGE)
    reverse_slabs(lambda v: pad_ref[0, box, v, body, :],
                  lambda u, x: pad_ref.__setitem__((1, box, u, body, slice(None)), x), 0, TILES)


def second_kernel(dest_hbm, part_hbm, anc_hbm, orb_hbm, inv_hbm, diag_hbm, rest_hbm,
                  orb_ref, ahead_ref, back_ref, tab_ref, inv_ref, diag_ref, rest_ref,
                  dest_ref, part_ref, anc_ref, flat_ref, sems):
    boxes = orb_ref.shape[1]
    pieces = [(part_hbm, part_ref), (dest_hbm, dest_ref), (anc_hbm, anc_ref)]
    pieces += [(orb_hbm.at[spin], orb_ref.at[spin]) for spin in (1, 0)]
    pieces += [(inv_hbm, inv_ref), (diag_hbm, diag_ref), (rest_hbm, rest_ref)]
    copies = [pltpu.make_async_copy(source, target, sems.at[k]) for k, (source, target) in enumerate(pieces)]
    for copy in copies:
        copy.start()
    for copy in copies[:3]:
        copy.wait()
    build_tables(dest_ref, part_ref, anc_ref, tab_ref, boxes)
    wanted = wanted_boxes(part_ref, boxes)
    copies[3].wait()
    split_boxes(orb_ref.at[1], flat_ref, boxes)
    for side, ref in enumerate((ahead_ref, back_ref)):
        ref[...] = flat_ref[pl.ds(wanted[side], FLAT, stride=8), :].astype(BF)
    for copy in copies[4:]:
        copy.wait()


def slabs_kernel(spin, near, orb_ref, *refs):
    pad_ref, flat_ref = refs[-2:]
    boxes = orb_ref.shape[1]
    low_half = 2 * lax.axis_index(AXES[-1]) < lax.axis_size(AXES[-1])

    @pl.when(low_half if near else jnp.logical_not(low_half))
    def _():
        split_boxes(orb_ref.at[spin], flat_ref, boxes)

        def slabs(box, _):
            flat_to_slabs(
                lambda t: flat_ref[pl.ds(box + 8 * t, HALF, stride=8 * PAIRT), :],
                lambda u, parity, x: pad_ref.__setitem__(
                    (0, box, u, pl.ds(PAD + parity, HALF, stride=2), slice(None)), x),
            )
            reverse_box(pad_ref, box)
            return 0

        lax.fori_loop(0, boxes, slabs, 0)


def modes_kernel(early, fac_hbm, *refs):
    to_ref, from_ref, fac_ref, sem = refs[-4:]
    first = lax.axis_index(AXES[-1]) == 0

    @pl.when(first if early else jnp.logical_not(first))
    def _():
        copy = pltpu.make_async_copy(fac_hbm, fac_ref, sem)
        copy.start()
        for part in range(2):
            to_ref[part, FOLD:, :] = jnp.zeros((FWIDE - FOLD, FWIDE), BF)
            from_ref[part, FOLD:, :] = jnp.zeros((FWIDE - FOLD, FWIDE), BF)
        front = lax.broadcasted_iota(jnp.int32, (EDGE, 1), 0) < HALF
        copy.wait()

        def build(i, _):
            where = pl.ds(pl.multiple_of(i * 2 * EDGE, 16), 2 * EDGE)
            for start, size in CHUNKS:
                cols = slice(start, start + size)
                line = [fac_ref[0, pl.ds(2 * i + k, 1), cols] for k in range(2)]
                mode = [fac_ref[3, pl.ds(4 * i + k, 1), cols] for k in range(4)]
                modes = [jnp.where(front, mode[2 * k], mode[2 * k + 1]) for k in range(2)]
                for part in range(2):
                    right = fac_ref[1 + part, :, cols]
                    to_ref[part, where, cols] = jnp.concatenate([x * right for x in line], axis=0).astype(BF)
                    right = fac_ref[4 + part, :, cols]
                    from_ref[part, where, cols] = jnp.concatenate([x * right for x in modes], axis=0).astype(BF)
            return 0

        lax.fori_loop(0, HALF // 2, build, 0)


def fill_kernel(old_ref, prev_ref, next_ref, pad_ref, flat_ref):
    boxes = pad_ref.shape[1] - 2
    for side, ref in ((0, prev_ref), (1, next_ref)):
        flat_ref[...] = ref[...].astype(F32)
        flat_to_slabs(
            lambda t: flat_ref[pl.ds(t, HALF, stride=PAIRT), :],
            lambda u, parity, x: pad_ref.__setitem__(
                (0, boxes + side, u, pl.ds(PAD + parity, HALF, stride=2), slice(None)), x),
        )
        reverse_box(pad_ref, boxes + side)


def pair_kernel(start, held, spins, final, tab_ref, to_ref, from_ref, diag_ref, inv_ref, *refs):
    pads, (mov_ref, x_ref, y_ref, half_ref, res_ref) = refs[:len(spins)], refs[-5:]
    boxes = pads[0].shape[1] - 2
    pairs, codes, _, leaves, order, homes, _ = table_layout(boxes)
    if final:
        low_ref, high_ref, out_ref, form_ref, sems = refs[len(spins):-5]

        def copy(slot):
            return pltpu.make_async_copy(form_ref.at[slot], out_ref.at[slot], sems.at[slot])

        def early(slot, _):
            code = tab_ref[codes + slot]

            @pl.when(code < start)
            def _():
                spot = jnp.minimum(code, start - 1)
                for spin, ref in enumerate((low_ref, high_ref)):
                    form_ref[slot, pl.ds(spin, FLAT, stride=2), :] = ref[spot]
                copy(slot).start()

            @pl.when(code >= boxes + AHEAD + BACK)
            def _():
                form_ref[slot] = jnp.zeros(form_ref.shape[1:], F32)
                copy(slot).start()

            return 0

        lax.fori_loop(0, CAP, early, 0)
    else:
        out_ref, sends = refs[len(spins)], refs[len(spins) + 1:-5]
    lanes = lane_iota()
    rows = lax.broadcasted_iota(jnp.int32, (EDGE, 1), 0)

    def dense(index, _):
        box = tab_ref[order + start + index]
        places = []
        for number in range(PARTNERS):
            base = pairs + (box * PARTNERS + number) * 4
            source = tab_ref[base]
            da, db, dc = tab_ref[base + 1], tab_ref[base + 2], tab_ref[base + 3]
            row_ok = jnp.abs(2 * (rows - da) - (EDGE - 1)) < EDGE
            for b_by, c_by in ((db, dc), (-db, -dc)):
                offset = ZERO_TILES * LANES - (b_by * EDGE + c_by)
                places.append((source, da, b_by, c_by, offset // LANES, offset % LANES, row_ok))
        last = [[None] * len(places) for _ in spins]
        for u in range(FTILES + 1):
            keep = []
            for source, da, b_by, c_by, quotient, rest, row_ok in places:
                if u > 0:
                    cell = lanes + (u - 1) * LANES
                    b = (cell * 52429) >> 21
                    c = cell - b * EDGE
                    ok = (jnp.abs(2 * (b - b_by) - (EDGE - 1)) < EDGE) & (jnp.abs(2 * (c - c_by) - (EDGE - 1)) < EDGE)
                    if u == FTILES:
                        ok = ok & (lanes < FOLD - (FTILES - 1) * LANES)
                    keep.append(row_ok & ok)
            for at, pad_ref in enumerate(pads):
                values = []
                for which, (source, da, b_by, c_by, quotient, rest, row_ok) in enumerate(places):
                    part = which % 2
                    tile = jnp.clip(quotient + (u - ZERO_TILES), 0, TILES - 1)
                    x = pad_ref[part, source, tile, pl.ds(PAD - da, EDGE), :]
                    turned = pltpu.roll(x, (LANES - rest) % LANES, 1)
                    if u > 0:
                        moved = jnp.where(keep[which], jnp.where(lanes < LANES - rest, last[at][which], turned), 0.0)
                        mov_ref[index, at, which // 2, part, u - 1] = moved
                        values.append(pad_ref[part, box, u - 1, pl.ds(PAD, EDGE), :] * moved)
                    last[at][which] = turned
                if u > 0:
                    where = pl.ds(pl.multiple_of((index * len(spins) + at) * PARTNERS * EDGE, 16), PARTNERS * EDGE)
                    front = jnp.concatenate(values[0::2], axis=0)
                    behind = jnp.concatenate(values[1::2], axis=0)
                    x_ref[where, (u - 1) * LANES:u * LANES] = (front + behind).astype(BF)
                    x_ref[where, FWIDE + (u - 1) * LANES:FWIDE + u * LANES] = (front - behind).astype(BF)
        return 0

    lax.fori_loop(0, held, dense, 0)

    cubes = held * len(spins) * PARTNERS
    diag = diag_ref[...]
    for first in range(0, 2 * FWIDE, NCHUNK):
        cols = slice(first, first + NCHUNK)
        y_ref[:, cols] = jnp.dot(diag, x_ref[:, cols], preferred_element_type=F32).astype(BF)

    def forward(first, size):
        for part in range(2):
            z = jnp.dot(y_ref[:, part * FWIDE:(part + 1) * FWIDE], to_ref[part, :, pl.ds(first, size)],
                        preferred_element_type=F32)
            cols = pl.ds(pl.multiple_of(part * FWIDE + first, LANES), size)
            z = z.reshape(cubes, EDGE, size) * inv_ref[:, cols][None]
            x_ref[:, cols] = z.reshape(cubes * EDGE, size).astype(BF)

    def backward(first, size):
        even, odd = [jnp.dot(x_ref[:, part * FWIDE:(part + 1) * FWIDE], from_ref[part, :, pl.ds(first, size)],
                             preferred_element_type=F32) for part in range(2)]
        y_ref[:, pl.ds(first, size)] = (even + odd).astype(BF)
        y_ref[:, pl.ds(pl.multiple_of(FWIDE + first, LANES), size)] = (even - odd).astype(BF)

    for step in (forward, backward):
        whole_steps = FWIDE // NCHUNK

        def looped(n, _):
            step(pl.multiple_of(n * NCHUNK, NCHUNK), NCHUNK)
            return 0

        lax.fori_loop(0, whole_steps, looped, 0)
        if FWIDE % NCHUNK:
            step(whole_steps * NCHUNK, FWIDE % NCHUNK)

    for first in range(0, 2 * FTILES, 2):
        potential = jnp.dot(diag, y_ref[:, first * LANES:(first + 2) * LANES], preferred_element_type=F32)
        for u in (first, first + 1):
            side = slice((u - first) * LANES, (u - first + 1) * LANES)
            for index in range(held):
                for at in range(len(spins)):
                    total = 0.0
                    for number in range(PARTNERS):
                        row = ((index * len(spins) + at) * PARTNERS + number) * EDGE
                        total = total + potential[row:row + EDGE, side] * mov_ref[index, at, number, u // FTILES, u % FTILES]
                    if u < FTILES:
                        res_ref[index * len(spins) + at, u] = total
                    else:
                        half_ref[index * len(spins) + at, u - FTILES] = total

    def unfold(row, _):
        middle = FTILES - 1

        def store(u, x):
            if u == middle:
                x = jnp.where(lanes < FOLD - middle * LANES, res_ref[row, middle], x)
            res_ref[row, u] = x

        reverse_slabs(lambda v: half_ref[row, v], store, middle, FTILES)
        return 0

    lax.fori_loop(0, held * len(spins), unfold, 0)

    if final:
        for index in range(held):
            home = tab_ref[homes + start + index]
            for at in range(len(spins)):
                slabs_to_flat(
                    lambda u, parity: res_ref[index * len(spins) + at, u, pl.ds(parity, HALF, stride=2), :],
                    lambda t, x: form_ref.__setitem__(
                        (home, pl.ds(2 * t + at, HALF, stride=2 * PAIRT), slice(None)), x),
                )
            copy(home).start()

        def finish(slot, _):
            code = tab_ref[codes + slot]

            @pl.when((code < boxes) | (code >= boxes + AHEAD + BACK))
            def _():
                copy(slot).wait()

            return 0

        lax.fori_loop(0, CAP, finish, 0)
        return

    def flatten(row, _):
        slabs_to_flat(
            lambda u, parity: res_ref[row, u, pl.ds(parity, HALF, stride=2), :],
            lambda t, x: out_ref.__setitem__((row, pl.ds(t, HALF, stride=PAIRT), slice(None)), x),
        )
        return 0

    lax.fori_loop(0, held * len(spins), flatten, 0)
    for k in range(AHEAD):
        sends[0][k] = out_ref[tab_ref[leaves + k]].astype(BF)
    for k in range(BACK):
        sends[1][k] = out_ref[tab_ref[leaves + AHEAD + k]].astype(BF)


def place_kernel(boxes, tab_ref, prev_low, next_low, prev_high, next_high, kept_ref, out_ref, form_ref, sems):
    slots = table_layout(boxes)[2]
    copies = []
    for k in range(AHEAD + BACK):
        pair, row = ((prev_low, prev_high), k) if k < AHEAD else ((next_low, next_high), k - AHEAD)
        slot = tab_ref[slots + k]
        copy = pltpu.make_async_copy(form_ref.at[k], out_ref.at[jnp.minimum(slot, CAP - 1)], sems.at[k])

        @pl.when(slot < CAP)
        def _():
            for spin, ref in enumerate(pair):
                form_ref[k, pl.ds(spin, FLAT, stride=2), :] = ref[row].astype(F32)
            copy.start()

        copies.append((slot, copy))
    for slot, copy in copies:
        @pl.when(slot < CAP)
        def _():
            copy.wait()


def from_behind(value, steps):
    count = lax.axis_size(AXES)
    return lax.ppermute(value, AXES, [(source, (source + steps) % count) for source in range(count)])


def whole(count):
    return [pl.BlockSpec(memory_space=pltpu.VMEM)] * count


SCALARS = pl.BlockSpec(memory_space=pltpu.SMEM)
ANYWHERE = pl.BlockSpec(memory_space=pltpu.MemorySpace.HBM)


def in_place(value):
    return pltpu.with_memory_space_constraint(jnp.asarray(value), pltpu.HBM)


def cost(flops, size):
    return pl.CostEstimate(flops=flops, bytes_accessed=size, transcendentals=0)


def shards(orbitals, dest, partners, anchors):
    boxes = orbitals.shape[1]
    sine, inverse, factors = tables()
    partners_t, anchors_t = partners.T, anchors.T

    box = jax.ShapeDtypeStruct((FLAT, LANES), BF)
    splitter = pltpu.VMEM((FLAT * 8, LANES), F32)
    ahead, back = pl.pallas_call(
        window_kernel,
        out_shape=[box] * 2,
        in_specs=[ANYWHERE] * 2,
        out_specs=whole(2),
        scratch_shapes=[pltpu.SMEM(partners_t.shape, jnp.int32), pltpu.VMEM(orbitals.shape[1:], BF),
                        splitter, pltpu.SemaphoreType.DMA((2,))],
        compiler_params=pltpu.CompilerParams(vmem_limit_bytes=12 << 20),
        name="window",
    )(*map(in_place, (partners_t, orbitals)))
    prev_low = from_behind(ahead, 1)
    next_low = from_behind(back, -1)

    folded = jax.ShapeDtypeStruct((2, FWIDE, FWIDE), BF)

    def build_modes(early, *before):
        return pl.pallas_call(
            lambda *refs: modes_kernel(early, *refs),
            out_shape=[folded] * 2,
            in_specs=[ANYWHERE] + whole(len(before)),
            out_specs=whole(2),
            scratch_shapes=[pltpu.VMEM(factors.shape, F32), pltpu.SemaphoreType.DMA],
            input_output_aliases={1: 0, 2: 1} if before else {},
            compiler_params=pltpu.CompilerParams(vmem_limit_bytes=12 << 20),
            cost_estimate=cost(4_000_000, 4_000_000),
        )(in_place(factors), *before)

    modes = build_modes(True)
    moving = AHEAD + BACK
    slabs = jax.ShapeDtypeStruct((2, boxes + 2, TILES, ROWS, LANES), F32)
    diags = [np.kron(np.eye(cubes, dtype=np.float32), sine).astype(jnp.bfloat16)
             for cubes in (moving * PARTNERS, (boxes - moving) * 2 * PARTNERS)]
    handed = (inverse, *diags)
    second = pl.pallas_call(
        second_kernel,
        out_shape=[jax.ShapeDtypeStruct(orbitals.shape, BF), box, box,
                   jax.ShapeDtypeStruct((table_layout(boxes)[-1],), jnp.int32)]
        + [jax.ShapeDtypeStruct(value.shape, value.dtype) for value in handed],
        in_specs=[ANYWHERE] * 7,
        out_specs=whole(3) + [SCALARS] + whole(3),
        scratch_shapes=[pltpu.SMEM(dest.shape, jnp.int32), pltpu.SMEM(partners_t.shape, jnp.int32),
                        pltpu.SMEM(anchors_t.shape, jnp.int32), splitter, pltpu.SemaphoreType.DMA((8,))],
        compiler_params=pltpu.CompilerParams(vmem_limit_bytes=12 << 20),
        cost_estimate=cost(1_000_000, 2_000_000),
        name="second",
    )
    held, ahead, back, table, inverse, *diags = second(
        *map(in_place, (dest, partners_t, anchors_t, orbitals, *handed)))
    prev_high = from_behind(ahead, 1)
    next_high = from_behind(back, -1)
    to_modes, from_modes = build_modes(False, *modes)

    def build_slabs(spin, near, *before):
        return pl.pallas_call(
            lambda *refs: slabs_kernel(spin, near, *refs),
            out_shape=slabs,
            in_specs=whole(1 + len(before)),
            out_specs=pl.BlockSpec(memory_space=pltpu.VMEM),
            scratch_shapes=[splitter],
            input_output_aliases={1: 0} if before else {},
            compiler_params=pltpu.CompilerParams(vmem_limit_bytes=12 << 20),
            cost_estimate=cost(2_000_000, 4_000_000),
        )(held, *before)

    pads = [build_slabs(0, True, build_slabs(0, False)), build_slabs(1, False, build_slabs(1, True))]
    for spin, halo in enumerate(((prev_low, next_low), (prev_high, next_high))):
        pads[spin] = pl.pallas_call(
            fill_kernel,
            out_shape=slabs,
            in_specs=whole(3),
            out_specs=pl.BlockSpec(memory_space=pltpu.VMEM),
            scratch_shapes=[pltpu.VMEM((FLAT, LANES), F32)],
            input_output_aliases={0: 0},
            compiler_params=pltpu.CompilerParams(vmem_limit_bytes=12 << 20),
            cost_estimate=cost(1_000_000, 2_000_000),
        )(pads[spin], *halo)

    shape = jax.ShapeDtypeStruct((CAP, 2 * FLAT, LANES), F32)

    def solve(start, held, spins, terms=None):
        cubes = held * len(spins) * PARTNERS
        final = terms is not None
        if final:
            shapes, specs = [shape], [ANYWHERE]
            extra = [pltpu.VMEM(shape.shape, F32), pltpu.SemaphoreType.DMA((CAP,))]
        else:
            shapes = [jax.ShapeDtypeStruct((held * len(spins), FLAT, LANES), F32)]
            shapes += [jax.ShapeDtypeStruct((count, FLAT, LANES), BF) for count in (AHEAD, BACK)]
            specs, extra = whole(3), []
        operands = [table, to_modes, from_modes, diags[final], inverse] + [pads[spin] for spin in spins] + (terms or [])
        return pl.pallas_call(
            lambda *refs: pair_kernel(start, held, spins, final, *refs),
            out_shape=shapes,
            in_specs=[SCALARS] + whole(len(operands) - 1),
            out_specs=specs,
            scratch_shapes=extra + [
                pltpu.VMEM((held, len(spins), PARTNERS, 2, FTILES, EDGE, LANES), F32),
                pltpu.VMEM((cubes * EDGE, 2 * FWIDE), BF),
                pltpu.VMEM((cubes * EDGE, 2 * FWIDE), BF),
                pltpu.VMEM((held * len(spins), FTILES, EDGE, LANES), F32),
                pltpu.VMEM((held * len(spins), TILES, EDGE, LANES), F32),
            ],
            compiler_params=pltpu.CompilerParams(vmem_limit_bytes=20 << 20),
            cost_estimate=cost(2 * cubes * EDGE * FACE * FACE, 10_000_000),
        )(*operands)

    terms, arrived = [], []
    for spin in range(2):
        mine, sent_ahead, sent_back = solve(0, moving, (spin,))
        terms.append(mine)
        ahead = from_behind(sent_ahead, 1)
        back = from_behind(sent_back, -1)
        arrived += [ahead, back]
    kept, = solve(moving, boxes - moving, (0, 1), terms)
    placed = pl.pallas_call(
        lambda *refs: place_kernel(boxes, *refs),
        out_shape=shape,
        in_specs=[SCALARS] + whole(4) + [ANYWHERE],
        out_specs=ANYWHERE,
        scratch_shapes=[pltpu.VMEM((AHEAD + BACK, 2 * FLAT, LANES), F32),
                        pltpu.SemaphoreType.DMA((AHEAD + BACK,))],
        input_output_aliases={5: 0},
        compiler_params=pltpu.CompilerParams(vmem_limit_bytes=8 << 20),
        cost_estimate=cost(1_000_000, 4_000_000),
        name="place",
    )(table, *arrived, kept)
    placed = placed.reshape(-1).reshape(CAP, FLAT, 2, LANES).transpose(0, 2, 1, 3)
    return placed.reshape(CAP, 2, FLAT * LANES).transpose(1, 0, 2)


def solution(mesh):
    return jax.shard_map(
        shards,
        mesh=mesh,
        in_specs=(P(None, AXES, None), P(), P(), P()),
        out_specs=P(None, AXES, None),
        check_vma=False,
    )
```

```python
import jax
import jax.numpy as jnp
import numpy as np
from jax import lax
from jax.experimental import pallas as pl
from jax.experimental.pallas import tpu as pltpu
from jax.sharding import PartitionSpec as P


EDGE = 40
PARTNERS = 2
GRID_X = 768
GRID_Y = 384
GRID_Z = 384
BACK = 2
AHEAD = 1
CAP = 7
SCREEN = 0.001

AXES = ("gx", "gy", "gz")
LANES = 128
FACE = EDGE * EDGE
TILES = -(-FACE // LANES)
NCHUNK = 256
FOLD = FACE // 2
FTILES = -(-FOLD // LANES)
FWIDE = FTILES * LANES
CHUNKS = [(min(first, FWIDE - NCHUNK), NCHUNK) for first in range(0, FWIDE, NCHUNK)]
FLAT = EDGE ** 3 // LANES
HALF = EDGE // 2
PAIRT = 2 * FACE // LANES
PAD = 24
ROWS = EDGE + 2 * PAD
ZERO_TILES = 7
BF = jnp.bfloat16
F32 = jnp.float32


def tables():
    counter = np.arange(EDGE) + 1
    turns = np.outer(counter, counter) % (2 * (EDGE + 1))
    sine = (np.sqrt(2.0 / (EDGE + 1.0)) * np.sin(np.pi * turns / (EDGE + 1.0))).astype(np.float32)
    sine = sine.astype(jnp.bfloat16).astype(np.float32)
    flipped = sine[::-1] * np.where(np.arange(EDGE) % 2 == 0, 1.0, -1.0)
    assert np.array_equal(sine, flipped)
    levels = 2.0 - 2.0 * np.cos(np.pi * counter / (EDGE + 1.0))
    number = np.arange(FOLD)
    second, step = number // HALF, number % HALF
    thirds = [2 * step + second % 2, 2 * step + 1 - second % 2]
    inverse = np.zeros((EDGE, 2 * FWIDE), np.float32)
    for part, third in enumerate(thirds):
        lam = levels[:, None] + levels[second] + levels[third] + SCREEN
        inverse[:, part * FWIDE:part * FWIDE + FOLD] = 1.0 / lam
    factors = np.zeros((6, EDGE, FWIDE), np.float32)
    factors[0, :HALF, :FOLD] = sine[:HALF][:, second]
    for part, third in enumerate(thirds):
        factors[1 + part, :, :FOLD] = sine[:, third]
    factors[3, :, :FOLD] = np.repeat(sine[:HALF], EDGE, axis=0).T
    lines = np.tile(sine, (HALF, 1)).T
    factors[4, :, :FOLD] = np.concatenate([lines[0::2], lines[1::2]])
    factors[5, :, :FOLD] = np.concatenate([lines[1::2], lines[0::2]])
    return sine, inverse, factors


def lane_iota():
    return lax.broadcasted_iota(jnp.int32, (1, LANES), 1)


def split_boxes(orb_ref, flat_ref, boxes):
    def step(i, _):
        base = pl.multiple_of(i * PAIRT * LANES, LANES)
        x = orb_ref[:, pl.ds(base, PAIRT * LANES)].astype(F32)
        for j in range(PAIRT):
            flat_ref[pl.ds(pl.multiple_of((i * PAIRT + j) * 8, 8), boxes), :] = x[:, j * LANES:(j + 1) * LANES]
        return 0

    lax.fori_loop(0, HALF, step, 0)


def flat_to_slabs(load, store):
    low = lane_iota() < LANES // 2
    rolled = None
    for t in range(PAIRT):
        x = load(t)
        if t < TILES:
            store(t, 0, x)
        if t >= TILES - 1:
            turned = pltpu.roll(x, LANES // 2, 1)
            if rolled is not None:
                store(t - TILES, 1, jnp.where(low, rolled, turned))
            rolled = turned
    store(TILES - 1, 1, rolled)


def turn(x):
    source = (LANES // 2 - 1 - lax.broadcasted_iota(jnp.int32, x.shape, 1)) & (LANES - 1)
    return jnp.take_along_axis(x, source, axis=1)


def reverse_slabs(load, store, first, count):
    low = lane_iota() < LANES // 2
    turned = [turn(load(v)) for v in range(count)]
    for u in range(first, TILES):
        v = TILES - 1 - u
        store(u, jnp.where(low, turned[v], turned[v - 1]) if v > 0 else turned[v])


def slabs_to_flat(load, store):
    low = lane_iota() < LANES // 2
    for t in range(TILES - 1):
        store(t, load(t, 0))
    before = load(TILES - 1, 0)
    for v in range(TILES):
        turned = pltpu.roll(load(v, 1), LANES // 2, 1)
        store(TILES - 1 + v, jnp.where(low, before, turned))
        before = turned


def wanted_boxes(part_ref, boxes):
    total = part_ref.shape[1]
    device = lax.axis_index(AXES)
    wanted = []
    for step in (1, -1):
        found = jnp.int32(0)
        for k in range(boxes):
            other = (device + step) * boxes + k
            inside = (other >= 0) & (other < total)
            for number in range(PARTNERS):
                local = part_ref[number, jnp.clip(other, 0, total - 1)] - device * boxes
                found = jnp.where(inside & (local >= 0) & (local < boxes), local, found)
        wanted.append(found)
    return wanted


def window_kernel(part_hbm, orb_hbm, ahead_ref, back_ref, orb_ref, part_ref, flat_ref, sems):
    boxes = orb_ref.shape[1]
    small = pltpu.make_async_copy(part_hbm, part_ref, sems.at[0])
    large = [pltpu.make_async_copy(orb_hbm.at[spin], orb_ref.at[spin], sems.at[1 + spin]) for spin in range(2)]
    small.start()
    for copy in large:
        copy.start()
    small.wait()
    wanted = wanted_boxes(part_ref, boxes)
    large[0].wait()
    split_boxes(orb_ref.at[0], flat_ref, boxes)
    for side, ref in enumerate((ahead_ref, back_ref)):
        ref[...] = flat_ref[pl.ds(wanted[side], FLAT, stride=8), :].astype(BF)
    large[1].wait()


def table_layout(boxes):
    pairs = 0
    codes = pairs + boxes * PARTNERS * 4
    slots = codes + CAP + 1
    leaves = slots + AHEAD + BACK + 1
    order = leaves + AHEAD + BACK + 1
    homes = order + boxes
    return pairs, codes, slots, leaves, order, homes, homes + boxes + 1


def build_tables(dest_ref, part_ref, anc_ref, tab_ref, boxes):
    total = part_ref.shape[1]
    device = lax.axis_index(AXES)
    pairs, codes, slots, leaves, order, homes, _ = table_layout(boxes)
    one, none = jnp.int32(1), jnp.int32(0)
    for k in range(CAP + 1):
        tab_ref[codes + k] = boxes + AHEAD + BACK
    for k in range(boxes + 1):
        tab_ref[homes + k] = 0
    for k in range(AHEAD + BACK + 1):
        tab_ref[slots + k] = CAP
        tab_ref[leaves + k] = 0
    goes = [dest_ref[device * boxes + k] for k in range(boxes)]
    ahead_all, back_all = none, none
    for k in range(boxes):
        ahead_all = ahead_all + jnp.where(goes[k] == device + 1, one, none)
        back_all = back_all + jnp.where(goes[k] == device - 1, one, none)
    ahead, back, stay = none, none, none
    spots = []
    for k in range(boxes):
        is_ahead, is_back = goes[k] == device + 1, goes[k] == device - 1
        spot = jnp.where(is_ahead, ahead, jnp.where(is_back, ahead_all + back, ahead_all + back_all + stay))
        spots.append(spot)
        tab_ref[order + spot] = k
        spare = leaves + AHEAD + BACK
        tab_ref[jnp.where(is_ahead, leaves + jnp.minimum(ahead, AHEAD - 1), spare)] = spot
        tab_ref[jnp.where(is_back, leaves + AHEAD + jnp.minimum(back, BACK - 1), spare)] = spot
        ahead = ahead + jnp.where(is_ahead, one, none)
        back = back + jnp.where(is_back, one, none)
        stay = stay + jnp.where(is_ahead | is_back, none, one)
    count = none
    for block in range(3):
        arrived = none
        for k in range(boxes):
            box = (device + (block - 1)) * boxes + k
            hit = (box >= 0) & (box < total) & (dest_ref[jnp.clip(box, 0, total - 1)] == device)
            if block == 1:
                code = spots[k]
                tab_ref[jnp.where(hit, homes + code, homes + boxes)] = jnp.minimum(count, CAP - 1)
            else:
                first, most = (0, AHEAD) if block == 0 else (AHEAD, BACK)
                where = first + jnp.minimum(arrived, most - 1)
                code = boxes + where
                tab_ref[jnp.where(hit, slots + where, slots + AHEAD + BACK)] = count
                arrived = arrived + jnp.where(hit, one, none)
            tab_ref[jnp.where(hit, codes + jnp.minimum(count, CAP - 1), codes + CAP)] = code
            count = count + jnp.where(hit, one, none)
    for box in range(boxes):
        me = device * boxes + box
        for number in range(PARTNERS):
            other = part_ref[number, me]
            local = other - device * boxes
            base = pairs + (box * PARTNERS + number) * 4
            tab_ref[base] = jnp.where(local < 0, boxes, jnp.where(local >= boxes, boxes + 1, local))
            for axis, extent in enumerate((GRID_X, GRID_Y, GRID_Z)):
                moved = anc_ref[axis, other] - anc_ref[axis, me] + extent // 2
                moved = jnp.where(moved < 0, moved + extent, jnp.where(moved >= extent, moved - extent, moved))
                tab_ref[base + 1 + axis] = jnp.clip(moved - extent // 2, -(PAD - 4), PAD - 4)


def reverse_box(pad_ref, box):
    body = pl.ds(PAD, EDGE)
    reverse_slabs(lambda v: pad_ref[0, box, v, body, :],
                  lambda u, x: pad_ref.__setitem__((1, box, u, body, slice(None)), x), 0, TILES)


def second_kernel(dest_hbm, part_hbm, anc_hbm, inv_hbm, diag_hbm, rest_hbm, orb_ref,
                  ahead_ref, back_ref, tab_ref, inv_ref, diag_ref, rest_ref,
                  dest_ref, part_ref, anc_ref, flat_ref, sems):
    boxes = orb_ref.shape[1]
    pieces = [(part_hbm, part_ref), (dest_hbm, dest_ref), (anc_hbm, anc_ref)]
    pieces += [(inv_hbm, inv_ref), (diag_hbm, diag_ref), (rest_hbm, rest_ref)]
    copies = [pltpu.make_async_copy(source, target, sems.at[k]) for k, (source, target) in enumerate(pieces)]
    for copy in copies:
        copy.start()
    split_boxes(orb_ref.at[1], flat_ref, boxes)
    for copy in copies[:3]:
        copy.wait()
    wanted = wanted_boxes(part_ref, boxes)
    for side, ref in enumerate((ahead_ref, back_ref)):
        ref[...] = flat_ref[pl.ds(wanted[side], FLAT, stride=8), :].astype(BF)
    build_tables(dest_ref, part_ref, anc_ref, tab_ref, boxes)
    for copy in copies[3:]:
        copy.wait()


def low_half():
    return 2 * lax.axis_index(AXES[-1]) < lax.axis_size(AXES[-1])


def slabs_kernel(spin, near, orb_ref, *refs):
    pad_ref, flat_ref = refs[-2:]
    boxes = orb_ref.shape[1]

    @pl.when(low_half() if near else jnp.logical_not(low_half()))
    def _():
        split_boxes(orb_ref.at[spin], flat_ref, boxes)

        def slabs(box, _):
            flat_to_slabs(
                lambda t: flat_ref[pl.ds(box + 8 * t, HALF, stride=8 * PAIRT), :],
                lambda u, parity, x: pad_ref.__setitem__(
                    (0, box, u, pl.ds(PAD + parity, HALF, stride=2), slice(None)), x),
            )
            reverse_box(pad_ref, box)
            return 0

        lax.fori_loop(0, boxes, slabs, 0)


def modes_kernel(early, fac_hbm, *refs):
    to_ref, from_ref, fac_ref, sem = refs[-4:]

    @pl.when(low_half() if early else jnp.logical_not(low_half()))
    def _():
        copy = pltpu.make_async_copy(fac_hbm, fac_ref, sem)
        copy.start()
        for part in range(2):
            to_ref[part, FOLD:, :] = jnp.zeros((FWIDE - FOLD, FWIDE), BF)
            from_ref[part, FOLD:, :] = jnp.zeros((FWIDE - FOLD, FWIDE), BF)
        front = lax.broadcasted_iota(jnp.int32, (EDGE, 1), 0) < HALF
        copy.wait()

        def build(i, _):
            where = pl.ds(pl.multiple_of(i * 2 * EDGE, 16), 2 * EDGE)
            for start, size in CHUNKS:
                cols = slice(start, start + size)
                line = [fac_ref[0, pl.ds(2 * i + k, 1), cols] for k in range(2)]
                mode = [fac_ref[3, pl.ds(4 * i + k, 1), cols] for k in range(4)]
                modes = [jnp.where(front, mode[2 * k], mode[2 * k + 1]) for k in range(2)]
                for part in range(2):
                    right = fac_ref[1 + part, :, cols]
                    to_ref[part, where, cols] = jnp.concatenate([x * right for x in line], axis=0).astype(BF)
                    right = fac_ref[4 + part, :, cols]
                    from_ref[part, where, cols] = jnp.concatenate([x * right for x in modes], axis=0).astype(BF)
            return 0

        lax.fori_loop(0, HALF // 2, build, 0)


def fill_kernel(old_ref, prev_ref, next_ref, pad_ref, flat_ref):
    boxes = pad_ref.shape[1] - 2
    for side, ref in ((0, prev_ref), (1, next_ref)):
        flat_ref[...] = ref[...].astype(F32)
        flat_to_slabs(
            lambda t: flat_ref[pl.ds(t, HALF, stride=PAIRT), :],
            lambda u, parity, x: pad_ref.__setitem__(
                (0, boxes + side, u, pl.ds(PAD + parity, HALF, stride=2), slice(None)), x),
        )
        reverse_box(pad_ref, boxes + side)


def pair_kernel(start, held, spins, final, tab_ref, to_ref, from_ref, diag_ref, inv_ref, *refs):
    pads, (mov_ref, x_ref, y_ref, half_ref, res_ref) = refs[:len(spins)], refs[-5:]
    boxes = pads[0].shape[1] - 2
    pairs, codes, _, leaves, order, homes, _ = table_layout(boxes)
    if final:
        low_ref, high_ref, out_ref, form_ref, sems = refs[len(spins):-5]

        def copy(slot):
            return pltpu.make_async_copy(form_ref.at[slot], out_ref.at[slot], sems.at[slot])

        def early(slot, _):
            code = tab_ref[codes + slot]

            @pl.when(code < start)
            def _():
                spot = jnp.minimum(code, start - 1)
                for spin, ref in enumerate((low_ref, high_ref)):
                    form_ref[slot, pl.ds(spin, FLAT, stride=2), :] = ref[spot]
                copy(slot).start()

            @pl.when(code >= boxes + AHEAD + BACK)
            def _():
                form_ref[slot] = jnp.zeros(form_ref.shape[1:], F32)
                copy(slot).start()

            return 0

        lax.fori_loop(0, CAP, early, 0)
    else:
        out_ref, sends = refs[len(spins)], refs[len(spins) + 1:-5]
    lanes = lane_iota()
    rows = lax.broadcasted_iota(jnp.int32, (EDGE, 1), 0)

    def dense(index, _):
        box = tab_ref[order + start + index]
        places = []
        for number in range(PARTNERS):
            base = pairs + (box * PARTNERS + number) * 4
            source = tab_ref[base]
            da, db, dc = tab_ref[base + 1], tab_ref[base + 2], tab_ref[base + 3]
            row_ok = jnp.abs(2 * (rows - da) - (EDGE - 1)) < EDGE
            for b_by, c_by in ((db, dc), (-db, -dc)):
                offset = ZERO_TILES * LANES - (b_by * EDGE + c_by)
                places.append((source, da, b_by, c_by, offset // LANES, offset % LANES, row_ok))
        last = [[None] * len(places) for _ in spins]
        for u in range(FTILES + 1):
            keep = []
            for source, da, b_by, c_by, quotient, rest, row_ok in places:
                if u > 0:
                    cell = lanes + (u - 1) * LANES
                    b = (cell * 52429) >> 21
                    c = cell - b * EDGE
                    ok = (jnp.abs(2 * (b - b_by) - (EDGE - 1)) < EDGE) & (jnp.abs(2 * (c - c_by) - (EDGE - 1)) < EDGE)
                    if u == FTILES:
                        ok = ok & (lanes < FOLD - (FTILES - 1) * LANES)
                    keep.append(row_ok & ok)
            for at, pad_ref in enumerate(pads):
                values = []
                for which, (source, da, b_by, c_by, quotient, rest, row_ok) in enumerate(places):
                    part = which % 2
                    tile = jnp.clip(quotient + (u - ZERO_TILES), 0, TILES - 1)
                    x = pad_ref[part, source, tile, pl.ds(PAD - da, EDGE), :]
                    turned = pltpu.roll(x, (LANES - rest) % LANES, 1)
                    if u > 0:
                        moved = jnp.where(keep[which], jnp.where(lanes < LANES - rest, last[at][which], turned), 0.0)
                        mov_ref[index, at, which // 2, part, u - 1] = moved
                        values.append(pad_ref[part, box, u - 1, pl.ds(PAD, EDGE), :] * moved)
                    last[at][which] = turned
                if u > 0:
                    where = pl.ds(pl.multiple_of((index * len(spins) + at) * PARTNERS * EDGE, 16), PARTNERS * EDGE)
                    front = jnp.concatenate(values[0::2], axis=0)
                    behind = jnp.concatenate(values[1::2], axis=0)
                    x_ref[where, (u - 1) * LANES:u * LANES] = (front + behind).astype(BF)
                    x_ref[where, FWIDE + (u - 1) * LANES:FWIDE + u * LANES] = (front - behind).astype(BF)
        return 0

    lax.fori_loop(0, held, dense, 0)

    cubes = held * len(spins) * PARTNERS
    diag = diag_ref[...]
    for first in range(0, 2 * FWIDE, NCHUNK):
        cols = slice(first, first + NCHUNK)
        y_ref[:, cols] = jnp.dot(diag, x_ref[:, cols], preferred_element_type=F32).astype(BF)

    def forward(first, size):
        for part in range(2):
            z = jnp.dot(y_ref[:, part * FWIDE:(part + 1) * FWIDE], to_ref[part, :, pl.ds(first, size)],
                        preferred_element_type=F32)
            cols = pl.ds(pl.multiple_of(part * FWIDE + first, LANES), size)
            z = z.reshape(cubes, EDGE, size) * inv_ref[:, cols][None]
            x_ref[:, cols] = z.reshape(cubes * EDGE, size).astype(BF)

    def backward(first, size):
        even, odd = [jnp.dot(x_ref[:, part * FWIDE:(part + 1) * FWIDE], from_ref[part, :, pl.ds(first, size)],
                             preferred_element_type=F32) for part in range(2)]
        y_ref[:, pl.ds(first, size)] = (even + odd).astype(BF)
        y_ref[:, pl.ds(pl.multiple_of(FWIDE + first, LANES), size)] = (even - odd).astype(BF)

    for step in (forward, backward):
        whole_steps = FWIDE // NCHUNK

        def looped(n, _):
            step(pl.multiple_of(n * NCHUNK, NCHUNK), NCHUNK)
            return 0

        lax.fori_loop(0, whole_steps, looped, 0)
        if FWIDE % NCHUNK:
            step(whole_steps * NCHUNK, FWIDE % NCHUNK)

    for first in range(0, 2 * FTILES, 2):
        potential = jnp.dot(diag, y_ref[:, first * LANES:(first + 2) * LANES], preferred_element_type=F32)
        for u in (first, first + 1):
            side = slice((u - first) * LANES, (u - first + 1) * LANES)
            for index in range(held):
                for at in range(len(spins)):
                    total = 0.0
                    for number in range(PARTNERS):
                        row = ((index * len(spins) + at) * PARTNERS + number) * EDGE
                        total = total + potential[row:row + EDGE, side] * mov_ref[index, at, number, u // FTILES, u % FTILES]
                    if u < FTILES:
                        res_ref[index * len(spins) + at, u] = total
                    else:
                        half_ref[index * len(spins) + at, u - FTILES] = total

    def unfold(row, _):
        middle = FTILES - 1

        def store(u, x):
            if u == middle:
                x = jnp.where(lanes < FOLD - middle * LANES, res_ref[row, middle], x)
            res_ref[row, u] = x

        reverse_slabs(lambda v: half_ref[row, v], store, middle, FTILES)
        return 0

    lax.fori_loop(0, held * len(spins), unfold, 0)

    if final:
        for index in range(held):
            home = tab_ref[homes + start + index]
            for at in range(len(spins)):
                slabs_to_flat(
                    lambda u, parity: res_ref[index * len(spins) + at, u, pl.ds(parity, HALF, stride=2), :],
                    lambda t, x: form_ref.__setitem__(
                        (home, pl.ds(2 * t + at, HALF, stride=2 * PAIRT), slice(None)), x),
                )
            copy(home).start()

        def finish(slot, _):
            code = tab_ref[codes + slot]

            @pl.when((code < boxes) | (code >= boxes + AHEAD + BACK))
            def _():
                copy(slot).wait()

            return 0

        lax.fori_loop(0, CAP, finish, 0)
        return

    def flatten(row, _):
        slabs_to_flat(
            lambda u, parity: res_ref[row, u, pl.ds(parity, HALF, stride=2), :],
            lambda t, x: out_ref.__setitem__((row, pl.ds(t, HALF, stride=PAIRT), slice(None)), x),
        )
        return 0

    lax.fori_loop(0, held * len(spins), flatten, 0)
    for k in range(AHEAD):
        sends[0][k] = out_ref[tab_ref[leaves + k]].astype(BF)
    for k in range(BACK):
        sends[1][k] = out_ref[tab_ref[leaves + AHEAD + k]].astype(BF)


def place_kernel(boxes, tab_ref, prev_low, next_low, prev_high, next_high, kept_ref, out_ref, form_ref, sems):
    slots = table_layout(boxes)[2]
    copies = []
    for k in range(AHEAD + BACK):
        pair, row = ((prev_low, prev_high), k) if k < AHEAD else ((next_low, next_high), k - AHEAD)
        slot = tab_ref[slots + k]
        copy = pltpu.make_async_copy(form_ref.at[k], out_ref.at[jnp.minimum(slot, CAP - 1)], sems.at[k])

        @pl.when(slot < CAP)
        def _():
            for spin, ref in enumerate(pair):
                form_ref[k, pl.ds(spin, FLAT, stride=2), :] = ref[row].astype(F32)
            copy.start()

        copies.append((slot, copy))
    for slot, copy in copies:
        @pl.when(slot < CAP)
        def _():
            copy.wait()


def from_behind(value, steps):
    count = lax.axis_size(AXES)
    return lax.ppermute(value, AXES, [(source, (source + steps) % count) for source in range(count)])


def whole(count):
    return [pl.BlockSpec(memory_space=pltpu.VMEM)] * count


SCALARS = pl.BlockSpec(memory_space=pltpu.SMEM)
ANYWHERE = pl.BlockSpec(memory_space=pltpu.MemorySpace.HBM)


def in_place(value):
    return pltpu.with_memory_space_constraint(jnp.asarray(value), pltpu.HBM)


def cost(flops, size):
    return pl.CostEstimate(flops=flops, bytes_accessed=size, transcendentals=0)


def shards(orbitals, dest, partners, anchors):
    boxes = orbitals.shape[1]
    sine, inverse, factors = tables()
    partners_t, anchors_t = partners.T, anchors.T

    box = jax.ShapeDtypeStruct((FLAT, LANES), BF)
    splitter = pltpu.VMEM((FLAT * 8, LANES), F32)
    ahead, back, held = pl.pallas_call(
        window_kernel,
        out_shape=[box] * 2 + [jax.ShapeDtypeStruct(orbitals.shape, BF)],
        in_specs=[ANYWHERE] * 2,
        out_specs=whole(3),
        scratch_shapes=[pltpu.SMEM(partners_t.shape, jnp.int32), splitter, pltpu.SemaphoreType.DMA((3,))],
        compiler_params=pltpu.CompilerParams(vmem_limit_bytes=12 << 20),
        name="window",
    )(*map(in_place, (partners_t, orbitals)))
    prev_low = from_behind(ahead, 1)
    next_low = from_behind(back, -1)

    folded = jax.ShapeDtypeStruct((2, FWIDE, FWIDE), BF)

    def build_modes(early, *before):
        return pl.pallas_call(
            lambda *refs: modes_kernel(early, *refs),
            out_shape=[folded] * 2,
            in_specs=[ANYWHERE] + whole(len(before)),
            out_specs=whole(2),
            scratch_shapes=[pltpu.VMEM(factors.shape, F32), pltpu.SemaphoreType.DMA],
            input_output_aliases={1: 0, 2: 1} if before else {},
            compiler_params=pltpu.CompilerParams(vmem_limit_bytes=12 << 20),
            cost_estimate=cost(4_000_000, 4_000_000),
        )(in_place(factors), *before)

    modes = build_modes(True)
    moving = AHEAD + BACK
    slabs = jax.ShapeDtypeStruct((2, boxes + 2, TILES, ROWS, LANES), F32)
    diags = [np.kron(np.eye(cubes, dtype=np.float32), sine).astype(jnp.bfloat16)
             for cubes in (moving * PARTNERS, (boxes - moving) * 2 * PARTNERS)]
    handed = (inverse, *diags)
    second = pl.pallas_call(
        second_kernel,
        out_shape=[box, box, jax.ShapeDtypeStruct((table_layout(boxes)[-1],), jnp.int32)]
        + [jax.ShapeDtypeStruct(value.shape, value.dtype) for value in handed],
        in_specs=[ANYWHERE] * 6 + whole(1),
        out_specs=whole(2) + [SCALARS] + whole(3),
        scratch_shapes=[pltpu.SMEM(dest.shape, jnp.int32), pltpu.SMEM(partners_t.shape, jnp.int32),
                        pltpu.SMEM(anchors_t.shape, jnp.int32), splitter, pltpu.SemaphoreType.DMA((6,))],
        compiler_params=pltpu.CompilerParams(vmem_limit_bytes=12 << 20),
        cost_estimate=cost(1_000_000, 2_000_000),
        name="second",
    )
    ahead, back, table, inverse, *diags = second(
        *map(in_place, (dest, partners_t, anchors_t, *handed)), held)
    prev_high = from_behind(ahead, 1)
    next_high = from_behind(back, -1)
    to_modes, from_modes = build_modes(False, *modes)

    def build_slabs(spin, near, *before):
        return pl.pallas_call(
            lambda *refs: slabs_kernel(spin, near, *refs),
            out_shape=slabs,
            in_specs=whole(1 + len(before)),
            out_specs=pl.BlockSpec(memory_space=pltpu.VMEM),
            scratch_shapes=[splitter],
            input_output_aliases={1: 0} if before else {},
            compiler_params=pltpu.CompilerParams(vmem_limit_bytes=12 << 20),
            cost_estimate=cost(2_000_000, 4_000_000),
        )(held, *before)

    pads = [build_slabs(0, True, build_slabs(0, False)), build_slabs(1, False, build_slabs(1, True))]
    for spin, halo in enumerate(((prev_low, next_low), (prev_high, next_high))):
        pads[spin] = pl.pallas_call(
            fill_kernel,
            out_shape=slabs,
            in_specs=whole(3),
            out_specs=pl.BlockSpec(memory_space=pltpu.VMEM),
            scratch_shapes=[pltpu.VMEM((FLAT, LANES), F32)],
            input_output_aliases={0: 0},
            compiler_params=pltpu.CompilerParams(vmem_limit_bytes=12 << 20),
            cost_estimate=cost(1_000_000, 2_000_000),
        )(pads[spin], *halo)

    shape = jax.ShapeDtypeStruct((CAP, 2 * FLAT, LANES), F32)

    def solve(start, held, spins, terms=None):
        cubes = held * len(spins) * PARTNERS
        final = terms is not None
        if final:
            shapes, specs = [shape], [ANYWHERE]
            extra = [pltpu.VMEM(shape.shape, F32), pltpu.SemaphoreType.DMA((CAP,))]
        else:
            shapes = [jax.ShapeDtypeStruct((held * len(spins), FLAT, LANES), F32)]
            shapes += [jax.ShapeDtypeStruct((count, FLAT, LANES), BF) for count in (AHEAD, BACK)]
            specs, extra = whole(3), []
        operands = [table, to_modes, from_modes, diags[final], inverse] + [pads[spin] for spin in spins] + (terms or [])
        return pl.pallas_call(
            lambda *refs: pair_kernel(start, held, spins, final, *refs),
            out_shape=shapes,
            in_specs=[SCALARS] + whole(len(operands) - 1),
            out_specs=specs,
            scratch_shapes=extra + [
                pltpu.VMEM((held, len(spins), PARTNERS, 2, FTILES, EDGE, LANES), F32),
                pltpu.VMEM((cubes * EDGE, 2 * FWIDE), BF),
                pltpu.VMEM((cubes * EDGE, 2 * FWIDE), BF),
                pltpu.VMEM((held * len(spins), FTILES, EDGE, LANES), F32),
                pltpu.VMEM((held * len(spins), TILES, EDGE, LANES), F32),
            ],
            compiler_params=pltpu.CompilerParams(vmem_limit_bytes=20 << 20),
            cost_estimate=cost(2 * cubes * EDGE * FACE * FACE, 10_000_000),
        )(*operands)

    terms, arrived = [], []
    for spin in range(2):
        mine, sent_ahead, sent_back = solve(0, moving, (spin,))
        terms.append(mine)
        ahead = from_behind(sent_ahead, 1)
        back = from_behind(sent_back, -1)
        arrived += [ahead, back]
    kept, = solve(moving, boxes - moving, (0, 1), terms)
    placed = pl.pallas_call(
        lambda *refs: place_kernel(boxes, *refs),
        out_shape=shape,
        in_specs=[SCALARS] + whole(4) + [ANYWHERE],
        out_specs=ANYWHERE,
        scratch_shapes=[pltpu.VMEM((AHEAD + BACK, 2 * FLAT, LANES), F32),
                        pltpu.SemaphoreType.DMA((AHEAD + BACK,))],
        input_output_aliases={5: 0},
        compiler_params=pltpu.CompilerParams(vmem_limit_bytes=8 << 20),
        cost_estimate=cost(1_000_000, 4_000_000),
        name="place",
    )(table, *arrived, kept)
    placed = placed.reshape(-1).reshape(CAP, FLAT, 2, LANES).transpose(0, 2, 1, 3)
    return placed.reshape(CAP, 2, FLAT * LANES).transpose(1, 0, 2)


def solution(mesh):
    return jax.shard_map(
        shards,
        mesh=mesh,
        in_specs=(P(None, AXES, None), P(), P(), P()),
        out_specs=P(None, AXES, None),
        check_vma=False,
    )
```

```python
import jax
import jax.numpy as jnp
import numpy as np
from jax import lax
from jax.experimental import pallas as pl
from jax.experimental.pallas import tpu as pltpu
from jax.sharding import PartitionSpec as P


EDGE = 40
PARTNERS = 2
GRID_X = 768
GRID_Y = 384
GRID_Z = 384
BACK = 2
AHEAD = 1
CAP = 7
SCREEN = 0.001

AXES = ("gx", "gy", "gz")
LANES = 128
FACE = EDGE * EDGE
TILES = -(-FACE // LANES)
NCHUNK = 256
FOLD = FACE // 2
FTILES = -(-FOLD // LANES)
FWIDE = FTILES * LANES
CHUNKS = [(min(first, FWIDE - NCHUNK), NCHUNK) for first in range(0, FWIDE, NCHUNK)]
FLAT = EDGE ** 3 // LANES
HALF = EDGE // 2
PAIRT = 2 * FACE // LANES
PAD = 24
ROWS = EDGE + 2 * PAD
ZERO_TILES = 7
BF = jnp.bfloat16
F32 = jnp.float32


def tables():
    counter = np.arange(EDGE) + 1
    turns = np.outer(counter, counter) % (2 * (EDGE + 1))
    sine = (np.sqrt(2.0 / (EDGE + 1.0)) * np.sin(np.pi * turns / (EDGE + 1.0))).astype(np.float32)
    sine = sine.astype(jnp.bfloat16).astype(np.float32)
    flipped = sine[::-1] * np.where(np.arange(EDGE) % 2 == 0, 1.0, -1.0)
    assert np.array_equal(sine, flipped)
    levels = 2.0 - 2.0 * np.cos(np.pi * counter / (EDGE + 1.0))
    number = np.arange(FOLD)
    second, step = number // HALF, number % HALF
    thirds = [2 * step + second % 2, 2 * step + 1 - second % 2]
    inverse = np.zeros((EDGE, 2 * FWIDE), np.float32)
    for part, third in enumerate(thirds):
        lam = levels[:, None] + levels[second] + levels[third] + SCREEN
        inverse[:, part * FWIDE:part * FWIDE + FOLD] = 1.0 / lam
    factors = np.zeros((6, EDGE, FWIDE), np.float32)
    factors[0, :HALF, :FOLD] = sine[:HALF][:, second]
    for part, third in enumerate(thirds):
        factors[1 + part, :, :FOLD] = sine[:, third]
    factors[3, :, :FOLD] = np.repeat(sine[:HALF], EDGE, axis=0).T
    lines = np.tile(sine, (HALF, 1)).T
    factors[4, :, :FOLD] = np.concatenate([lines[0::2], lines[1::2]])
    factors[5, :, :FOLD] = np.concatenate([lines[1::2], lines[0::2]])
    return sine, inverse, factors


def lane_iota():
    return lax.broadcasted_iota(jnp.int32, (1, LANES), 1)


def split_boxes(orb_ref, flat_ref, boxes):
    def step(i, _):
        base = pl.multiple_of(i * PAIRT * LANES, LANES)
        x = orb_ref[:, pl.ds(base, PAIRT * LANES)].astype(F32)
        for j in range(PAIRT):
            flat_ref[pl.ds(pl.multiple_of((i * PAIRT + j) * 8, 8), boxes), :] = x[:, j * LANES:(j + 1) * LANES]
        return 0

    lax.fori_loop(0, HALF, step, 0)


def flat_to_slabs(load, store):
    low = lane_iota() < LANES // 2
    rolled = None
    for t in range(PAIRT):
        x = load(t)
        if t < TILES:
            store(t, 0, x)
        if t >= TILES - 1:
            turned = pltpu.roll(x, LANES // 2, 1)
            if rolled is not None:
                store(t - TILES, 1, jnp.where(low, rolled, turned))
            rolled = turned
    store(TILES - 1, 1, rolled)


def turn(x):
    source = (LANES // 2 - 1 - lax.broadcasted_iota(jnp.int32, x.shape, 1)) & (LANES - 1)
    return jnp.take_along_axis(x, source, axis=1)


def reverse_slabs(load, store, first, count):
    low = lane_iota() < LANES // 2
    turned = [turn(load(v)) for v in range(count)]
    for u in range(first, TILES):
        v = TILES - 1 - u
        store(u, jnp.where(low, turned[v], turned[v - 1]) if v > 0 else turned[v])


def slabs_to_flat(load, store):
    low = lane_iota() < LANES // 2
    for t in range(TILES - 1):
        store(t, load(t, 0))
    before = load(TILES - 1, 0)
    for v in range(TILES):
        turned = pltpu.roll(load(v, 1), LANES // 2, 1)
        store(TILES - 1 + v, jnp.where(low, before, turned))
        before = turned


def wanted_boxes(part_ref, boxes):
    total = part_ref.shape[1]
    device = lax.axis_index(AXES)
    wanted = []
    for step in (1, -1):
        found = jnp.int32(0)
        for k in range(boxes):
            other = (device + step) * boxes + k
            inside = (other >= 0) & (other < total)
            for number in range(PARTNERS):
                local = part_ref[number, jnp.clip(other, 0, total - 1)] - device * boxes
                found = jnp.where(inside & (local >= 0) & (local < boxes), local, found)
        wanted.append(found)
    return wanted


def window_kernel(part_hbm, orb_hbm, ahead_ref, back_ref, orb_ref, part_ref, flat_ref, sems):
    boxes = orb_ref.shape[1]
    small = pltpu.make_async_copy(part_hbm, part_ref, sems.at[0])
    large = [pltpu.make_async_copy(orb_hbm.at[spin], orb_ref.at[spin], sems.at[1 + spin]) for spin in range(2)]
    small.start()
    for copy in large:
        copy.start()
    small.wait()
    wanted = wanted_boxes(part_ref, boxes)
    large[0].wait()
    split_boxes(orb_ref.at[0], flat_ref, boxes)
    for side, ref in enumerate((ahead_ref, back_ref)):
        ref[...] = flat_ref[pl.ds(wanted[side], FLAT, stride=8), :].astype(BF)
    large[1].wait()


def table_layout(boxes):
    pairs = 0
    codes = pairs + boxes * PARTNERS * 4
    slots = codes + CAP + 1
    leaves = slots + AHEAD + BACK + 1
    order = leaves + AHEAD + BACK + 1
    homes = order + boxes
    return pairs, codes, slots, leaves, order, homes, homes + boxes + 1


def build_tables(dest_ref, part_ref, anc_ref, tab_ref, boxes):
    total = part_ref.shape[1]
    device = lax.axis_index(AXES)
    pairs, codes, slots, leaves, order, homes, _ = table_layout(boxes)
    one, none = jnp.int32(1), jnp.int32(0)
    for k in range(CAP + 1):
        tab_ref[codes + k] = boxes + AHEAD + BACK
    for k in range(boxes + 1):
        tab_ref[homes + k] = 0
    for k in range(AHEAD + BACK + 1):
        tab_ref[slots + k] = CAP
        tab_ref[leaves + k] = 0
    goes = [dest_ref[device * boxes + k] for k in range(boxes)]
    ahead_all, back_all = none, none
    for k in range(boxes):
        ahead_all = ahead_all + jnp.where(goes[k] == device + 1, one, none)
        back_all = back_all + jnp.where(goes[k] == device - 1, one, none)
    ahead, back, stay = none, none, none
    spots = []
    for k in range(boxes):
        is_ahead, is_back = goes[k] == device + 1, goes[k] == device - 1
        spot = jnp.where(is_ahead, ahead, jnp.where(is_back, ahead_all + back, ahead_all + back_all + stay))
        spots.append(spot)
        tab_ref[order + spot] = k
        spare = leaves + AHEAD + BACK
        tab_ref[jnp.where(is_ahead, leaves + jnp.minimum(ahead, AHEAD - 1), spare)] = spot
        tab_ref[jnp.where(is_back, leaves + AHEAD + jnp.minimum(back, BACK - 1), spare)] = spot
        ahead = ahead + jnp.where(is_ahead, one, none)
        back = back + jnp.where(is_back, one, none)
        stay = stay + jnp.where(is_ahead | is_back, none, one)
    count = none
    for block in range(3):
        arrived = none
        for k in range(boxes):
            box = (device + (block - 1)) * boxes + k
            hit = (box >= 0) & (box < total) & (dest_ref[jnp.clip(box, 0, total - 1)] == device)
            if block == 1:
                code = spots[k]
                tab_ref[jnp.where(hit, homes + code, homes + boxes)] = jnp.minimum(count, CAP - 1)
            else:
                first, most = (0, AHEAD) if block == 0 else (AHEAD, BACK)
                where = first + jnp.minimum(arrived, most - 1)
                code = boxes + where
                tab_ref[jnp.where(hit, slots + where, slots + AHEAD + BACK)] = count
                arrived = arrived + jnp.where(hit, one, none)
            tab_ref[jnp.where(hit, codes + jnp.minimum(count, CAP - 1), codes + CAP)] = code
            count = count + jnp.where(hit, one, none)
    for box in range(boxes):
        me = device * boxes + box
        for number in range(PARTNERS):
            other = part_ref[number, me]
            local = other - device * boxes
            base = pairs + (box * PARTNERS + number) * 4
            tab_ref[base] = jnp.where(local < 0, boxes, jnp.where(local >= boxes, boxes + 1, local))
            for axis, extent in enumerate((GRID_X, GRID_Y, GRID_Z)):
                moved = anc_ref[axis, other] - anc_ref[axis, me] + extent // 2
                moved = jnp.where(moved < 0, moved + extent, jnp.where(moved >= extent, moved - extent, moved))
                tab_ref[base + 1 + axis] = jnp.clip(moved - extent // 2, -(PAD - 4), PAD - 4)


def reverse_box(pad_ref, box):
    body = pl.ds(PAD, EDGE)
    reverse_slabs(lambda v: pad_ref[0, box, v, body, :],
                  lambda u, x: pad_ref.__setitem__((1, box, u, body, slice(None)), x), 0, TILES)


def second_kernel(dest_hbm, part_hbm, anc_hbm, inv_hbm, diag_hbm, rest_hbm, orb_ref,
                  ahead_ref, back_ref, tab_ref, inv_ref, diag_ref, rest_ref,
                  dest_ref, part_ref, anc_ref, flat_ref, sems):
    boxes = orb_ref.shape[1]
    pieces = [(part_hbm, part_ref), (dest_hbm, dest_ref), (anc_hbm, anc_ref)]
    pieces += [(inv_hbm, inv_ref), (diag_hbm, diag_ref), (rest_hbm, rest_ref)]
    copies = [pltpu.make_async_copy(source, target, sems.at[k]) for k, (source, target) in enumerate(pieces)]
    for copy in copies:
        copy.start()
    split_boxes(orb_ref.at[1], flat_ref, boxes)
    for copy in copies[:3]:
        copy.wait()
    wanted = wanted_boxes(part_ref, boxes)
    for side, ref in enumerate((ahead_ref, back_ref)):
        ref[...] = flat_ref[pl.ds(wanted[side], FLAT, stride=8), :].astype(BF)
    build_tables(dest_ref, part_ref, anc_ref, tab_ref, boxes)
    for copy in copies[3:]:
        copy.wait()


def place_along():
    return lax.axis_index(AXES[-1]), lax.axis_size(AXES[-1])


def low_half():
    place, count = place_along()
    return 2 * place < count


def at_end():
    place, count = place_along()
    return place == count - 1


def slabs_kernel(spin, chosen, orb_ref, *refs):
    pad_ref, flat_ref = refs[-2:]
    boxes = orb_ref.shape[1]

    @pl.when(chosen())
    def _():
        split_boxes(orb_ref.at[spin], flat_ref, boxes)

        def slabs(box, _):
            flat_to_slabs(
                lambda t: flat_ref[pl.ds(box + 8 * t, HALF, stride=8 * PAIRT), :],
                lambda u, parity, x: pad_ref.__setitem__(
                    (0, box, u, pl.ds(PAD + parity, HALF, stride=2), slice(None)), x),
            )
            reverse_box(pad_ref, box)
            return 0

        lax.fori_loop(0, boxes, slabs, 0)


def modes_kernel(early, fac_hbm, *refs):
    to_ref, from_ref, fac_ref, sem = refs[-4:]

    @pl.when(jnp.logical_not(at_end()) if early else at_end())
    def _():
        copy = pltpu.make_async_copy(fac_hbm, fac_ref, sem)
        copy.start()
        for part in range(2):
            to_ref[part, FOLD:, :] = jnp.zeros((FWIDE - FOLD, FWIDE), BF)
            from_ref[part, FOLD:, :] = jnp.zeros((FWIDE - FOLD, FWIDE), BF)
        front = lax.broadcasted_iota(jnp.int32, (EDGE, 1), 0) < HALF
        copy.wait()

        def build(i, _):
            where = pl.ds(pl.multiple_of(i * 2 * EDGE, 16), 2 * EDGE)
            for start, size in CHUNKS:
                cols = slice(start, start + size)
                line = [fac_ref[0, pl.ds(2 * i + k, 1), cols] for k in range(2)]
                mode = [fac_ref[3, pl.ds(4 * i + k, 1), cols] for k in range(4)]
                modes = [jnp.where(front, mode[2 * k], mode[2 * k + 1]) for k in range(2)]
                for part in range(2):
                    right = fac_ref[1 + part, :, cols]
                    to_ref[part, where, cols] = jnp.concatenate([x * right for x in line], axis=0).astype(BF)
                    right = fac_ref[4 + part, :, cols]
                    from_ref[part, where, cols] = jnp.concatenate([x * right for x in modes], axis=0).astype(BF)
            return 0

        lax.fori_loop(0, HALF // 2, build, 0)


def fill_kernel(old_ref, prev_ref, next_ref, pad_ref, flat_ref):
    boxes = pad_ref.shape[1] - 2
    for side, ref in ((0, prev_ref), (1, next_ref)):
        flat_ref[...] = ref[...].astype(F32)
        flat_to_slabs(
            lambda t: flat_ref[pl.ds(t, HALF, stride=PAIRT), :],
            lambda u, parity, x: pad_ref.__setitem__(
                (0, boxes + side, u, pl.ds(PAD + parity, HALF, stride=2), slice(None)), x),
        )
        reverse_box(pad_ref, boxes + side)


def pair_kernel(start, held, spins, final, tab_ref, to_ref, from_ref, diag_ref, inv_ref, *refs):
    pads, (mov_ref, x_ref, y_ref, half_ref, res_ref) = refs[:len(spins)], refs[-5:]
    boxes = pads[0].shape[1] - 2
    pairs, codes, _, leaves, order, homes, _ = table_layout(boxes)
    if final:
        low_ref, high_ref, out_ref, form_ref, sems = refs[len(spins):-5]

        def copy(slot):
            return pltpu.make_async_copy(form_ref.at[slot], out_ref.at[slot], sems.at[slot])

        def early(slot, _):
            code = tab_ref[codes + slot]

            @pl.when(code < start)
            def _():
                spot = jnp.minimum(code, start - 1)
                for spin, ref in enumerate((low_ref, high_ref)):
                    form_ref[slot, pl.ds(spin, FLAT, stride=2), :] = ref[spot]
                copy(slot).start()

            @pl.when(code >= boxes + AHEAD + BACK)
            def _():
                form_ref[slot] = jnp.zeros(form_ref.shape[1:], F32)
                copy(slot).start()

            return 0

        lax.fori_loop(0, CAP, early, 0)
    else:
        out_ref, sends = refs[len(spins)], refs[len(spins) + 1:-5]
    lanes = lane_iota()
    rows = lax.broadcasted_iota(jnp.int32, (EDGE, 1), 0)

    def dense(index):
        box = tab_ref[order + start + index]
        places = []
        for number in range(PARTNERS):
            base = pairs + (box * PARTNERS + number) * 4
            source = tab_ref[base]
            da, db, dc = tab_ref[base + 1], tab_ref[base + 2], tab_ref[base + 3]
            row_ok = jnp.abs(2 * (rows - da) - (EDGE - 1)) < EDGE
            for b_by, c_by in ((db, dc), (-db, -dc)):
                offset = ZERO_TILES * LANES - (b_by * EDGE + c_by)
                places.append((source, da, b_by, c_by, offset // LANES, offset % LANES, row_ok))
        last = [[None] * len(places) for _ in spins]
        for u in range(FTILES + 1):
            keep = []
            for source, da, b_by, c_by, quotient, rest, row_ok in places:
                if u > 0:
                    cell = lanes + (u - 1) * LANES
                    b = (cell * 52429) >> 21
                    c = cell - b * EDGE
                    ok = (jnp.abs(2 * (b - b_by) - (EDGE - 1)) < EDGE) & (jnp.abs(2 * (c - c_by) - (EDGE - 1)) < EDGE)
                    if u == FTILES:
                        ok = ok & (lanes < FOLD - (FTILES - 1) * LANES)
                    keep.append(row_ok & ok)
            for at, pad_ref in enumerate(pads):
                values = []
                for which, (source, da, b_by, c_by, quotient, rest, row_ok) in enumerate(places):
                    part = which % 2
                    tile = jnp.clip(quotient + (u - ZERO_TILES), 0, TILES - 1)
                    x = pad_ref[part, source, tile, pl.ds(PAD - da, EDGE), :]
                    turned = pltpu.roll(x, (LANES - rest) % LANES, 1)
                    if u > 0:
                        moved = jnp.where(keep[which], jnp.where(lanes < LANES - rest, last[at][which], turned), 0.0)
                        mov_ref[index, at, which // 2, part, u - 1] = moved
                        values.append(pad_ref[part, box, u - 1, pl.ds(PAD, EDGE), :] * moved)
                    last[at][which] = turned
                if u > 0:
                    where = pl.ds((index * len(spins) + at) * PARTNERS * EDGE, PARTNERS * EDGE)
                    front = jnp.concatenate(values[0::2], axis=0)
                    behind = jnp.concatenate(values[1::2], axis=0)
                    x_ref[where, (u - 1) * LANES:u * LANES] = (front + behind).astype(BF)
                    x_ref[where, FWIDE + (u - 1) * LANES:FWIDE + u * LANES] = (front - behind).astype(BF)
        return 0

    for index in range(held):
        dense(index)

    cubes = held * len(spins) * PARTNERS
    diag = diag_ref[...]
    for first in range(0, 2 * FWIDE, NCHUNK):
        cols = slice(first, first + NCHUNK)
        y_ref[:, cols] = jnp.dot(diag, x_ref[:, cols], preferred_element_type=F32).astype(BF)

    def forward(first, size):
        for part in range(2):
            z = jnp.dot(y_ref[:, part * FWIDE:(part + 1) * FWIDE], to_ref[part, :, pl.ds(first, size)],
                        preferred_element_type=F32)
            cols = pl.ds(pl.multiple_of(part * FWIDE + first, LANES), size)
            z = z.reshape(cubes, EDGE, size) * inv_ref[:, cols][None]
            x_ref[:, cols] = z.reshape(cubes * EDGE, size).astype(BF)

    def backward(first, size):
        even, odd = [jnp.dot(x_ref[:, part * FWIDE:(part + 1) * FWIDE], from_ref[part, :, pl.ds(first, size)],
                             preferred_element_type=F32) for part in range(2)]
        y_ref[:, pl.ds(first, size)] = (even + odd).astype(BF)
        y_ref[:, pl.ds(pl.multiple_of(FWIDE + first, LANES), size)] = (even - odd).astype(BF)

    for step in (forward, backward):
        step(0, FWIDE)

    for first in range(0, 2 * FTILES, 2):
        potential = jnp.dot(diag, y_ref[:, first * LANES:(first + 2) * LANES], preferred_element_type=F32)
        for u in (first, first + 1):
            side = slice((u - first) * LANES, (u - first + 1) * LANES)
            for index in range(held):
                for at in range(len(spins)):
                    total = 0.0
                    for number in range(PARTNERS):
                        row = ((index * len(spins) + at) * PARTNERS + number) * EDGE
                        total = total + potential[row:row + EDGE, side] * mov_ref[index, at, number, u // FTILES, u % FTILES]
                    if u < FTILES:
                        res_ref[index * len(spins) + at, u] = total
                    else:
                        half_ref[index * len(spins) + at, u - FTILES] = total

    def unfold(row):
        middle = FTILES - 1

        def store(u, x):
            if u == middle:
                x = jnp.where(lanes < FOLD - middle * LANES, res_ref[row, middle], x)
            res_ref[row, u] = x

        reverse_slabs(lambda v: half_ref[row, v], store, middle, FTILES)
        return 0

    for row in range(held * len(spins)):
        unfold(row)

    if final:
        for index in range(held):
            home = tab_ref[homes + start + index]
            for at in range(len(spins)):
                slabs_to_flat(
                    lambda u, parity: res_ref[index * len(spins) + at, u, pl.ds(parity, HALF, stride=2), :],
                    lambda t, x: form_ref.__setitem__(
                        (home, pl.ds(2 * t + at, HALF, stride=2 * PAIRT), slice(None)), x),
                )
            copy(home).start()

        def finish(slot, _):
            code = tab_ref[codes + slot]

            @pl.when((code < boxes) | (code >= boxes + AHEAD + BACK))
            def _():
                copy(slot).wait()

            return 0

        lax.fori_loop(0, CAP, finish, 0)
        return

    def flatten(row):
        slabs_to_flat(
            lambda u, parity: res_ref[row, u, pl.ds(parity, HALF, stride=2), :],
            lambda t, x: out_ref.__setitem__((row, pl.ds(t, HALF, stride=PAIRT), slice(None)), x),
        )
        return 0

    for row in range(held * len(spins)):
        flatten(row)
    for k in range(AHEAD):
        sends[0][k] = out_ref[tab_ref[leaves + k]].astype(BF)
    for k in range(BACK):
        sends[1][k] = out_ref[tab_ref[leaves + AHEAD + k]].astype(BF)


def place_kernel(boxes, tab_ref, prev_low, next_low, prev_high, next_high, kept_ref, out_ref, form_ref, sems):
    slots = table_layout(boxes)[2]
    copies = []
    for k in range(AHEAD + BACK):
        pair, row = ((prev_low, prev_high), k) if k < AHEAD else ((next_low, next_high), k - AHEAD)
        slot = tab_ref[slots + k]
        copy = pltpu.make_async_copy(form_ref.at[k], out_ref.at[jnp.minimum(slot, CAP - 1)], sems.at[k])

        @pl.when(slot < CAP)
        def _():
            for spin, ref in enumerate(pair):
                form_ref[k, pl.ds(spin, FLAT, stride=2), :] = ref[row].astype(F32)
            copy.start()

        copies.append((slot, copy))
    for slot, copy in copies:
        @pl.when(slot < CAP)
        def _():
            copy.wait()


def from_behind(value, steps):
    count = lax.axis_size(AXES)
    return lax.ppermute(value, AXES, [(source, (source + steps) % count) for source in range(count)])


def whole(count):
    return [pl.BlockSpec(memory_space=pltpu.VMEM)] * count


SCALARS = pl.BlockSpec(memory_space=pltpu.SMEM)
ANYWHERE = pl.BlockSpec(memory_space=pltpu.MemorySpace.HBM)


def in_place(value):
    return pltpu.with_memory_space_constraint(jnp.asarray(value), pltpu.HBM)


def cost(flops, size):
    return pl.CostEstimate(flops=flops, bytes_accessed=size, transcendentals=0)


def shards(orbitals, dest, partners, anchors):
    boxes = orbitals.shape[1]
    sine, inverse, factors = tables()
    partners_t, anchors_t = partners.T, anchors.T

    box = jax.ShapeDtypeStruct((FLAT, LANES), BF)
    splitter = pltpu.VMEM((FLAT * 8, LANES), F32)
    ahead, back, held = pl.pallas_call(
        window_kernel,
        out_shape=[box] * 2 + [jax.ShapeDtypeStruct(orbitals.shape, BF)],
        in_specs=[ANYWHERE] * 2,
        out_specs=whole(3),
        scratch_shapes=[pltpu.SMEM(partners_t.shape, jnp.int32), splitter, pltpu.SemaphoreType.DMA((3,))],
        compiler_params=pltpu.CompilerParams(vmem_limit_bytes=12 << 20),
        name="window",
    )(*map(in_place, (partners_t, orbitals)))
    prev_low = from_behind(ahead, 1)
    next_low = from_behind(back, -1)

    folded = jax.ShapeDtypeStruct((2, FWIDE, FWIDE), BF)

    def build_modes(early, *before):
        return pl.pallas_call(
            lambda *refs: modes_kernel(early, *refs),
            out_shape=[folded] * 2,
            in_specs=[ANYWHERE] + whole(len(before)),
            out_specs=whole(2),
            scratch_shapes=[pltpu.VMEM(factors.shape, F32), pltpu.SemaphoreType.DMA],
            input_output_aliases={1: 0, 2: 1} if before else {},
            compiler_params=pltpu.CompilerParams(vmem_limit_bytes=12 << 20),
            cost_estimate=cost(4_000_000, 4_000_000),
        )(in_place(factors), *before)

    modes = build_modes(True)
    moving = AHEAD + BACK
    slabs = jax.ShapeDtypeStruct((2, boxes + 2, TILES, ROWS, LANES), F32)
    diags = [np.kron(np.eye(cubes, dtype=np.float32), sine).astype(jnp.bfloat16)
             for cubes in (moving * PARTNERS, (boxes - moving) * 2 * PARTNERS)]
    handed = (inverse, *diags)
    second = pl.pallas_call(
        second_kernel,
        out_shape=[box, box, jax.ShapeDtypeStruct((table_layout(boxes)[-1],), jnp.int32)]
        + [jax.ShapeDtypeStruct(value.shape, value.dtype) for value in handed],
        in_specs=[ANYWHERE] * 6 + whole(1),
        out_specs=whole(2) + [SCALARS] + whole(3),
        scratch_shapes=[pltpu.SMEM(dest.shape, jnp.int32), pltpu.SMEM(partners_t.shape, jnp.int32),
                        pltpu.SMEM(anchors_t.shape, jnp.int32), splitter, pltpu.SemaphoreType.DMA((6,))],
        compiler_params=pltpu.CompilerParams(vmem_limit_bytes=12 << 20),
        cost_estimate=cost(1_000_000, 2_000_000),
        name="second",
    )
    ahead, back, table, inverse, *diags = second(
        *map(in_place, (dest, partners_t, anchors_t, *handed)), held)
    prev_high = from_behind(ahead, 1)
    next_high = from_behind(back, -1)
    to_modes, from_modes = build_modes(False, *modes)

    def inner():
        return jnp.logical_not(low_half() | at_end())

    def build_slabs(spin, *before):
        here = (inner, low_half)[spin]
        late = len(before) > 0

        def chosen():
            return jnp.logical_not(here()) if late else here()

        return pl.pallas_call(
            lambda *refs: slabs_kernel(spin, chosen, *refs),
            out_shape=slabs,
            in_specs=whole(1 + len(before)),
            out_specs=pl.BlockSpec(memory_space=pltpu.VMEM),
            scratch_shapes=[splitter],
            input_output_aliases={1: 0} if before else {},
            compiler_params=pltpu.CompilerParams(vmem_limit_bytes=12 << 20),
            cost_estimate=cost(2_000_000, 4_000_000),
        )(held, *before)

    pads = [build_slabs(0, build_slabs(0)), build_slabs(1, build_slabs(1))]
    for spin, halo in enumerate(((prev_low, next_low), (prev_high, next_high))):
        pads[spin] = pl.pallas_call(
            fill_kernel,
            out_shape=slabs,
            in_specs=whole(3),
            out_specs=pl.BlockSpec(memory_space=pltpu.VMEM),
            scratch_shapes=[pltpu.VMEM((FLAT, LANES), F32)],
            input_output_aliases={0: 0},
            compiler_params=pltpu.CompilerParams(vmem_limit_bytes=12 << 20),
            cost_estimate=cost(1_000_000, 2_000_000),
        )(pads[spin], *halo)

    shape = jax.ShapeDtypeStruct((CAP, 2 * FLAT, LANES), F32)

    def solve(start, held, spins, terms=None):
        cubes = held * len(spins) * PARTNERS
        final = terms is not None
        if final:
            shapes, specs = [shape], [ANYWHERE]
            extra = [pltpu.VMEM(shape.shape, F32), pltpu.SemaphoreType.DMA((CAP,))]
        else:
            shapes = [jax.ShapeDtypeStruct((held * len(spins), FLAT, LANES), F32)]
            shapes += [jax.ShapeDtypeStruct((count, FLAT, LANES), BF) for count in (AHEAD, BACK)]
            specs, extra = whole(3), []
        operands = [table, to_modes, from_modes, diags[final], inverse] + [pads[spin] for spin in spins] + (terms or [])
        return pl.pallas_call(
            lambda *refs: pair_kernel(start, held, spins, final, *refs),
            out_shape=shapes,
            in_specs=[SCALARS] + whole(len(operands) - 1),
            out_specs=specs,
            scratch_shapes=extra + [
                pltpu.VMEM((held, len(spins), PARTNERS, 2, FTILES, EDGE, LANES), F32),
                pltpu.VMEM((cubes * EDGE, 2 * FWIDE), BF),
                pltpu.VMEM((cubes * EDGE, 2 * FWIDE), BF),
                pltpu.VMEM((held * len(spins), FTILES, EDGE, LANES), F32),
                pltpu.VMEM((held * len(spins), TILES, EDGE, LANES), F32),
            ],
            compiler_params=pltpu.CompilerParams(vmem_limit_bytes=20 << 20),
            cost_estimate=cost(2 * cubes * EDGE * FACE * FACE, 10_000_000),
        )(*operands)

    terms, arrived = [], []
    for spin in range(2):
        mine, sent_ahead, sent_back = solve(0, moving, (spin,))
        terms.append(mine)
        ahead = from_behind(sent_ahead, 1)
        back = from_behind(sent_back, -1)
        arrived += [ahead, back]
    kept, = solve(moving, boxes - moving, (0, 1), terms)
    placed = pl.pallas_call(
        lambda *refs: place_kernel(boxes, *refs),
        out_shape=shape,
        in_specs=[SCALARS] + whole(4) + [ANYWHERE],
        out_specs=ANYWHERE,
        scratch_shapes=[pltpu.VMEM((AHEAD + BACK, 2 * FLAT, LANES), F32),
                        pltpu.SemaphoreType.DMA((AHEAD + BACK,))],
        input_output_aliases={5: 0},
        compiler_params=pltpu.CompilerParams(vmem_limit_bytes=8 << 20),
        cost_estimate=cost(1_000_000, 4_000_000),
        name="place",
    )(table, *arrived, kept)
    placed = placed.reshape(-1).reshape(CAP, FLAT, 2, LANES).transpose(0, 2, 1, 3)
    return placed.reshape(CAP, 2, FLAT * LANES).transpose(1, 0, 2)


def solution(mesh):
    return jax.shard_map(
        shards,
        mesh=mesh,
        in_specs=(P(None, AXES, None), P(), P(), P()),
        out_specs=P(None, AXES, None),
        check_vma=False,
    )
```

```python
import jax
import jax.numpy as jnp
import numpy as np
from jax import lax
from jax.experimental import pallas as pl
from jax.experimental.pallas import tpu as pltpu
from jax.sharding import PartitionSpec as P


EDGE = 40
PARTNERS = 2
GRID_X = 768
GRID_Y = 384
GRID_Z = 384
BACK = 2
AHEAD = 1
CAP = 7
SCREEN = 0.001

AXES = ("gx", "gy", "gz")
LANES = 128
FACE = EDGE * EDGE
TILES = -(-FACE // LANES)
NCHUNK = 256
FOLD = FACE // 2
FTILES = -(-FOLD // LANES)
FWIDE = FTILES * LANES
CHUNKS = [(min(first, FWIDE - NCHUNK), NCHUNK) for first in range(0, FWIDE, NCHUNK)]
FLAT = EDGE ** 3 // LANES
HALF = EDGE // 2
PAIRT = 2 * FACE // LANES
PAD = 24
ROWS = EDGE + 2 * PAD
ZERO_TILES = 7
BF = jnp.bfloat16
F32 = jnp.float32


def tables():
    counter = np.arange(EDGE) + 1
    turns = np.outer(counter, counter) % (2 * (EDGE + 1))
    sine = (np.sqrt(2.0 / (EDGE + 1.0)) * np.sin(np.pi * turns / (EDGE + 1.0))).astype(np.float32)
    sine = sine.astype(jnp.bfloat16).astype(np.float32)
    flipped = sine[::-1] * np.where(np.arange(EDGE) % 2 == 0, 1.0, -1.0)
    assert np.array_equal(sine, flipped)
    levels = 2.0 - 2.0 * np.cos(np.pi * counter / (EDGE + 1.0))
    number = np.arange(FOLD)
    second, step = number // HALF, number % HALF
    thirds = [2 * step + second % 2, 2 * step + 1 - second % 2]
    inverse = np.zeros((EDGE, 2 * FWIDE), np.float32)
    for part, third in enumerate(thirds):
        lam = levels[:, None] + levels[second] + levels[third] + SCREEN
        inverse[:, part * FWIDE:part * FWIDE + FOLD] = 1.0 / lam
    factors = np.zeros((6, EDGE, FWIDE), np.float32)
    factors[0, :HALF, :FOLD] = sine[:HALF][:, second]
    for part, third in enumerate(thirds):
        factors[1 + part, :, :FOLD] = sine[:, third]
    factors[3, :, :FOLD] = np.repeat(sine[:HALF], EDGE, axis=0).T
    lines = np.tile(sine, (HALF, 1)).T
    factors[4, :, :FOLD] = np.concatenate([lines[0::2], lines[1::2]])
    factors[5, :, :FOLD] = np.concatenate([lines[1::2], lines[0::2]])
    return sine, inverse, factors


def lane_iota():
    return lax.broadcasted_iota(jnp.int32, (1, LANES), 1)


def split_boxes(orb_ref, flat_ref, boxes):
    def step(i, _):
        base = pl.multiple_of(i * PAIRT * LANES, LANES)
        x = orb_ref[:, pl.ds(base, PAIRT * LANES)].astype(F32)
        for j in range(PAIRT):
            flat_ref[pl.ds(pl.multiple_of((i * PAIRT + j) * 8, 8), boxes), :] = x[:, j * LANES:(j + 1) * LANES]
        return 0

    lax.fori_loop(0, HALF, step, 0)


def flat_to_slabs(load, store):
    low = lane_iota() < LANES // 2
    rolled = None
    for t in range(PAIRT):
        x = load(t)
        if t < TILES:
            store(t, 0, x)
        if t >= TILES - 1:
            turned = pltpu.roll(x, LANES // 2, 1)
            if rolled is not None:
                store(t - TILES, 1, jnp.where(low, rolled, turned))
            rolled = turned
    store(TILES - 1, 1, rolled)


def turn(x):
    source = (LANES // 2 - 1 - lax.broadcasted_iota(jnp.int32, x.shape, 1)) & (LANES - 1)
    return jnp.take_along_axis(x, source, axis=1)


def reverse_slabs(load, store, first, count):
    low = lane_iota() < LANES // 2
    turned = [turn(load(v)) for v in range(count)]
    for u in range(first, TILES):
        v = TILES - 1 - u
        store(u, jnp.where(low, turned[v], turned[v - 1]) if v > 0 else turned[v])


def slabs_to_flat(load, store):
    low = lane_iota() < LANES // 2
    for t in range(TILES - 1):
        store(t, load(t, 0))
    before = load(TILES - 1, 0)
    for v in range(TILES):
        turned = pltpu.roll(load(v, 1), LANES // 2, 1)
        store(TILES - 1 + v, jnp.where(low, before, turned))
        before = turned


def wanted_boxes(part_ref, boxes):
    total = part_ref.shape[1]
    device = lax.axis_index(AXES)
    wanted = []
    for step in (1, -1):
        found = jnp.int32(0)
        for k in range(boxes):
            other = (device + step) * boxes + k
            inside = (other >= 0) & (other < total)
            for number in range(PARTNERS):
                local = part_ref[number, jnp.clip(other, 0, total - 1)] - device * boxes
                found = jnp.where(inside & (local >= 0) & (local < boxes), local, found)
        wanted.append(found)
    return wanted


def window_kernel(part_hbm, orb_hbm, ahead_ref, back_ref, orb_ref, part_ref, flat_ref, sems):
    boxes = orb_ref.shape[1]
    small = pltpu.make_async_copy(part_hbm, part_ref, sems.at[0])
    large = [pltpu.make_async_copy(orb_hbm.at[spin], orb_ref.at[spin], sems.at[1 + spin]) for spin in range(2)]
    small.start()
    for copy in large:
        copy.start()
    small.wait()
    wanted = wanted_boxes(part_ref, boxes)
    large[0].wait()
    split_boxes(orb_ref.at[0], flat_ref, boxes)
    for side, ref in enumerate((ahead_ref, back_ref)):
        ref[...] = flat_ref[pl.ds(wanted[side], FLAT, stride=8), :].astype(BF)
    large[1].wait()


def table_layout(boxes):
    pairs = 0
    codes = pairs + boxes * PARTNERS * 4
    slots = codes + CAP + 1
    leaves = slots + AHEAD + BACK + 1
    order = leaves + AHEAD + BACK + 1
    homes = order + boxes
    return pairs, codes, slots, leaves, order, homes, homes + boxes + 1


def build_tables(dest_ref, part_ref, anc_ref, tab_ref, boxes):
    total = part_ref.shape[1]
    device = lax.axis_index(AXES)
    pairs, codes, slots, leaves, order, homes, _ = table_layout(boxes)
    one, none = jnp.int32(1), jnp.int32(0)
    for k in range(CAP + 1):
        tab_ref[codes + k] = boxes + AHEAD + BACK
    for k in range(boxes + 1):
        tab_ref[homes + k] = 0
    for k in range(AHEAD + BACK + 1):
        tab_ref[slots + k] = CAP
        tab_ref[leaves + k] = 0
    goes = [dest_ref[device * boxes + k] for k in range(boxes)]
    ahead_all, back_all = none, none
    for k in range(boxes):
        ahead_all = ahead_all + jnp.where(goes[k] == device + 1, one, none)
        back_all = back_all + jnp.where(goes[k] == device - 1, one, none)
    ahead, back, stay = none, none, none
    spots = []
    for k in range(boxes):
        is_ahead, is_back = goes[k] == device + 1, goes[k] == device - 1
        spot = jnp.where(is_ahead, ahead, jnp.where(is_back, ahead_all + back, ahead_all + back_all + stay))
        spots.append(spot)
        tab_ref[order + spot] = k
        spare = leaves + AHEAD + BACK
        tab_ref[jnp.where(is_ahead, leaves + jnp.minimum(ahead, AHEAD - 1), spare)] = spot
        tab_ref[jnp.where(is_back, leaves + AHEAD + jnp.minimum(back, BACK - 1), spare)] = spot
        ahead = ahead + jnp.where(is_ahead, one, none)
        back = back + jnp.where(is_back, one, none)
        stay = stay + jnp.where(is_ahead | is_back, none, one)
    count = none
    for block in range(3):
        arrived = none
        for k in range(boxes):
            box = (device + (block - 1)) * boxes + k
            hit = (box >= 0) & (box < total) & (dest_ref[jnp.clip(box, 0, total - 1)] == device)
            if block == 1:
                code = spots[k]
                tab_ref[jnp.where(hit, homes + code, homes + boxes)] = jnp.minimum(count, CAP - 1)
            else:
                first, most = (0, AHEAD) if block == 0 else (AHEAD, BACK)
                where = first + jnp.minimum(arrived, most - 1)
                code = boxes + where
                tab_ref[jnp.where(hit, slots + where, slots + AHEAD + BACK)] = count
                arrived = arrived + jnp.where(hit, one, none)
            tab_ref[jnp.where(hit, codes + jnp.minimum(count, CAP - 1), codes + CAP)] = code
            count = count + jnp.where(hit, one, none)
    for box in range(boxes):
        me = device * boxes + box
        for number in range(PARTNERS):
            other = part_ref[number, me]
            local = other - device * boxes
            base = pairs + (box * PARTNERS + number) * 4
            tab_ref[base] = jnp.where(local < 0, boxes, jnp.where(local >= boxes, boxes + 1, local))
            for axis, extent in enumerate((GRID_X, GRID_Y, GRID_Z)):
                moved = anc_ref[axis, other] - anc_ref[axis, me] + extent // 2
                moved = jnp.where(moved < 0, moved + extent, jnp.where(moved >= extent, moved - extent, moved))
                tab_ref[base + 1 + axis] = jnp.clip(moved - extent // 2, -(PAD - 4), PAD - 4)


def reverse_box(pad_ref, box):
    body = pl.ds(PAD, EDGE)
    reverse_slabs(lambda v: pad_ref[0, box, v, body, :],
                  lambda u, x: pad_ref.__setitem__((1, box, u, body, slice(None)), x), 0, TILES)


def second_kernel(dest_hbm, part_hbm, anc_hbm, inv_hbm, diag_hbm, rest_hbm, orb_ref,
                  ahead_ref, back_ref, tab_ref, inv_ref, diag_ref, rest_ref,
                  dest_ref, part_ref, anc_ref, flat_ref, sems):
    boxes = orb_ref.shape[1]
    pieces = [(part_hbm, part_ref), (dest_hbm, dest_ref), (anc_hbm, anc_ref)]
    pieces += [(inv_hbm, inv_ref), (diag_hbm, diag_ref), (rest_hbm, rest_ref)]
    copies = [pltpu.make_async_copy(source, target, sems.at[k]) for k, (source, target) in enumerate(pieces)]
    for copy in copies:
        copy.start()
    split_boxes(orb_ref.at[1], flat_ref, boxes)
    for copy in copies[:3]:
        copy.wait()
    wanted = wanted_boxes(part_ref, boxes)
    for side, ref in enumerate((ahead_ref, back_ref)):
        ref[...] = flat_ref[pl.ds(wanted[side], FLAT, stride=8), :].astype(BF)
    build_tables(dest_ref, part_ref, anc_ref, tab_ref, boxes)
    for copy in copies[3:]:
        copy.wait()


def low_half():
    return 2 * lax.axis_index(AXES[-1]) < lax.axis_size(AXES[-1])


def slabs_kernel(spin, chosen, orb_ref, *refs):
    pad_ref, flat_ref = refs[-2:]
    boxes = orb_ref.shape[1]

    @pl.when(chosen() if chosen else True)
    def _():
        split_boxes(orb_ref.at[spin], flat_ref, boxes)

        def slabs(box, _):
            flat_to_slabs(
                lambda t: flat_ref[pl.ds(box + 8 * t, HALF, stride=8 * PAIRT), :],
                lambda u, parity, x: pad_ref.__setitem__(
                    (0, box, u, pl.ds(PAD + parity, HALF, stride=2), slice(None)), x),
            )
            reverse_box(pad_ref, box)
            return 0

        lax.fori_loop(0, boxes, slabs, 0)


def modes_kernel(early, fac_hbm, *refs):
    to_ref, from_ref, fac_ref, sem = refs[-4:]

    @pl.when(low_half() if early else jnp.logical_not(low_half()))
    def _():
        copy = pltpu.make_async_copy(fac_hbm, fac_ref, sem)
        copy.start()
        for part in range(2):
            to_ref[part, FOLD:, :] = jnp.zeros((FWIDE - FOLD, FWIDE), BF)
            from_ref[part, FOLD:, :] = jnp.zeros((FWIDE - FOLD, FWIDE), BF)
        front = lax.broadcasted_iota(jnp.int32, (EDGE, 1), 0) < HALF
        copy.wait()

        def build(i, _):
            where = pl.ds(pl.multiple_of(i * 2 * EDGE, 16), 2 * EDGE)
            for start, size in CHUNKS:
                cols = slice(start, start + size)
                line = [fac_ref[0, pl.ds(2 * i + k, 1), cols] for k in range(2)]
                mode = [fac_ref[3, pl.ds(4 * i + k, 1), cols] for k in range(4)]
                modes = [jnp.where(front, mode[2 * k], mode[2 * k + 1]) for k in range(2)]
                for part in range(2):
                    right = fac_ref[1 + part, :, cols]
                    to_ref[part, where, cols] = jnp.concatenate([x * right for x in line], axis=0).astype(BF)
                    right = fac_ref[4 + part, :, cols]
                    from_ref[part, where, cols] = jnp.concatenate([x * right for x in modes], axis=0).astype(BF)
            return 0

        lax.fori_loop(0, HALF // 2, build, 0)


def fill_kernel(old_ref, prev_ref, next_ref, pad_ref, flat_ref):
    boxes = pad_ref.shape[1] - 2
    for side, ref in ((0, prev_ref), (1, next_ref)):
        flat_ref[...] = ref[...].astype(F32)
        flat_to_slabs(
            lambda t: flat_ref[pl.ds(t, HALF, stride=PAIRT), :],
            lambda u, parity, x: pad_ref.__setitem__(
                (0, boxes + side, u, pl.ds(PAD + parity, HALF, stride=2), slice(None)), x),
        )
        reverse_box(pad_ref, boxes + side)


def pair_kernel(start, held, spins, final, tab_ref, to_ref, from_ref, diag_ref, inv_ref, *refs):
    pads, (mov_ref, x_ref, y_ref, half_ref, res_ref) = refs[:len(spins)], refs[-5:]
    boxes = pads[0].shape[1] - 2
    pairs, codes, _, leaves, order, homes, _ = table_layout(boxes)
    if final:
        low_ref, high_ref, out_ref, form_ref, sems = refs[len(spins):-5]

        def copy(slot):
            return pltpu.make_async_copy(form_ref.at[slot], out_ref.at[slot], sems.at[slot])

        def early(slot, _):
            code = tab_ref[codes + slot]

            @pl.when(code < start)
            def _():
                spot = jnp.minimum(code, start - 1)
                for spin, ref in enumerate((low_ref, high_ref)):
                    form_ref[slot, pl.ds(spin, FLAT, stride=2), :] = ref[spot]
                copy(slot).start()

            @pl.when(code >= boxes + AHEAD + BACK)
            def _():
                form_ref[slot] = jnp.zeros(form_ref.shape[1:], F32)
                copy(slot).start()

            return 0

        lax.fori_loop(0, CAP, early, 0)
    else:
        out_ref, sends = refs[len(spins)], refs[len(spins) + 1:-5]
    lanes = lane_iota()
    rows = lax.broadcasted_iota(jnp.int32, (EDGE, 1), 0)

    def dense(index):
        box = tab_ref[order + start + index]
        places = []
        for number in range(PARTNERS):
            base = pairs + (box * PARTNERS + number) * 4
            source = tab_ref[base]
            da, db, dc = tab_ref[base + 1], tab_ref[base + 2], tab_ref[base + 3]
            row_ok = jnp.abs(2 * (rows - da) - (EDGE - 1)) < EDGE
            for b_by, c_by in ((db, dc), (-db, -dc)):
                offset = ZERO_TILES * LANES - (b_by * EDGE + c_by)
                places.append((source, da, b_by, c_by, offset // LANES, offset % LANES, row_ok))
        last = [[None] * len(places) for _ in spins]
        for u in range(FTILES + 1):
            keep = []
            for source, da, b_by, c_by, quotient, rest, row_ok in places:
                if u > 0:
                    cell = lanes + (u - 1) * LANES
                    b = (cell * 52429) >> 21
                    c = cell - b * EDGE
                    ok = (jnp.abs(2 * (b - b_by) - (EDGE - 1)) < EDGE) & (jnp.abs(2 * (c - c_by) - (EDGE - 1)) < EDGE)
                    if u == FTILES:
                        ok = ok & (lanes < FOLD - (FTILES - 1) * LANES)
                    keep.append(row_ok & ok)
            for at, pad_ref in enumerate(pads):
                values = []
                for which, (source, da, b_by, c_by, quotient, rest, row_ok) in enumerate(places):
                    part = which % 2
                    tile = jnp.clip(quotient + (u - ZERO_TILES), 0, TILES - 1)
                    x = pad_ref[part, source, tile, pl.ds(PAD - da, EDGE), :]
                    turned = pltpu.roll(x, (LANES - rest) % LANES, 1)
                    if u > 0:
                        moved = jnp.where(keep[which], jnp.where(lanes < LANES - rest, last[at][which], turned), 0.0)
                        mov_ref[index, at, which // 2, part, u - 1] = moved
                        values.append(pad_ref[part, box, u - 1, pl.ds(PAD, EDGE), :] * moved)
                    last[at][which] = turned
                if u > 0:
                    where = pl.ds((index * len(spins) + at) * PARTNERS * EDGE, PARTNERS * EDGE)
                    front = jnp.concatenate(values[0::2], axis=0)
                    behind = jnp.concatenate(values[1::2], axis=0)
                    x_ref[where, (u - 1) * LANES:u * LANES] = (front + behind).astype(BF)
                    x_ref[where, FWIDE + (u - 1) * LANES:FWIDE + u * LANES] = (front - behind).astype(BF)
        return 0

    for index in range(held):
        dense(index)

    cubes = held * len(spins) * PARTNERS
    diag = diag_ref[...]
    for first in range(0, 2 * FWIDE, NCHUNK):
        cols = slice(first, first + NCHUNK)
        y_ref[:, cols] = jnp.dot(diag, x_ref[:, cols], preferred_element_type=F32).astype(BF)

    def forward(first, size):
        for part in range(2):
            z = jnp.dot(y_ref[:, part * FWIDE:(part + 1) * FWIDE], to_ref[part, :, pl.ds(first, size)],
                        preferred_element_type=F32)
            cols = pl.ds(pl.multiple_of(part * FWIDE + first, LANES), size)
            z = z.reshape(cubes, EDGE, size) * inv_ref[:, cols][None]
            x_ref[:, cols] = z.reshape(cubes * EDGE, size).astype(BF)

    def backward(first, size):
        even, odd = [jnp.dot(x_ref[:, part * FWIDE:(part + 1) * FWIDE], from_ref[part, :, pl.ds(first, size)],
                             preferred_element_type=F32) for part in range(2)]
        y_ref[:, pl.ds(first, size)] = (even + odd).astype(BF)
        y_ref[:, pl.ds(pl.multiple_of(FWIDE + first, LANES), size)] = (even - odd).astype(BF)

    for step in (forward, backward):
        step(0, FWIDE)

    for first in range(0, 2 * FTILES, 2):
        potential = jnp.dot(diag, y_ref[:, first * LANES:(first + 2) * LANES], preferred_element_type=F32)
        for u in (first, first + 1):
            side = slice((u - first) * LANES, (u - first + 1) * LANES)
            for index in range(held):
                for at in range(len(spins)):
                    total = 0.0
                    for number in range(PARTNERS):
                        row = ((index * len(spins) + at) * PARTNERS + number) * EDGE
                        total = total + potential[row:row + EDGE, side] * mov_ref[index, at, number, u // FTILES, u % FTILES]
                    if u < FTILES:
                        res_ref[index * len(spins) + at, u] = total
                    else:
                        half_ref[index * len(spins) + at, u - FTILES] = total

    def unfold(row):
        middle = FTILES - 1

        def store(u, x):
            if u == middle:
                x = jnp.where(lanes < FOLD - middle * LANES, res_ref[row, middle], x)
            res_ref[row, u] = x

        reverse_slabs(lambda v: half_ref[row, v], store, middle, FTILES)
        return 0

    for row in range(held * len(spins)):
        unfold(row)

    if final:
        for index in range(held):
            home = tab_ref[homes + start + index]
            for at in range(len(spins)):
                slabs_to_flat(
                    lambda u, parity: res_ref[index * len(spins) + at, u, pl.ds(parity, HALF, stride=2), :],
                    lambda t, x: form_ref.__setitem__(
                        (home, pl.ds(2 * t + at, HALF, stride=2 * PAIRT), slice(None)), x),
                )
            copy(home).start()

        def finish(slot, _):
            code = tab_ref[codes + slot]

            @pl.when((code < boxes) | (code >= boxes + AHEAD + BACK))
            def _():
                copy(slot).wait()

            return 0

        lax.fori_loop(0, CAP, finish, 0)
        return

    def flatten(row):
        slabs_to_flat(
            lambda u, parity: res_ref[row, u, pl.ds(parity, HALF, stride=2), :],
            lambda t, x: out_ref.__setitem__((row, pl.ds(t, HALF, stride=PAIRT), slice(None)), x),
        )
        return 0

    for row in range(held * len(spins)):
        flatten(row)
    for k in range(AHEAD):
        sends[0][k] = out_ref[tab_ref[leaves + k]].astype(BF)
    for k in range(BACK):
        sends[1][k] = out_ref[tab_ref[leaves + AHEAD + k]].astype(BF)


def place_kernel(boxes, tab_ref, prev_low, next_low, prev_high, next_high, kept_ref, out_ref, form_ref, sems):
    slots = table_layout(boxes)[2]
    copies = []
    for k in range(AHEAD + BACK):
        pair, row = ((prev_low, prev_high), k) if k < AHEAD else ((next_low, next_high), k - AHEAD)
        slot = tab_ref[slots + k]
        copy = pltpu.make_async_copy(form_ref.at[k], out_ref.at[jnp.minimum(slot, CAP - 1)], sems.at[k])

        @pl.when(slot < CAP)
        def _():
            for spin, ref in enumerate(pair):
                form_ref[k, pl.ds(spin, FLAT, stride=2), :] = ref[row].astype(F32)
            copy.start()

        copies.append((slot, copy))
    for slot, copy in copies:
        @pl.when(slot < CAP)
        def _():
            copy.wait()


def from_behind(value, steps):
    count = lax.axis_size(AXES)
    return lax.ppermute(value, AXES, [(source, (source + steps) % count) for source in range(count)])


def whole(count):
    return [pl.BlockSpec(memory_space=pltpu.VMEM)] * count


SCALARS = pl.BlockSpec(memory_space=pltpu.SMEM)
ANYWHERE = pl.BlockSpec(memory_space=pltpu.MemorySpace.HBM)


def in_place(value):
    return pltpu.with_memory_space_constraint(jnp.asarray(value), pltpu.HBM)


def cost(flops, size):
    return pl.CostEstimate(flops=flops, bytes_accessed=size, transcendentals=0)


def shards(orbitals, dest, partners, anchors):
    boxes = orbitals.shape[1]
    sine, inverse, factors = tables()
    partners_t, anchors_t = partners.T, anchors.T

    box = jax.ShapeDtypeStruct((FLAT, LANES), BF)
    splitter = pltpu.VMEM((FLAT * 8, LANES), F32)
    ahead, back, held = pl.pallas_call(
        window_kernel,
        out_shape=[box] * 2 + [jax.ShapeDtypeStruct(orbitals.shape, BF)],
        in_specs=[ANYWHERE] * 2,
        out_specs=whole(3),
        scratch_shapes=[pltpu.SMEM(partners_t.shape, jnp.int32), splitter, pltpu.SemaphoreType.DMA((3,))],
        compiler_params=pltpu.CompilerParams(vmem_limit_bytes=12 << 20),
        name="window",
    )(*map(in_place, (partners_t, orbitals)))
    prev_low = from_behind(ahead, 1)
    next_low = from_behind(back, -1)

    folded = jax.ShapeDtypeStruct((2, FWIDE, FWIDE), BF)

    def build_modes(early, *before):
        return pl.pallas_call(
            lambda *refs: modes_kernel(early, *refs),
            out_shape=[folded] * 2,
            in_specs=[ANYWHERE] + whole(len(before)),
            out_specs=whole(2),
            scratch_shapes=[pltpu.VMEM(factors.shape, F32), pltpu.SemaphoreType.DMA],
            input_output_aliases={1: 0, 2: 1} if before else {},
            compiler_params=pltpu.CompilerParams(vmem_limit_bytes=12 << 20),
            cost_estimate=cost(4_000_000, 4_000_000),
        )(in_place(factors), *before)

    modes = build_modes(True)
    moving = AHEAD + BACK
    slabs = jax.ShapeDtypeStruct((2, boxes + 2, TILES, ROWS, LANES), F32)
    diags = [np.kron(np.eye(cubes, dtype=np.float32), sine).astype(jnp.bfloat16)
             for cubes in (moving * PARTNERS, (boxes - moving) * 2 * PARTNERS)]
    handed = (inverse, *diags)
    second = pl.pallas_call(
        second_kernel,
        out_shape=[box, box, jax.ShapeDtypeStruct((table_layout(boxes)[-1],), jnp.int32)]
        + [jax.ShapeDtypeStruct(value.shape, value.dtype) for value in handed],
        in_specs=[ANYWHERE] * 6 + whole(1),
        out_specs=whole(2) + [SCALARS] + whole(3),
        scratch_shapes=[pltpu.SMEM(dest.shape, jnp.int32), pltpu.SMEM(partners_t.shape, jnp.int32),
                        pltpu.SMEM(anchors_t.shape, jnp.int32), splitter, pltpu.SemaphoreType.DMA((6,))],
        compiler_params=pltpu.CompilerParams(vmem_limit_bytes=12 << 20),
        cost_estimate=cost(1_000_000, 2_000_000),
        name="second",
    )
    ahead, back, table, inverse, *diags = second(
        *map(in_place, (dest, partners_t, anchors_t, *handed)), held)
    prev_high = from_behind(ahead, 1)
    next_high = from_behind(back, -1)
    to_modes, from_modes = build_modes(False, *modes)

    def build_slabs(spin, *before, chosen=None):
        return pl.pallas_call(
            lambda *refs: slabs_kernel(spin, chosen, *refs),
            out_shape=slabs,
            in_specs=whole(1 + len(before)),
            out_specs=pl.BlockSpec(memory_space=pltpu.VMEM),
            scratch_shapes=[splitter],
            input_output_aliases={1: 0} if before else {},
            compiler_params=pltpu.CompilerParams(vmem_limit_bytes=12 << 20),
            cost_estimate=cost(2_000_000, 4_000_000),
        )(held, *before)

    pads = [build_slabs(0), build_slabs(1, build_slabs(1, chosen=low_half), chosen=lambda: jnp.logical_not(low_half()))]
    for spin, halo in enumerate(((prev_low, next_low), (prev_high, next_high))):
        pads[spin] = pl.pallas_call(
            fill_kernel,
            out_shape=slabs,
            in_specs=whole(3),
            out_specs=pl.BlockSpec(memory_space=pltpu.VMEM),
            scratch_shapes=[pltpu.VMEM((FLAT, LANES), F32)],
            input_output_aliases={0: 0},
            compiler_params=pltpu.CompilerParams(vmem_limit_bytes=12 << 20),
            cost_estimate=cost(1_000_000, 2_000_000),
        )(pads[spin], *halo)

    shape = jax.ShapeDtypeStruct((CAP, 2 * FLAT, LANES), F32)

    def solve(start, held, spins, terms=None):
        cubes = held * len(spins) * PARTNERS
        final = terms is not None
        if final:
            shapes, specs = [shape], [ANYWHERE]
            extra = [pltpu.VMEM(shape.shape, F32), pltpu.SemaphoreType.DMA((CAP,))]
        else:
            shapes = [jax.ShapeDtypeStruct((held * len(spins), FLAT, LANES), F32)]
            shapes += [jax.ShapeDtypeStruct((count, FLAT, LANES), BF) for count in (AHEAD, BACK)]
            specs, extra = whole(3), []
        operands = [table, to_modes, from_modes, diags[final], inverse] + [pads[spin] for spin in spins] + (terms or [])
        return pl.pallas_call(
            lambda *refs: pair_kernel(start, held, spins, final, *refs),
            out_shape=shapes,
            in_specs=[SCALARS] + whole(len(operands) - 1),
            out_specs=specs,
            scratch_shapes=extra + [
                pltpu.VMEM((held, len(spins), PARTNERS, 2, FTILES, EDGE, LANES), F32),
                pltpu.VMEM((cubes * EDGE, 2 * FWIDE), BF),
                pltpu.VMEM((cubes * EDGE, 2 * FWIDE), BF),
                pltpu.VMEM((held * len(spins), FTILES, EDGE, LANES), F32),
                pltpu.VMEM((held * len(spins), TILES, EDGE, LANES), F32),
            ],
            compiler_params=pltpu.CompilerParams(vmem_limit_bytes=20 << 20),
            cost_estimate=cost(2 * cubes * EDGE * FACE * FACE, 10_000_000),
        )(*operands)

    terms, arrived = [], []
    for spin in range(2):
        mine, sent_ahead, sent_back = solve(0, moving, (spin,))
        terms.append(mine)
        ahead = from_behind(sent_ahead, 1)
        back = from_behind(sent_back, -1)
        arrived += [ahead, back]
    kept, = solve(moving, boxes - moving, (0, 1), terms)
    placed = pl.pallas_call(
        lambda *refs: place_kernel(boxes, *refs),
        out_shape=shape,
        in_specs=[SCALARS] + whole(4) + [ANYWHERE],
        out_specs=ANYWHERE,
        scratch_shapes=[pltpu.VMEM((AHEAD + BACK, 2 * FLAT, LANES), F32),
                        pltpu.SemaphoreType.DMA((AHEAD + BACK,))],
        input_output_aliases={5: 0},
        compiler_params=pltpu.CompilerParams(vmem_limit_bytes=8 << 20),
        cost_estimate=cost(1_000_000, 4_000_000),
        name="place",
    )(table, *arrived, kept)
    placed = placed.reshape(-1).reshape(CAP, FLAT, 2, LANES).transpose(0, 2, 1, 3)
    return placed.reshape(CAP, 2, FLAT * LANES).transpose(1, 0, 2)


def solution(mesh):
    return jax.shard_map(
        shards,
        mesh=mesh,
        in_specs=(P(None, AXES, None), P(), P(), P()),
        out_specs=P(None, AXES, None),
        check_vma=False,
    )
```

```python
import jax
import jax.numpy as jnp
import numpy as np
from jax import lax
from jax.experimental import pallas as pl
from jax.experimental.pallas import tpu as pltpu
from jax.sharding import PartitionSpec as P


EDGE = 40
PARTNERS = 2
GRID_X = 768
GRID_Y = 384
GRID_Z = 384
BACK = 2
AHEAD = 1
CAP = 7
SCREEN = 0.001

AXES = ("gx", "gy", "gz")
LANES = 128
FACE = EDGE * EDGE
TILES = -(-FACE // LANES)
NCHUNK = 256
FOLD = FACE // 2
FTILES = -(-FOLD // LANES)
FWIDE = FTILES * LANES
CHUNKS = [(min(first, FWIDE - NCHUNK), NCHUNK) for first in range(0, FWIDE, NCHUNK)]
FLAT = EDGE ** 3 // LANES
HALF = EDGE // 2
PAIRT = 2 * FACE // LANES
PAD = 24
ROWS = EDGE + 2 * PAD
ZERO_TILES = 7
BF = jnp.bfloat16
F32 = jnp.float32


def tables():
    counter = np.arange(EDGE) + 1
    turns = np.outer(counter, counter) % (2 * (EDGE + 1))
    sine = (np.sqrt(2.0 / (EDGE + 1.0)) * np.sin(np.pi * turns / (EDGE + 1.0))).astype(np.float32)
    sine = sine.astype(jnp.bfloat16).astype(np.float32)
    flipped = sine[::-1] * np.where(np.arange(EDGE) % 2 == 0, 1.0, -1.0)
    assert np.array_equal(sine, flipped)
    levels = 2.0 - 2.0 * np.cos(np.pi * counter / (EDGE + 1.0))
    number = np.arange(FOLD)
    second, step = number // HALF, number % HALF
    thirds = [2 * step + second % 2, 2 * step + 1 - second % 2]
    inverse = np.zeros((EDGE, 2 * FWIDE), np.float32)
    for part, third in enumerate(thirds):
        lam = levels[:, None] + levels[second] + levels[third] + SCREEN
        inverse[:, part * FWIDE:part * FWIDE + FOLD] = 1.0 / lam
    factors = np.zeros((6, EDGE, FWIDE), np.float32)
    factors[0, :HALF, :FOLD] = sine[:HALF][:, second]
    for part, third in enumerate(thirds):
        factors[1 + part, :, :FOLD] = sine[:, third]
    factors[3, :, :FOLD] = np.repeat(sine[:HALF], EDGE, axis=0).T
    lines = np.tile(sine, (HALF, 1)).T
    factors[4, :, :FOLD] = np.concatenate([lines[0::2], lines[1::2]])
    factors[5, :, :FOLD] = np.concatenate([lines[1::2], lines[0::2]])
    return sine, inverse, factors


def lane_iota():
    return lax.broadcasted_iota(jnp.int32, (1, LANES), 1)


def split_boxes(orb_ref, flat_ref, boxes):
    def step(i, _):
        base = pl.multiple_of(i * PAIRT * LANES, LANES)
        x = orb_ref[:, pl.ds(base, PAIRT * LANES)].astype(F32)
        for j in range(PAIRT):
            flat_ref[pl.ds(pl.multiple_of((i * PAIRT + j) * 8, 8), boxes), :] = x[:, j * LANES:(j + 1) * LANES]
        return 0

    lax.fori_loop(0, HALF, step, 0)


def flat_to_slabs(load, store):
    low = lane_iota() < LANES // 2
    rolled = None
    for t in range(PAIRT):
        x = load(t)
        if t < TILES:
            store(t, 0, x)
        if t >= TILES - 1:
            turned = pltpu.roll(x, LANES // 2, 1)
            if rolled is not None:
                store(t - TILES, 1, jnp.where(low, rolled, turned))
            rolled = turned
    store(TILES - 1, 1, rolled)


def turn(x):
    source = (LANES // 2 - 1 - lax.broadcasted_iota(jnp.int32, x.shape, 1)) & (LANES - 1)
    return jnp.take_along_axis(x, source, axis=1)


def reverse_slabs(load, store, first, count):
    low = lane_iota() < LANES // 2
    turned = [turn(load(v)) for v in range(count)]
    for u in range(first, TILES):
        v = TILES - 1 - u
        store(u, jnp.where(low, turned[v], turned[v - 1]) if v > 0 else turned[v])


def slabs_to_flat(load, store):
    low = lane_iota() < LANES // 2
    for t in range(TILES - 1):
        store(t, load(t, 0))
    before = load(TILES - 1, 0)
    for v in range(TILES):
        turned = pltpu.roll(load(v, 1), LANES // 2, 1)
        store(TILES - 1 + v, jnp.where(low, before, turned))
        before = turned


def wanted_boxes(part_ref, boxes):
    total = part_ref.shape[1]
    device = lax.axis_index(AXES)
    wanted = []
    for step in (1, -1):
        found = jnp.int32(0)
        for k in range(boxes):
            other = (device + step) * boxes + k
            inside = (other >= 0) & (other < total)
            for number in range(PARTNERS):
                local = part_ref[number, jnp.clip(other, 0, total - 1)] - device * boxes
                found = jnp.where(inside & (local >= 0) & (local < boxes), local, found)
        wanted.append(found)
    return wanted


def window_kernel(part_hbm, orb_hbm, fac_hbm, ahead_ref, back_ref, orb_ref, fac_ref, part_ref, flat_ref, sems):
    boxes = orb_ref.shape[1]
    small = pltpu.make_async_copy(part_hbm, part_ref, sems.at[0])
    large = [pltpu.make_async_copy(orb_hbm.at[spin], orb_ref.at[spin], sems.at[1 + spin]) for spin in range(2)]
    factors = pltpu.make_async_copy(fac_hbm, fac_ref, sems.at[3])
    small.start()
    for copy in (*large, factors):
        copy.start()
    small.wait()
    wanted = wanted_boxes(part_ref, boxes)
    large[0].wait()
    split_boxes(orb_ref.at[0], flat_ref, boxes)
    for side, ref in enumerate((ahead_ref, back_ref)):
        ref[...] = flat_ref[pl.ds(wanted[side], FLAT, stride=8), :].astype(BF)
    large[1].wait()
    factors.wait()


def table_layout(boxes):
    pairs = 0
    codes = pairs + boxes * PARTNERS * 4
    slots = codes + CAP + 1
    leaves = slots + AHEAD + BACK + 1
    order = leaves + AHEAD + BACK + 1
    homes = order + boxes
    return pairs, codes, slots, leaves, order, homes, homes + boxes + 1


def build_tables(dest_ref, part_ref, anc_ref, tab_ref, boxes):
    total = part_ref.shape[1]
    device = lax.axis_index(AXES)
    pairs, codes, slots, leaves, order, homes, _ = table_layout(boxes)
    one, none = jnp.int32(1), jnp.int32(0)
    for k in range(CAP + 1):
        tab_ref[codes + k] = boxes + AHEAD + BACK
    for k in range(boxes + 1):
        tab_ref[homes + k] = 0
    for k in range(AHEAD + BACK + 1):
        tab_ref[slots + k] = CAP
        tab_ref[leaves + k] = 0
    goes = [dest_ref[device * boxes + k] for k in range(boxes)]
    ahead_all, back_all = none, none
    for k in range(boxes):
        ahead_all = ahead_all + jnp.where(goes[k] == device + 1, one, none)
        back_all = back_all + jnp.where(goes[k] == device - 1, one, none)
    ahead, back, stay = none, none, none
    spots = []
    for k in range(boxes):
        is_ahead, is_back = goes[k] == device + 1, goes[k] == device - 1
        spot = jnp.where(is_ahead, ahead, jnp.where(is_back, ahead_all + back, ahead_all + back_all + stay))
        spots.append(spot)
        tab_ref[order + spot] = k
        spare = leaves + AHEAD + BACK
        tab_ref[jnp.where(is_ahead, leaves + jnp.minimum(ahead, AHEAD - 1), spare)] = spot
        tab_ref[jnp.where(is_back, leaves + AHEAD + jnp.minimum(back, BACK - 1), spare)] = spot
        ahead = ahead + jnp.where(is_ahead, one, none)
        back = back + jnp.where(is_back, one, none)
        stay = stay + jnp.where(is_ahead | is_back, none, one)
    count = none
    for block in range(3):
        arrived = none
        for k in range(boxes):
            box = (device + (block - 1)) * boxes + k
            hit = (box >= 0) & (box < total) & (dest_ref[jnp.clip(box, 0, total - 1)] == device)
            if block == 1:
                code = spots[k]
                tab_ref[jnp.where(hit, homes + code, homes + boxes)] = jnp.minimum(count, CAP - 1)
            else:
                first, most = (0, AHEAD) if block == 0 else (AHEAD, BACK)
                where = first + jnp.minimum(arrived, most - 1)
                code = boxes + where
                tab_ref[jnp.where(hit, slots + where, slots + AHEAD + BACK)] = count
                arrived = arrived + jnp.where(hit, one, none)
            tab_ref[jnp.where(hit, codes + jnp.minimum(count, CAP - 1), codes + CAP)] = code
            count = count + jnp.where(hit, one, none)
    for box in range(boxes):
        me = device * boxes + box
        for number in range(PARTNERS):
            other = part_ref[number, me]
            local = other - device * boxes
            base = pairs + (box * PARTNERS + number) * 4
            tab_ref[base] = jnp.where(local < 0, boxes, jnp.where(local >= boxes, boxes + 1, local))
            for axis, extent in enumerate((GRID_X, GRID_Y, GRID_Z)):
                moved = anc_ref[axis, other] - anc_ref[axis, me] + extent // 2
                moved = jnp.where(moved < 0, moved + extent, jnp.where(moved >= extent, moved - extent, moved))
                tab_ref[base + 1 + axis] = jnp.clip(moved - extent // 2, -(PAD - 4), PAD - 4)


def reverse_box(pad_ref, box):
    body = pl.ds(PAD, EDGE)
    reverse_slabs(lambda v: pad_ref[0, box, v, body, :],
                  lambda u, x: pad_ref.__setitem__((1, box, u, body, slice(None)), x), 0, TILES)


def second_kernel(dest_hbm, part_hbm, anc_hbm, inv_hbm, diag_hbm, rest_hbm, orb_ref,
                  ahead_ref, back_ref, tab_ref, inv_ref, diag_ref, rest_ref,
                  dest_ref, part_ref, anc_ref, flat_ref, sems):
    boxes = orb_ref.shape[1]
    pieces = [(part_hbm, part_ref), (dest_hbm, dest_ref), (anc_hbm, anc_ref)]
    pieces += [(inv_hbm, inv_ref), (diag_hbm, diag_ref), (rest_hbm, rest_ref)]
    copies = [pltpu.make_async_copy(source, target, sems.at[k]) for k, (source, target) in enumerate(pieces)]
    for copy in copies:
        copy.start()
    split_boxes(orb_ref.at[1], flat_ref, boxes)
    for copy in copies[:3]:
        copy.wait()
    wanted = wanted_boxes(part_ref, boxes)
    for side, ref in enumerate((ahead_ref, back_ref)):
        ref[...] = flat_ref[pl.ds(wanted[side], FLAT, stride=8), :].astype(BF)
    build_tables(dest_ref, part_ref, anc_ref, tab_ref, boxes)
    for copy in copies[3:]:
        copy.wait()


def low_half():
    return 2 * lax.axis_index(AXES[-1]) < lax.axis_size(AXES[-1])


def slabs_kernel(spin, chosen, orb_ref, *refs):
    pad_ref, flat_ref = refs[-2:]
    boxes = orb_ref.shape[1]

    @pl.when(chosen() if chosen else True)
    def _():
        split_boxes(orb_ref.at[spin], flat_ref, boxes)

        for box in range(boxes):
            flat_to_slabs(
                lambda t: flat_ref[pl.ds(box + 8 * t, HALF, stride=8 * PAIRT), :],
                lambda u, parity, x: pad_ref.__setitem__(
                    (0, box, u, pl.ds(PAD + parity, HALF, stride=2), slice(None)), x),
            )
            reverse_box(pad_ref, box)


def modes_kernel(early, fac_ref, *refs):
    to_ref, from_ref = refs[-2:]

    @pl.when(low_half() if early else jnp.logical_not(low_half()))
    def _():
        front = lax.broadcasted_iota(jnp.int32, (EDGE, 1), 0) < HALF

        def build(i, _):
            where = pl.ds(pl.multiple_of(i * 2 * EDGE, 16), 2 * EDGE)
            for start, size in CHUNKS:
                cols = slice(start, start + size)
                line = [fac_ref[0, pl.ds(2 * i + k, 1), cols] for k in range(2)]
                mode = [fac_ref[3, pl.ds(4 * i + k, 1), cols] for k in range(4)]
                modes = [jnp.where(front, mode[2 * k], mode[2 * k + 1]) for k in range(2)]
                for part in range(2):
                    right = fac_ref[1 + part, :, cols]
                    to_ref[part, where, cols] = jnp.concatenate([x * right for x in line], axis=0).astype(BF)
                    right = fac_ref[4 + part, :, cols]
                    from_ref[part, where, cols] = jnp.concatenate([x * right for x in modes], axis=0).astype(BF)
            return 0

        lax.fori_loop(0, HALF // 2, build, 0)
        for part in range(2):
            to_ref[part, FOLD:, :] = jnp.zeros((FWIDE - FOLD, FWIDE), BF)
            from_ref[part, FOLD:, :] = jnp.zeros((FWIDE - FOLD, FWIDE), BF)


def fill_kernel(old_ref, prev_ref, next_ref, pad_ref, flat_ref):
    boxes = pad_ref.shape[1] - 2
    for side, ref in ((0, prev_ref), (1, next_ref)):
        flat_ref[...] = ref[...].astype(F32)
        flat_to_slabs(
            lambda t: flat_ref[pl.ds(t, HALF, stride=PAIRT), :],
            lambda u, parity, x: pad_ref.__setitem__(
                (0, boxes + side, u, pl.ds(PAD + parity, HALF, stride=2), slice(None)), x),
        )
        reverse_box(pad_ref, boxes + side)


def pair_kernel(start, held, spins, final, tab_ref, to_ref, from_ref, diag_ref, inv_ref, *refs):
    pads, (mov_ref, x_ref, y_ref, half_ref, res_ref) = refs[:len(spins)], refs[-5:]
    boxes = pads[0].shape[1] - 2
    pairs, codes, _, leaves, order, homes, _ = table_layout(boxes)
    if final:
        low_ref, high_ref, out_ref, form_ref, sems = refs[len(spins):-5]

        def copy(slot):
            return pltpu.make_async_copy(form_ref.at[slot], out_ref.at[slot], sems.at[slot])

        def early(slot, _):
            code = tab_ref[codes + slot]

            @pl.when(code < start)
            def _():
                spot = jnp.minimum(code, start - 1)
                for spin, ref in enumerate((low_ref, high_ref)):
                    form_ref[slot, pl.ds(spin, FLAT, stride=2), :] = ref[spot]
                copy(slot).start()

            @pl.when(code >= boxes + AHEAD + BACK)
            def _():
                form_ref[slot] = jnp.zeros(form_ref.shape[1:], F32)
                copy(slot).start()

            return 0

        lax.fori_loop(0, CAP, early, 0)
    else:
        out_ref, sends = refs[len(spins)], refs[len(spins) + 1:-5]
    lanes = lane_iota()
    rows = lax.broadcasted_iota(jnp.int32, (EDGE, 1), 0)

    def dense(index):
        box = tab_ref[order + start + index]
        places = []
        for number in range(PARTNERS):
            base = pairs + (box * PARTNERS + number) * 4
            source = tab_ref[base]
            da, db, dc = tab_ref[base + 1], tab_ref[base + 2], tab_ref[base + 3]
            row_ok = jnp.abs(2 * (rows - da) - (EDGE - 1)) < EDGE
            for b_by, c_by in ((db, dc), (-db, -dc)):
                offset = ZERO_TILES * LANES - (b_by * EDGE + c_by)
                places.append((source, da, b_by, c_by, offset // LANES, offset % LANES, row_ok))
        last = [[None] * len(places) for _ in spins]
        for u in range(FTILES + 1):
            keep = []
            for source, da, b_by, c_by, quotient, rest, row_ok in places:
                if u > 0:
                    cell = lanes + (u - 1) * LANES
                    b = (cell * 52429) >> 21
                    c = cell - b * EDGE
                    ok = (jnp.abs(2 * (b - b_by) - (EDGE - 1)) < EDGE) & (jnp.abs(2 * (c - c_by) - (EDGE - 1)) < EDGE)
                    if u == FTILES:
                        ok = ok & (lanes < FOLD - (FTILES - 1) * LANES)
                    keep.append(row_ok & ok)
            for at, pad_ref in enumerate(pads):
                values = []
                for which, (source, da, b_by, c_by, quotient, rest, row_ok) in enumerate(places):
                    part = which % 2
                    tile = jnp.clip(quotient + (u - ZERO_TILES), 0, TILES - 1)
                    x = pad_ref[part, source, tile, pl.ds(PAD - da, EDGE), :]
                    turned = pltpu.roll(x, (LANES - rest) % LANES, 1)
                    if u > 0:
                        moved = jnp.where(keep[which], jnp.where(lanes < LANES - rest, last[at][which], turned), 0.0)
                        mov_ref[index, at, which // 2, part, u - 1] = moved
                        values.append(pad_ref[part, box, u - 1, pl.ds(PAD, EDGE), :] * moved)
                    last[at][which] = turned
                if u > 0:
                    where = pl.ds((index * len(spins) + at) * PARTNERS * EDGE, PARTNERS * EDGE)
                    front = jnp.concatenate(values[0::2], axis=0)
                    behind = jnp.concatenate(values[1::2], axis=0)
                    x_ref[where, (u - 1) * LANES:u * LANES] = (front + behind).astype(BF)
                    x_ref[where, FWIDE + (u - 1) * LANES:FWIDE + u * LANES] = (front - behind).astype(BF)
        return 0

    for index in range(held):
        dense(index)

    cubes = held * len(spins) * PARTNERS
    diag = diag_ref[...]
    for first in range(0, 2 * FWIDE, NCHUNK):
        cols = slice(first, first + NCHUNK)
        y_ref[:, cols] = jnp.dot(diag, x_ref[:, cols], preferred_element_type=F32).astype(BF)

    def forward(first, size):
        for part in range(2):
            z = jnp.dot(y_ref[:, part * FWIDE:(part + 1) * FWIDE], to_ref[part, :, pl.ds(first, size)],
                        preferred_element_type=F32)
            cols = pl.ds(pl.multiple_of(part * FWIDE + first, LANES), size)
            z = z.reshape(cubes, EDGE, size) * inv_ref[:, cols][None]
            x_ref[:, cols] = z.reshape(cubes * EDGE, size).astype(BF)

    def backward(first, size):
        even, odd = [jnp.dot(x_ref[:, part * FWIDE:(part + 1) * FWIDE], from_ref[part, :, pl.ds(first, size)],
                             preferred_element_type=F32) for part in range(2)]
        y_ref[:, pl.ds(first, size)] = (even + odd).astype(BF)
        y_ref[:, pl.ds(pl.multiple_of(FWIDE + first, LANES), size)] = (even - odd).astype(BF)

    for step in (forward, backward):
        step(0, FWIDE)

    for first in range(0, 2 * FTILES, 2):
        potential = jnp.dot(diag, y_ref[:, first * LANES:(first + 2) * LANES], preferred_element_type=F32)
        for u in (first, first + 1):
            side = slice((u - first) * LANES, (u - first + 1) * LANES)
            for index in range(held):
                for at in range(len(spins)):
                    total = 0.0
                    for number in range(PARTNERS):
                        row = ((index * len(spins) + at) * PARTNERS + number) * EDGE
                        total = total + potential[row:row + EDGE, side] * mov_ref[index, at, number, u // FTILES, u % FTILES]
                    if u < FTILES:
                        res_ref[index * len(spins) + at, u] = total
                    else:
                        half_ref[index * len(spins) + at, u - FTILES] = total

    def unfold(row):
        middle = FTILES - 1

        def store(u, x):
            if u == middle:
                x = jnp.where(lanes < FOLD - middle * LANES, res_ref[row, middle], x)
            res_ref[row, u] = x

        reverse_slabs(lambda v: half_ref[row, v], store, middle, FTILES)
        return 0

    for row in range(held * len(spins)):
        unfold(row)

    if final:
        for index in range(held):
            home = tab_ref[homes + start + index]
            for at in range(len(spins)):
                slabs_to_flat(
                    lambda u, parity: res_ref[index * len(spins) + at, u, pl.ds(parity, HALF, stride=2), :],
                    lambda t, x: form_ref.__setitem__(
                        (home, pl.ds(2 * t + at, HALF, stride=2 * PAIRT), slice(None)), x),
                )
            copy(home).start()

        def finish(slot, _):
            code = tab_ref[codes + slot]

            @pl.when((code < boxes) | (code >= boxes + AHEAD + BACK))
            def _():
                copy(slot).wait()

            return 0

        lax.fori_loop(0, CAP, finish, 0)
        return

    def flatten(row):
        slabs_to_flat(
            lambda u, parity: res_ref[row, u, pl.ds(parity, HALF, stride=2), :],
            lambda t, x: out_ref.__setitem__((row, pl.ds(t, HALF, stride=PAIRT), slice(None)), x),
        )
        return 0

    for row in range(held * len(spins)):
        flatten(row)
    for k in range(AHEAD):
        sends[0][k] = out_ref[tab_ref[leaves + k]].astype(BF)
    for k in range(BACK):
        sends[1][k] = out_ref[tab_ref[leaves + AHEAD + k]].astype(BF)


def place_kernel(boxes, tab_ref, prev_low, next_low, prev_high, next_high, kept_ref, out_ref, form_ref, sems):
    slots = table_layout(boxes)[2]
    copies = []
    for k in range(AHEAD + BACK):
        pair, row = ((prev_low, prev_high), k) if k < AHEAD else ((next_low, next_high), k - AHEAD)
        slot = tab_ref[slots + k]
        copy = pltpu.make_async_copy(form_ref.at[k], out_ref.at[jnp.minimum(slot, CAP - 1)], sems.at[k])

        @pl.when(slot < CAP)
        def _():
            for spin, ref in enumerate(pair):
                form_ref[k, pl.ds(spin, FLAT, stride=2), :] = ref[row].astype(F32)
            copy.start()

        copies.append((slot, copy))
    for slot, copy in copies:
        @pl.when(slot < CAP)
        def _():
            copy.wait()


def from_behind(value, steps):
    count = lax.axis_size(AXES)
    return lax.ppermute(value, AXES, [(source, (source + steps) % count) for source in range(count)])


def whole(count):
    return [pl.BlockSpec(memory_space=pltpu.VMEM)] * count


SCALARS = pl.BlockSpec(memory_space=pltpu.SMEM)
ANYWHERE = pl.BlockSpec(memory_space=pltpu.MemorySpace.HBM)


def in_place(value):
    return pltpu.with_memory_space_constraint(jnp.asarray(value), pltpu.HBM)


def cost(flops, size):
    return pl.CostEstimate(flops=flops, bytes_accessed=size, transcendentals=0)


def shards(orbitals, dest, partners, anchors):
    boxes = orbitals.shape[1]
    sine, inverse, factors = tables()
    partners_t, anchors_t = partners.T, anchors.T

    box = jax.ShapeDtypeStruct((FLAT, LANES), BF)
    splitter = pltpu.VMEM((FLAT * 8, LANES), F32)
    ahead, back, held, factors = pl.pallas_call(
        window_kernel,
        out_shape=[box] * 2 + [jax.ShapeDtypeStruct(orbitals.shape, BF), jax.ShapeDtypeStruct(factors.shape, F32)],
        in_specs=[ANYWHERE] * 3,
        out_specs=whole(4),
        scratch_shapes=[pltpu.SMEM(partners_t.shape, jnp.int32), splitter, pltpu.SemaphoreType.DMA((4,))],
        compiler_params=pltpu.CompilerParams(vmem_limit_bytes=12 << 20),
        name="window",
    )(*map(in_place, (partners_t, orbitals, factors)))
    prev_low = from_behind(ahead, 1)
    next_low = from_behind(back, -1)

    folded = jax.ShapeDtypeStruct((2, FWIDE, FWIDE), BF)

    def build_modes(early, *before):
        return pl.pallas_call(
            lambda *refs: modes_kernel(early, *refs),
            out_shape=[folded] * 2,
            in_specs=whole(1 + len(before)),
            out_specs=whole(2),
            input_output_aliases={1: 0, 2: 1} if before else {},
            compiler_params=pltpu.CompilerParams(vmem_limit_bytes=12 << 20),
            cost_estimate=cost(4_000_000, 4_000_000),
        )(factors, *before)

    modes = build_modes(True)
    moving = AHEAD + BACK
    slabs = jax.ShapeDtypeStruct((2, boxes + 2, TILES, ROWS, LANES), F32)
    diags = [np.kron(np.eye(cubes, dtype=np.float32), sine).astype(jnp.bfloat16)
             for cubes in (moving * PARTNERS, (boxes - moving) * 2 * PARTNERS)]
    handed = (inverse, *diags)
    second = pl.pallas_call(
        second_kernel,
        out_shape=[box, box, jax.ShapeDtypeStruct((table_layout(boxes)[-1],), jnp.int32)]
        + [jax.ShapeDtypeStruct(value.shape, value.dtype) for value in handed],
        in_specs=[ANYWHERE] * 6 + whole(1),
        out_specs=whole(2) + [SCALARS] + whole(3),
        scratch_shapes=[pltpu.SMEM(dest.shape, jnp.int32), pltpu.SMEM(partners_t.shape, jnp.int32),
                        pltpu.SMEM(anchors_t.shape, jnp.int32), splitter, pltpu.SemaphoreType.DMA((6,))],
        compiler_params=pltpu.CompilerParams(vmem_limit_bytes=12 << 20),
        cost_estimate=cost(1_000_000, 2_000_000),
        name="second",
    )
    ahead, back, table, inverse, *diags = second(
        *map(in_place, (dest, partners_t, anchors_t, *handed)), held)
    prev_high = from_behind(ahead, 1)
    next_high = from_behind(back, -1)
    to_modes, from_modes = build_modes(False, *modes)

    def build_slabs(spin, *before, chosen=None):
        return pl.pallas_call(
            lambda *refs: slabs_kernel(spin, chosen, *refs),
            out_shape=slabs,
            in_specs=whole(1 + len(before)),
            out_specs=pl.BlockSpec(memory_space=pltpu.VMEM),
            scratch_shapes=[splitter],
            input_output_aliases={1: 0} if before else {},
            compiler_params=pltpu.CompilerParams(vmem_limit_bytes=12 << 20),
            cost_estimate=cost(2_000_000, 4_000_000),
        )(held, *before)

    pads = [build_slabs(0), build_slabs(1, build_slabs(1, chosen=low_half), chosen=lambda: jnp.logical_not(low_half()))]
    for spin, halo in enumerate(((prev_low, next_low), (prev_high, next_high))):
        pads[spin] = pl.pallas_call(
            fill_kernel,
            out_shape=slabs,
            in_specs=whole(3),
            out_specs=pl.BlockSpec(memory_space=pltpu.VMEM),
            scratch_shapes=[pltpu.VMEM((FLAT, LANES), F32)],
            input_output_aliases={0: 0},
            compiler_params=pltpu.CompilerParams(vmem_limit_bytes=12 << 20),
            cost_estimate=cost(1_000_000, 2_000_000),
        )(pads[spin], *halo)

    shape = jax.ShapeDtypeStruct((CAP, 2 * FLAT, LANES), F32)

    def solve(start, held, spins, terms=None):
        cubes = held * len(spins) * PARTNERS
        final = terms is not None
        if final:
            shapes, specs = [shape], [ANYWHERE]
            extra = [pltpu.VMEM(shape.shape, F32), pltpu.SemaphoreType.DMA((CAP,))]
        else:
            shapes = [jax.ShapeDtypeStruct((held * len(spins), FLAT, LANES), F32)]
            shapes += [jax.ShapeDtypeStruct((count, FLAT, LANES), BF) for count in (AHEAD, BACK)]
            specs, extra = whole(3), []
        operands = [table, to_modes, from_modes, diags[final], inverse] + [pads[spin] for spin in spins] + (terms or [])
        return pl.pallas_call(
            lambda *refs: pair_kernel(start, held, spins, final, *refs),
            out_shape=shapes,
            in_specs=[SCALARS] + whole(len(operands) - 1),
            out_specs=specs,
            scratch_shapes=extra + [
                pltpu.VMEM((held, len(spins), PARTNERS, 2, FTILES, EDGE, LANES), F32),
                pltpu.VMEM((cubes * EDGE, 2 * FWIDE), BF),
                pltpu.VMEM((cubes * EDGE, 2 * FWIDE), BF),
                pltpu.VMEM((held * len(spins), FTILES, EDGE, LANES), F32),
                pltpu.VMEM((held * len(spins), TILES, EDGE, LANES), F32),
            ],
            compiler_params=pltpu.CompilerParams(vmem_limit_bytes=20 << 20),
            cost_estimate=cost(2 * cubes * EDGE * FACE * FACE, 10_000_000),
        )(*operands)

    terms, arrived = [], []
    for spin in range(2):
        mine, sent_ahead, sent_back = solve(0, moving, (spin,))
        terms.append(mine)
        ahead = from_behind(sent_ahead, 1)
        back = from_behind(sent_back, -1)
        arrived += [ahead, back]
    kept, = solve(moving, boxes - moving, (0, 1), terms)
    placed = pl.pallas_call(
        lambda *refs: place_kernel(boxes, *refs),
        out_shape=shape,
        in_specs=[SCALARS] + whole(4) + [ANYWHERE],
        out_specs=ANYWHERE,
        scratch_shapes=[pltpu.VMEM((AHEAD + BACK, 2 * FLAT, LANES), F32),
                        pltpu.SemaphoreType.DMA((AHEAD + BACK,))],
        input_output_aliases={5: 0},
        compiler_params=pltpu.CompilerParams(vmem_limit_bytes=8 << 20),
        cost_estimate=cost(1_000_000, 4_000_000),
        name="place",
    )(table, *arrived, kept)
    placed = placed.reshape(-1).reshape(CAP, FLAT, 2, LANES).transpose(0, 2, 1, 3)
    return placed.reshape(CAP, 2, FLAT * LANES).transpose(1, 0, 2)


def solution(mesh):
    return jax.shard_map(
        shards,
        mesh=mesh,
        in_specs=(P(None, AXES, None), P(), P(), P()),
        out_specs=P(None, AXES, None),
        check_vma=False,
    )
```

```python
import jax
import jax.numpy as jnp
import numpy as np
from jax import lax
from jax.experimental import pallas as pl
from jax.experimental.pallas import tpu as pltpu
from jax.sharding import PartitionSpec as P


EDGE = 40
PARTNERS = 2
GRID_X = 768
GRID_Y = 384
GRID_Z = 384
BACK = 2
AHEAD = 1
CAP = 7
SCREEN = 0.001

AXES = ("gx", "gy", "gz")
LANES = 128
FACE = EDGE * EDGE
TILES = -(-FACE // LANES)
NCHUNK = 256
FOLD = FACE // 2
FTILES = -(-FOLD // LANES)
FWIDE = FTILES * LANES
CHUNKS = [(min(first, FWIDE - NCHUNK), NCHUNK) for first in range(0, FWIDE, NCHUNK)]
FLAT = EDGE ** 3 // LANES
HALF = EDGE // 2
PAIRT = 2 * FACE // LANES
PAD = 24
ROWS = EDGE + 2 * PAD
ZERO_TILES = 7
BF = jnp.bfloat16
F32 = jnp.float32


def tables():
    counter = np.arange(EDGE) + 1
    turns = np.outer(counter, counter) % (2 * (EDGE + 1))
    sine = (np.sqrt(2.0 / (EDGE + 1.0)) * np.sin(np.pi * turns / (EDGE + 1.0))).astype(np.float32)
    sine = sine.astype(jnp.bfloat16).astype(np.float32)
    flipped = sine[::-1] * np.where(np.arange(EDGE) % 2 == 0, 1.0, -1.0)
    assert np.array_equal(sine, flipped)
    levels = 2.0 - 2.0 * np.cos(np.pi * counter / (EDGE + 1.0))
    number = np.arange(FOLD)
    second, step = number // HALF, number % HALF
    thirds = [2 * step + second % 2, 2 * step + 1 - second % 2]
    inverse = np.zeros((EDGE, 2 * FWIDE), np.float32)
    for part, third in enumerate(thirds):
        lam = levels[:, None] + levels[second] + levels[third] + SCREEN
        inverse[:, part * FWIDE:part * FWIDE + FOLD] = 1.0 / lam
    factors = np.zeros((6, EDGE, FWIDE), np.float32)
    factors[0, :HALF, :FOLD] = sine[:HALF][:, second]
    for part, third in enumerate(thirds):
        factors[1 + part, :, :FOLD] = sine[:, third]
    factors[3, :, :FOLD] = np.repeat(sine[:HALF], EDGE, axis=0).T
    lines = np.tile(sine, (HALF, 1)).T
    factors[4, :, :FOLD] = np.concatenate([lines[0::2], lines[1::2]])
    factors[5, :, :FOLD] = np.concatenate([lines[1::2], lines[0::2]])
    return sine, inverse, factors


def lane_iota():
    return lax.broadcasted_iota(jnp.int32, (1, LANES), 1)


def split_boxes(orb_ref, flat_ref, boxes):
    def step(i, _):
        base = pl.multiple_of(i * PAIRT * LANES, LANES)
        x = orb_ref[:, pl.ds(base, PAIRT * LANES)].astype(F32)
        for j in range(PAIRT):
            flat_ref[pl.ds(pl.multiple_of((i * PAIRT + j) * 8, 8), boxes), :] = x[:, j * LANES:(j + 1) * LANES]
        return 0

    lax.fori_loop(0, HALF, step, 0)


def flat_to_slabs(load, store):
    low = lane_iota() < LANES // 2
    rolled = None
    for t in range(PAIRT):
        x = load(t)
        if t < TILES:
            store(t, 0, x)
        if t >= TILES - 1:
            turned = pltpu.roll(x, LANES // 2, 1)
            if rolled is not None:
                store(t - TILES, 1, jnp.where(low, rolled, turned))
            rolled = turned
    store(TILES - 1, 1, rolled)


def turn(x):
    source = (LANES // 2 - 1 - lax.broadcasted_iota(jnp.int32, x.shape, 1)) & (LANES - 1)
    return jnp.take_along_axis(x, source, axis=1)


def reverse_slabs(load, store, first, count):
    low = lane_iota() < LANES // 2
    turned = [turn(load(v)) for v in range(count)]
    for u in range(first, TILES):
        v = TILES - 1 - u
        store(u, jnp.where(low, turned[v], turned[v - 1]) if v > 0 else turned[v])


def slabs_to_flat(load, store):
    low = lane_iota() < LANES // 2
    for t in range(TILES - 1):
        store(t, load(t, 0))
    before = load(TILES - 1, 0)
    for v in range(TILES):
        turned = pltpu.roll(load(v, 1), LANES // 2, 1)
        store(TILES - 1 + v, jnp.where(low, before, turned))
        before = turned


def wanted_boxes(part_ref, boxes):
    total = part_ref.shape[1]
    device = lax.axis_index(AXES)
    wanted = []
    for step in (1, -1):
        found = jnp.int32(0)
        for k in range(boxes):
            other = (device + step) * boxes + k
            inside = (other >= 0) & (other < total)
            for number in range(PARTNERS):
                local = part_ref[number, jnp.clip(other, 0, total - 1)] - device * boxes
                found = jnp.where(inside & (local >= 0) & (local < boxes), local, found)
        wanted.append(found)
    return wanted


def window_kernel(part_hbm, orb_hbm, fac_hbm, ahead_ref, back_ref, orb_ref, fac_ref, part_ref, flat_ref, sems):
    boxes = orb_ref.shape[1]
    small = pltpu.make_async_copy(part_hbm, part_ref, sems.at[0])
    large = [pltpu.make_async_copy(orb_hbm.at[spin], orb_ref.at[spin], sems.at[1 + spin]) for spin in range(2)]
    factors = pltpu.make_async_copy(fac_hbm, fac_ref, sems.at[3])
    small.start()
    for copy in (*large, factors):
        copy.start()
    small.wait()
    wanted = wanted_boxes(part_ref, boxes)
    large[0].wait()
    split_boxes(orb_ref.at[0], flat_ref, boxes)
    for side, ref in enumerate((ahead_ref, back_ref)):
        ref[...] = flat_ref[pl.ds(wanted[side], FLAT, stride=8), :].astype(BF)
    large[1].wait()
    factors.wait()


def table_layout(boxes):
    pairs = 0
    codes = pairs + boxes * PARTNERS * 4
    slots = codes + CAP + 1
    leaves = slots + AHEAD + BACK + 1
    order = leaves + AHEAD + BACK + 1
    homes = order + boxes
    return pairs, codes, slots, leaves, order, homes, homes + boxes + 1


def build_tables(dest_ref, part_ref, anc_ref, tab_ref, boxes):
    total = part_ref.shape[1]
    device = lax.axis_index(AXES)
    pairs, codes, slots, leaves, order, homes, _ = table_layout(boxes)
    one, none = jnp.int32(1), jnp.int32(0)
    for k in range(CAP + 1):
        tab_ref[codes + k] = boxes + AHEAD + BACK
    for k in range(boxes + 1):
        tab_ref[homes + k] = 0
    for k in range(AHEAD + BACK + 1):
        tab_ref[slots + k] = CAP
        tab_ref[leaves + k] = 0
    goes = [dest_ref[device * boxes + k] for k in range(boxes)]
    ahead_all, back_all = none, none
    for k in range(boxes):
        ahead_all = ahead_all + jnp.where(goes[k] == device + 1, one, none)
        back_all = back_all + jnp.where(goes[k] == device - 1, one, none)
    ahead, back, stay = none, none, none
    spots = []
    for k in range(boxes):
        is_ahead, is_back = goes[k] == device + 1, goes[k] == device - 1
        spot = jnp.where(is_ahead, ahead, jnp.where(is_back, ahead_all + back, ahead_all + back_all + stay))
        spots.append(spot)
        tab_ref[order + spot] = k
        spare = leaves + AHEAD + BACK
        tab_ref[jnp.where(is_ahead, leaves + jnp.minimum(ahead, AHEAD - 1), spare)] = spot
        tab_ref[jnp.where(is_back, leaves + AHEAD + jnp.minimum(back, BACK - 1), spare)] = spot
        ahead = ahead + jnp.where(is_ahead, one, none)
        back = back + jnp.where(is_back, one, none)
        stay = stay + jnp.where(is_ahead | is_back, none, one)
    count = none
    for block in range(3):
        arrived = none
        for k in range(boxes):
            box = (device + (block - 1)) * boxes + k
            hit = (box >= 0) & (box < total) & (dest_ref[jnp.clip(box, 0, total - 1)] == device)
            if block == 1:
                code = spots[k]
                tab_ref[jnp.where(hit, homes + code, homes + boxes)] = jnp.minimum(count, CAP - 1)
            else:
                first, most = (0, AHEAD) if block == 0 else (AHEAD, BACK)
                where = first + jnp.minimum(arrived, most - 1)
                code = boxes + where
                tab_ref[jnp.where(hit, slots + where, slots + AHEAD + BACK)] = count
                arrived = arrived + jnp.where(hit, one, none)
            tab_ref[jnp.where(hit, codes + jnp.minimum(count, CAP - 1), codes + CAP)] = code
            count = count + jnp.where(hit, one, none)
    for box in range(boxes):
        me = device * boxes + box
        for number in range(PARTNERS):
            other = part_ref[number, me]
            local = other - device * boxes
            base = pairs + (box * PARTNERS + number) * 4
            tab_ref[base] = jnp.where(local < 0, boxes, jnp.where(local >= boxes, boxes + 1, local))
            for axis, extent in enumerate((GRID_X, GRID_Y, GRID_Z)):
                moved = anc_ref[axis, other] - anc_ref[axis, me] + extent // 2
                moved = jnp.where(moved < 0, moved + extent, jnp.where(moved >= extent, moved - extent, moved))
                tab_ref[base + 1 + axis] = jnp.clip(moved - extent // 2, -(PAD - 4), PAD - 4)


def reverse_box(pad_ref, box):
    body = pl.ds(PAD, EDGE)
    reverse_slabs(lambda v: pad_ref[0, box, v, body, :],
                  lambda u, x: pad_ref.__setitem__((1, box, u, body, slice(None)), x), 0, TILES)


def second_kernel(dest_hbm, part_hbm, anc_hbm, inv_hbm, diag_hbm, rest_hbm, orb_ref,
                  ahead_ref, back_ref, tab_ref, inv_ref, diag_ref, rest_ref,
                  dest_ref, part_ref, anc_ref, flat_ref, sems):
    boxes = orb_ref.shape[1]
    pieces = [(part_hbm, part_ref), (dest_hbm, dest_ref), (anc_hbm, anc_ref)]
    pieces += [(inv_hbm, inv_ref), (diag_hbm, diag_ref), (rest_hbm, rest_ref)]
    copies = [pltpu.make_async_copy(source, target, sems.at[k]) for k, (source, target) in enumerate(pieces)]
    for copy in copies:
        copy.start()
    split_boxes(orb_ref.at[1], flat_ref, boxes)
    for copy in copies[:3]:
        copy.wait()
    wanted = wanted_boxes(part_ref, boxes)
    for side, ref in enumerate((ahead_ref, back_ref)):
        ref[...] = flat_ref[pl.ds(wanted[side], FLAT, stride=8), :].astype(BF)
    build_tables(dest_ref, part_ref, anc_ref, tab_ref, boxes)
    for copy in copies[3:]:
        copy.wait()


def low_half():
    return 2 * lax.axis_index(AXES[-1]) < lax.axis_size(AXES[-1])


def at_start():
    return lax.axis_index(AXES[-1]) == 0


def at_end():
    return lax.axis_index(AXES[-1]) == lax.axis_size(AXES[-1]) - 1


def slabs_kernel(spin, chosen, orb_ref, *refs):
    pad_ref, flat_ref = refs[-2:]
    boxes = orb_ref.shape[1]

    @pl.when(chosen() if chosen else True)
    def _():
        split_boxes(orb_ref.at[spin], flat_ref, boxes)

        for box in range(boxes):
            flat_to_slabs(
                lambda t: flat_ref[pl.ds(box + 8 * t, HALF, stride=8 * PAIRT), :],
                lambda u, parity, x: pad_ref.__setitem__(
                    (0, box, u, pl.ds(PAD + parity, HALF, stride=2), slice(None)), x),
            )
            reverse_box(pad_ref, box)


def modes_kernel(chosen, fac_ref, *refs):
    to_ref, from_ref = refs[-2:]

    @pl.when(chosen())
    def _():
        front = lax.broadcasted_iota(jnp.int32, (EDGE, 1), 0) < HALF

        def build(i, _):
            where = pl.ds(pl.multiple_of(i * 2 * EDGE, 16), 2 * EDGE)
            for start, size in CHUNKS:
                cols = slice(start, start + size)
                line = [fac_ref[0, pl.ds(2 * i + k, 1), cols] for k in range(2)]
                mode = [fac_ref[3, pl.ds(4 * i + k, 1), cols] for k in range(4)]
                modes = [jnp.where(front, mode[2 * k], mode[2 * k + 1]) for k in range(2)]
                for part in range(2):
                    right = fac_ref[1 + part, :, cols]
                    to_ref[part, where, cols] = jnp.concatenate([x * right for x in line], axis=0).astype(BF)
                    right = fac_ref[4 + part, :, cols]
                    from_ref[part, where, cols] = jnp.concatenate([x * right for x in modes], axis=0).astype(BF)
            return 0

        lax.fori_loop(0, HALF // 2, build, 0)
        for part in range(2):
            to_ref[part, FOLD:, :] = jnp.zeros((FWIDE - FOLD, FWIDE), BF)
            from_ref[part, FOLD:, :] = jnp.zeros((FWIDE - FOLD, FWIDE), BF)


def fill_kernel(old_ref, prev_ref, next_ref, pad_ref, flat_ref):
    boxes = pad_ref.shape[1] - 2
    for side, ref in ((0, prev_ref), (1, next_ref)):
        flat_ref[...] = ref[...].astype(F32)
        flat_to_slabs(
            lambda t: flat_ref[pl.ds(t, HALF, stride=PAIRT), :],
            lambda u, parity, x: pad_ref.__setitem__(
                (0, boxes + side, u, pl.ds(PAD + parity, HALF, stride=2), slice(None)), x),
        )
        reverse_box(pad_ref, boxes + side)


def pair_kernel(start, held, spins, final, tab_ref, to_ref, from_ref, diag_ref, inv_ref, *refs):
    pads, (mov_ref, x_ref, y_ref, half_ref, res_ref) = refs[:len(spins)], refs[-5:]
    boxes = pads[0].shape[1] - 2
    pairs, codes, _, leaves, order, homes, _ = table_layout(boxes)
    if final:
        low_ref, high_ref, out_ref, form_ref, sems = refs[len(spins):-5]

        def copy(slot):
            return pltpu.make_async_copy(form_ref.at[slot], out_ref.at[slot], sems.at[slot])

        def early(slot, _):
            code = tab_ref[codes + slot]

            @pl.when(code < start)
            def _():
                spot = jnp.minimum(code, start - 1)
                for spin, ref in enumerate((low_ref, high_ref)):
                    form_ref[slot, pl.ds(spin, FLAT, stride=2), :] = ref[spot]
                copy(slot).start()

            @pl.when(code >= boxes + AHEAD + BACK)
            def _():
                form_ref[slot] = jnp.zeros(form_ref.shape[1:], F32)
                copy(slot).start()

            return 0

        lax.fori_loop(0, CAP, early, 0)
    else:
        out_ref, sends = refs[len(spins)], refs[len(spins) + 1:-5]
    lanes = lane_iota()
    rows = lax.broadcasted_iota(jnp.int32, (EDGE, 1), 0)

    def dense(index):
        box = tab_ref[order + start + index]
        places = []
        for number in range(PARTNERS):
            base = pairs + (box * PARTNERS + number) * 4
            source = tab_ref[base]
            da, db, dc = tab_ref[base + 1], tab_ref[base + 2], tab_ref[base + 3]
            row_ok = jnp.abs(2 * (rows - da) - (EDGE - 1)) < EDGE
            for b_by, c_by in ((db, dc), (-db, -dc)):
                offset = ZERO_TILES * LANES - (b_by * EDGE + c_by)
                places.append((source, da, b_by, c_by, offset // LANES, offset % LANES, row_ok))
        last = [[None] * len(places) for _ in spins]
        for u in range(FTILES + 1):
            keep = []
            for source, da, b_by, c_by, quotient, rest, row_ok in places:
                if u > 0:
                    cell = lanes + (u - 1) * LANES
                    b = (cell * 52429) >> 21
                    c = cell - b * EDGE
                    ok = (jnp.abs(2 * (b - b_by) - (EDGE - 1)) < EDGE) & (jnp.abs(2 * (c - c_by) - (EDGE - 1)) < EDGE)
                    if u == FTILES:
                        ok = ok & (lanes < FOLD - (FTILES - 1) * LANES)
                    keep.append(row_ok & ok)
            for at, pad_ref in enumerate(pads):
                values = []
                for which, (source, da, b_by, c_by, quotient, rest, row_ok) in enumerate(places):
                    part = which % 2
                    tile = jnp.clip(quotient + (u - ZERO_TILES), 0, TILES - 1)
                    x = pad_ref[part, source, tile, pl.ds(PAD - da, EDGE), :]
                    turned = pltpu.roll(x, (LANES - rest) % LANES, 1)
                    if u > 0:
                        moved = jnp.where(keep[which], jnp.where(lanes < LANES - rest, last[at][which], turned), 0.0)
                        mov_ref[index, at, which // 2, part, u - 1] = moved
                        values.append(pad_ref[part, box, u - 1, pl.ds(PAD, EDGE), :] * moved)
                    last[at][which] = turned
                if u > 0:
                    where = pl.ds((index * len(spins) + at) * PARTNERS * EDGE, PARTNERS * EDGE)
                    front = jnp.concatenate(values[0::2], axis=0)
                    behind = jnp.concatenate(values[1::2], axis=0)
                    x_ref[where, (u - 1) * LANES:u * LANES] = (front + behind).astype(BF)
                    x_ref[where, FWIDE + (u - 1) * LANES:FWIDE + u * LANES] = (front - behind).astype(BF)
        return 0

    for index in range(held):
        dense(index)

    cubes = held * len(spins) * PARTNERS
    diag = diag_ref[...]
    for first in range(0, 2 * FWIDE, NCHUNK):
        cols = slice(first, first + NCHUNK)
        y_ref[:, cols] = jnp.dot(diag, x_ref[:, cols], preferred_element_type=F32).astype(BF)

    def forward(first, size):
        for part in range(2):
            z = jnp.dot(y_ref[:, part * FWIDE:(part + 1) * FWIDE], to_ref[part, :, pl.ds(first, size)],
                        preferred_element_type=F32)
            cols = pl.ds(pl.multiple_of(part * FWIDE + first, LANES), size)
            z = z.reshape(cubes, EDGE, size) * inv_ref[:, cols][None]
            x_ref[:, cols] = z.reshape(cubes * EDGE, size).astype(BF)

    def backward(first, size):
        even, odd = [jnp.dot(x_ref[:, part * FWIDE:(part + 1) * FWIDE], from_ref[part, :, pl.ds(first, size)],
                             preferred_element_type=F32) for part in range(2)]
        y_ref[:, pl.ds(first, size)] = (even + odd).astype(BF)
        y_ref[:, pl.ds(pl.multiple_of(FWIDE + first, LANES), size)] = (even - odd).astype(BF)

    for step in (forward, backward):
        step(0, FWIDE)

    for first in range(0, 2 * FTILES, 2):
        potential = jnp.dot(diag, y_ref[:, first * LANES:(first + 2) * LANES], preferred_element_type=F32)
        for u in (first, first + 1):
            side = slice((u - first) * LANES, (u - first + 1) * LANES)
            for index in range(held):
                for at in range(len(spins)):
                    total = 0.0
                    for number in range(PARTNERS):
                        row = ((index * len(spins) + at) * PARTNERS + number) * EDGE
                        total = total + potential[row:row + EDGE, side] * mov_ref[index, at, number, u // FTILES, u % FTILES]
                    if u < FTILES:
                        res_ref[index * len(spins) + at, u] = total
                    else:
                        half_ref[index * len(spins) + at, u - FTILES] = total

    def unfold(row):
        middle = FTILES - 1

        def store(u, x):
            if u == middle:
                x = jnp.where(lanes < FOLD - middle * LANES, res_ref[row, middle], x)
            res_ref[row, u] = x

        reverse_slabs(lambda v: half_ref[row, v], store, middle, FTILES)
        return 0

    for row in range(held * len(spins)):
        unfold(row)

    if final:
        for index in range(held):
            home = tab_ref[homes + start + index]
            for at in range(len(spins)):
                slabs_to_flat(
                    lambda u, parity: res_ref[index * len(spins) + at, u, pl.ds(parity, HALF, stride=2), :],
                    lambda t, x: form_ref.__setitem__(
                        (home, pl.ds(2 * t + at, HALF, stride=2 * PAIRT), slice(None)), x),
                )
            copy(home).start()

        def finish(slot, _):
            code = tab_ref[codes + slot]

            @pl.when((code < boxes) | (code >= boxes + AHEAD + BACK))
            def _():
                copy(slot).wait()

            return 0

        lax.fori_loop(0, CAP, finish, 0)
        return

    def flatten(row):
        slabs_to_flat(
            lambda u, parity: res_ref[row, u, pl.ds(parity, HALF, stride=2), :],
            lambda t, x: out_ref.__setitem__((row, pl.ds(t, HALF, stride=PAIRT), slice(None)), x),
        )
        return 0

    for row in range(held * len(spins)):
        flatten(row)
    for k in range(AHEAD):
        sends[0][k] = out_ref[tab_ref[leaves + k]].astype(BF)
    for k in range(BACK):
        sends[1][k] = out_ref[tab_ref[leaves + AHEAD + k]].astype(BF)


def place_kernel(boxes, tab_ref, prev_low, next_low, prev_high, next_high, kept_ref, out_ref, form_ref, sems):
    slots = table_layout(boxes)[2]
    copies = []
    for k in range(AHEAD + BACK):
        pair, row = ((prev_low, prev_high), k) if k < AHEAD else ((next_low, next_high), k - AHEAD)
        slot = tab_ref[slots + k]
        copy = pltpu.make_async_copy(form_ref.at[k], out_ref.at[jnp.minimum(slot, CAP - 1)], sems.at[k])

        @pl.when(slot < CAP)
        def _():
            for spin, ref in enumerate(pair):
                form_ref[k, pl.ds(spin, FLAT, stride=2), :] = ref[row].astype(F32)
            copy.start()

        copies.append((slot, copy))
    for slot, copy in copies:
        @pl.when(slot < CAP)
        def _():
            copy.wait()


def from_behind(value, steps):
    count = lax.axis_size(AXES)
    return lax.ppermute(value, AXES, [(source, (source + steps) % count) for source in range(count)])


def whole(count):
    return [pl.BlockSpec(memory_space=pltpu.VMEM)] * count


SCALARS = pl.BlockSpec(memory_space=pltpu.SMEM)
ANYWHERE = pl.BlockSpec(memory_space=pltpu.MemorySpace.HBM)


def in_place(value):
    return pltpu.with_memory_space_constraint(jnp.asarray(value), pltpu.HBM)


def cost(flops, size):
    return pl.CostEstimate(flops=flops, bytes_accessed=size, transcendentals=0)


def shards(orbitals, dest, partners, anchors):
    boxes = orbitals.shape[1]
    sine, inverse, factors = tables()
    partners_t, anchors_t = partners.T, anchors.T

    box = jax.ShapeDtypeStruct((FLAT, LANES), BF)
    splitter = pltpu.VMEM((FLAT * 8, LANES), F32)
    ahead, back, held, factors = pl.pallas_call(
        window_kernel,
        out_shape=[box] * 2 + [jax.ShapeDtypeStruct(orbitals.shape, BF), jax.ShapeDtypeStruct(factors.shape, F32)],
        in_specs=[ANYWHERE] * 3,
        out_specs=whole(4),
        scratch_shapes=[pltpu.SMEM(partners_t.shape, jnp.int32), splitter, pltpu.SemaphoreType.DMA((4,))],
        compiler_params=pltpu.CompilerParams(vmem_limit_bytes=12 << 20),
        name="window",
    )(*map(in_place, (partners_t, orbitals, factors)))
    prev_low = from_behind(ahead, 1)
    next_low = from_behind(back, -1)

    folded = jax.ShapeDtypeStruct((2, FWIDE, FWIDE), BF)

    def build_modes(place, *before):
        chosen = (at_start, lambda: low_half() & jnp.logical_not(at_start()), lambda: jnp.logical_not(low_half()))[place]
        return pl.pallas_call(
            lambda *refs: modes_kernel(chosen, *refs),
            out_shape=[folded] * 2,
            in_specs=whole(1 + len(before)),
            out_specs=whole(2),
            input_output_aliases={1: 0, 2: 1} if before else {},
            compiler_params=pltpu.CompilerParams(vmem_limit_bytes=12 << 20),
            cost_estimate=cost(4_000_000, 4_000_000),
        )(factors, *before)

    modes = build_modes(0)
    moving = AHEAD + BACK
    slabs = jax.ShapeDtypeStruct((2, boxes + 2, TILES, ROWS, LANES), F32)
    diags = [np.kron(np.eye(cubes, dtype=np.float32), sine).astype(jnp.bfloat16)
             for cubes in (moving * PARTNERS, (boxes - moving) * 2 * PARTNERS)]
    handed = (inverse, *diags)
    second = pl.pallas_call(
        second_kernel,
        out_shape=[box, box, jax.ShapeDtypeStruct((table_layout(boxes)[-1],), jnp.int32)]
        + [jax.ShapeDtypeStruct(value.shape, value.dtype) for value in handed],
        in_specs=[ANYWHERE] * 6 + whole(1),
        out_specs=whole(2) + [SCALARS] + whole(3),
        scratch_shapes=[pltpu.SMEM(dest.shape, jnp.int32), pltpu.SMEM(partners_t.shape, jnp.int32),
                        pltpu.SMEM(anchors_t.shape, jnp.int32), splitter, pltpu.SemaphoreType.DMA((6,))],
        compiler_params=pltpu.CompilerParams(vmem_limit_bytes=12 << 20),
        cost_estimate=cost(1_000_000, 2_000_000),
        name="second",
    )
    ahead, back, table, inverse, *diags = second(
        *map(in_place, (dest, partners_t, anchors_t, *handed)), held)
    prev_high = from_behind(ahead, 1)
    next_high = from_behind(back, -1)
    to_modes, from_modes = build_modes(2, *build_modes(1, *modes))

    def build_slabs(spin, *before, chosen=None):
        return pl.pallas_call(
            lambda *refs: slabs_kernel(spin, chosen, *refs),
            out_shape=slabs,
            in_specs=whole(1 + len(before)),
            out_specs=pl.BlockSpec(memory_space=pltpu.VMEM),
            scratch_shapes=[splitter],
            input_output_aliases={1: 0} if before else {},
            compiler_params=pltpu.CompilerParams(vmem_limit_bytes=12 << 20),
            cost_estimate=cost(2_000_000, 4_000_000),
        )(held, *before)

    pads = [build_slabs(0, build_slabs(0, chosen=at_end), chosen=lambda: jnp.logical_not(at_end())), build_slabs(1, build_slabs(1, chosen=at_start), chosen=lambda: jnp.logical_not(at_start()))]
    for spin, halo in enumerate(((prev_low, next_low), (prev_high, next_high))):
        pads[spin] = pl.pallas_call(
            fill_kernel,
            out_shape=slabs,
            in_specs=whole(3),
            out_specs=pl.BlockSpec(memory_space=pltpu.VMEM),
            scratch_shapes=[pltpu.VMEM((FLAT, LANES), F32)],
            input_output_aliases={0: 0},
            compiler_params=pltpu.CompilerParams(vmem_limit_bytes=12 << 20),
            cost_estimate=cost(1_000_000, 2_000_000),
        )(pads[spin], *halo)

    shape = jax.ShapeDtypeStruct((CAP, 2 * FLAT, LANES), F32)

    def solve(start, held, spins, terms=None):
        cubes = held * len(spins) * PARTNERS
        final = terms is not None
        if final:
            shapes, specs = [shape], [ANYWHERE]
            extra = [pltpu.VMEM(shape.shape, F32), pltpu.SemaphoreType.DMA((CAP,))]
        else:
            shapes = [jax.ShapeDtypeStruct((held * len(spins), FLAT, LANES), F32)]
            shapes += [jax.ShapeDtypeStruct((count, FLAT, LANES), BF) for count in (AHEAD, BACK)]
            specs, extra = whole(3), []
        operands = [table, to_modes, from_modes, diags[final], inverse] + [pads[spin] for spin in spins] + (terms or [])
        return pl.pallas_call(
            lambda *refs: pair_kernel(start, held, spins, final, *refs),
            out_shape=shapes,
            in_specs=[SCALARS] + whole(len(operands) - 1),
            out_specs=specs,
            scratch_shapes=extra + [
                pltpu.VMEM((held, len(spins), PARTNERS, 2, FTILES, EDGE, LANES), F32),
                pltpu.VMEM((cubes * EDGE, 2 * FWIDE), BF),
                pltpu.VMEM((cubes * EDGE, 2 * FWIDE), BF),
                pltpu.VMEM((held * len(spins), FTILES, EDGE, LANES), F32),
                pltpu.VMEM((held * len(spins), TILES, EDGE, LANES), F32),
            ],
            compiler_params=pltpu.CompilerParams(vmem_limit_bytes=20 << 20),
            cost_estimate=cost(2 * cubes * EDGE * FACE * FACE, 10_000_000),
        )(*operands)

    terms, arrived = [], []
    for spin in range(2):
        mine, sent_ahead, sent_back = solve(0, moving, (spin,))
        terms.append(mine)
        ahead = from_behind(sent_ahead, 1)
        back = from_behind(sent_back, -1)
        arrived += [ahead, back]
    kept, = solve(moving, boxes - moving, (0, 1), terms)
    placed = pl.pallas_call(
        lambda *refs: place_kernel(boxes, *refs),
        out_shape=shape,
        in_specs=[SCALARS] + whole(4) + [ANYWHERE],
        out_specs=ANYWHERE,
        scratch_shapes=[pltpu.VMEM((AHEAD + BACK, 2 * FLAT, LANES), F32),
                        pltpu.SemaphoreType.DMA((AHEAD + BACK,))],
        input_output_aliases={5: 0},
        compiler_params=pltpu.CompilerParams(vmem_limit_bytes=8 << 20),
        cost_estimate=cost(1_000_000, 4_000_000),
        name="place",
    )(table, *arrived, kept)
    placed = placed.reshape(-1).reshape(CAP, FLAT, 2, LANES).transpose(0, 2, 1, 3)
    return placed.reshape(CAP, 2, FLAT * LANES).transpose(1, 0, 2)


def solution(mesh):
    return jax.shard_map(
        shards,
        mesh=mesh,
        in_specs=(P(None, AXES, None), P(), P(), P()),
        out_specs=P(None, AXES, None),
        check_vma=False,
    )
```
